32 devices in a mesh: groups: 2 (over x), gx: 16 (over z, y, core).
Axes of the slice: x: 2, y: 2, z: 4, core: 2. Of those that a mesh axis runs over, the one named last changes fastest.
Arguments:
- features: bfloat16 [64, 16, 64, 128], P(('groups', 'gx')), parts along dimension 0, may hold values from -6 to 6
- cotangent: bfloat16 [64, 16, 64, 128], P(('groups', 'gx')), parts along dimension 0, may hold values from -6 to 6
- wall_flags: int32 [64, 16, 128], P(('groups', 'gx')), parts along dimension 0, may hold values 0 or 1
- mode_counts: int32 [64], replicated, may hold values from 1 to 16, as said below
- offsets: int32 [6, 3], replicated, may hold values from -2 to 2, as said below
- point_weight: bfloat16 [64, 64], replicated, may hold values from -0.75 to 0.75
- kernel_weight: bfloat16 [6, 64, 64], replicated, may hold values from -0.3125 to 0.3125
- lap_weight: bfloat16 [64, 64], replicated, may hold values from -0.125 to 0.125
- spec_weight: bfloat16 [16, 64, 64], replicated, may hold values from -1 to 1
- bias: float32 [64], replicated, may hold values from -3 to 3
Outputs:
- input_grad: bfloat16 [64, 16, 64, 128], P(('groups', 'gx')), parts along dimension 0
- kernel_grad: float32 [12, 64, 64], P('groups'), parts along dimension 0
The draws below stay inside these ranges and needn't reach their ends.
There are 2 independent parts, one for each index of `groups`. The reference program is written for one: setup_inputs(seed, part) draws one part's arguments, and reference() takes and returns one part's arrays. A program takes and returns all parts, laid end to end along the dimension named above; an argument that names none is the same for every part. Nothing has to cross between parts.
Inputs may be any that keep to these rules, and one draw needn't show every extreme that they name: Column 0 holds x offsets in -1..1 and both -1 and 1 occur; columns 1 and 2 hold y and z offsets in -2..2, and -2 and 2 occur in each of them. `mode_counts`: some channel keeps 16 modes and some channel keeps 1.
All inputs are finite; a program needn't handle non-finite values. No bound on the sum of `wall_flags` on one device may be relied on, other than what follows from the above.
Results may differ from the reference program's by a relative error of at most 0.0066.
Values may be sent and summed in bfloat16 or wider, within the bound.
A program may use at most 256 MiB of HBM per device.

```python
import math
from functools import partial
import jax
import jax.numpy as jnp
from jax import lax

C = 64
MX = 16
S = 6
RAD = 2
NZ = 128
NX = 32
NY = 16


def draw_offsets(key, part):
    key_along, key_across, key_depth, key_order = jax.random.split(key, 4)
    row_index = jnp.arange(S, dtype=jnp.int32)
    along_x = jax.random.randint(key_along, (S,), -1, 2, dtype=jnp.int32)
    along_y = jax.random.randint(key_across, (S,), -RAD, RAD + 1, dtype=jnp.int32)
    along_z = jax.random.randint(key_depth, (S,), -RAD, RAD + 1, dtype=jnp.int32)
    along_x = jnp.where(row_index == 0, 1, jnp.where(row_index == 1, -1, along_x))
    along_y = jnp.where(row_index == 2, RAD, jnp.where(row_index == 3, -RAD, along_y))
    along_z = jnp.where(row_index == 0, RAD, jnp.where(row_index == 1, -RAD, along_z))
    reorder = jax.random.permutation(key_order, S)
    return jnp.stack([along_x, along_y, along_z], axis=1)[reorder].astype(jnp.int32)


def draw_mode_counts(key, part):
    key_counts, key_first, key_second = jax.random.split(key, 3)
    counts = jax.random.randint(key_counts, (C,), 1, MX + 1, dtype=jnp.int32)
    first_row = jax.random.randint(key_first, (), 0, C, dtype=jnp.int32)
    second = (first_row + jax.random.randint(key_second, (), 1, C, dtype=jnp.int32)) % C
    row_index = jnp.arange(C, dtype=jnp.int32)
    counts = jnp.where(row_index == first_row, MX, counts)
    return jnp.where(row_index == second, 1, counts).astype(jnp.int32)


def place_ends(entries, stream_key, least, largest):
    shape = entries.shape
    place = [jax.random.randint(jax.random.fold_in(stream_key, axis), (), 0, shape[axis]) for axis in range(len(shape))]
    entries = entries.at[tuple(place)].set(least)
    longest = shape.index(max(shape))
    place[longest] = (place[longest] + 1) % shape[longest]
    return entries.at[tuple(place)].set(largest)


def shard_levels(key, shape, pieces, smallest, high):
    gain = 1.0
    for dim, shards_of in pieces:
        draws = jax.random.uniform(jax.random.fold_in(jax.random.fold_in(key, 6), dim), (shards_of,), jnp.float32, smallest / len(pieces), high / len(pieces))
        gain = gain * jnp.repeat(jnp.exp(draws), shape[dim] // shards_of).reshape((-1,) + (1,) * (len(shape) - 1 - dim))
    return gain


def noise(stream_key, extent, deviation, most, cuts=(), kind=jnp.bfloat16):
    values = deviation * jax.random.normal(stream_key, extent, jnp.float32)
    if cuts:
        values = values * shard_levels(stream_key, extent, cuts, -0.22, 0.18)
    return jnp.clip(values, -most, most).astype(kind)


def setup_inputs(seed: int = 0, part: int = 0) -> dict:
    key_of = jax.random.split(jax.random.key(seed), 11)
    part_splits = jax.random.split(jax.random.fold_in(key_of[10], part), 11)
    features = noise(part_splits[0], (NX, NY, C, NZ), 1.0, 6.0, ((0, 16),))
    cotangent = noise(part_splits[1], (NX, NY, C, NZ), 1.0, 6.0, ((0, 16),))
    wall_flags = place_ends((jax.random.randint(part_splits[2], (NX, NY, NZ), 0, 8) < 1).astype(jnp.int32), jax.random.fold_in(part_splits[2], 1), 0, 1)
    mode_counts = draw_mode_counts(jax.random.fold_in(key_of[10], 71), part)
    offsets = draw_offsets(jax.random.fold_in(key_of[10], 71), part)
    point_weight = noise(key_of[5], (C, C), C ** -0.5, 0.75)
    kernel_weight = noise(key_of[6], (S, C, C), (S * C) ** -0.5, 0.3125)
    lap_weight = noise(key_of[7], (C, C), (42 * C) ** -0.5, 0.125)
    spec_weight = noise(key_of[8], (MX, C, C), (max(1, MX * C // NX)) ** -0.5, 1.0)
    bias = noise(key_of[9], (C,), 0.5, 3.0, (), jnp.float32)
    return {"features": features, "cotangent": cotangent, "wall_flags": wall_flags, "mode_counts": mode_counts, "offsets": offsets, "point_weight": point_weight, "kernel_weight": kernel_weight, "lap_weight": lap_weight, "spec_weight": spec_weight, "bias": bias}


def basis_table(mode_total, length):
    mode_index = jnp.arange(mode_total, dtype=jnp.float32)[:, None]
    cell_index = jnp.arange(length, dtype=jnp.float32)[None, :]
    phase_angle = math.pi / (2.0 * length) * mode_index * (2.0 * cell_index + 1.0)
    amplitude = jnp.where(mode_index == 0.0, math.sqrt(1.0 / length), math.sqrt(2.0 / length))
    return (amplitude * jnp.cos(phase_angle)).astype(jnp.bfloat16)

def spectral(values, spec_weight, kept_modes, basis, adjoint):
    wide_basis = basis.astype(jnp.float32)
    coefficients = jnp.einsum('kx,xycz->kycz', wide_basis, values.astype(jnp.float32)).astype(jnp.bfloat16)
    weights = spec_weight.astype(jnp.float32)
    if adjoint:
        masked = coefficients.astype(jnp.float32) * kept_modes[:, None, :, None]
        mixed_modes = jnp.einsum('koc,kyoz->kycz', weights, masked).astype(jnp.bfloat16)
    else:
        mixed_modes = jnp.einsum('koc,kycz->kyoz', weights, coefficients.astype(jnp.float32))
        mixed_modes = (mixed_modes * kept_modes[:, None, :, None]).astype(jnp.bfloat16)
    return jnp.einsum('kx,kyoz->xyoz', wide_basis, mixed_modes.astype(jnp.float32)).astype(jnp.bfloat16)

def laplace(values):
    padded = jnp.pad(values.astype(jnp.float32), ((1, 1), (1, 1), (0, 0), (1, 1)))
    centre_cells = padded[1:-1, 1:-1, :, 1:-1]
    neighbours = padded[2:, 1:-1, :, 1:-1] + padded[:-2, 1:-1, :, 1:-1]
    neighbours = neighbours + padded[1:-1, 2:, :, 1:-1] + padded[1:-1, :-2, :, 1:-1]
    neighbours = neighbours + padded[1:-1, 1:-1, :, 2:] + padded[1:-1, 1:-1, :, :-2]
    return (neighbours - 6.0 * centre_cells).astype(jnp.bfloat16)

def shifted(values, offset, direction):
    padded = jnp.pad(values, ((1, 1), (RAD, RAD), (0, 0), (RAD, RAD)))
    starts = ((1 + direction * offset[0]).astype(jnp.int32), (RAD + direction * offset[1]).astype(jnp.int32), jnp.int32(0), (RAD + direction * offset[2]).astype(jnp.int32))
    return lax.dynamic_slice(padded, starts, values.shape)

def mix_forward(weight, values):
    return jnp.einsum('oc,xycz->xyoz', weight.astype(jnp.float32), values.astype(jnp.float32))

def mix_back(weight, values):
    return jnp.einsum('oc,xyoz->xycz', weight.astype(jnp.float32), values.astype(jnp.float32))

def reference(features, cotangent, wall_flags, mode_counts, offsets, point_weight, kernel_weight, lap_weight, spec_weight, bias):
    basis = basis_table(MX, NX)
    kept_modes = (jnp.arange(MX, dtype=jnp.int32)[:, None] < mode_counts[None, :]).astype(jnp.float32)
    fluid_mask = (1 - wall_flags).astype(jnp.float32)[:, :, None, :]
    spectral_part = spectral(features, spec_weight, kept_modes, basis, False)
    lap_field = laplace(features)
    preact = mix_forward(point_weight, features) + mix_forward(lap_weight, lap_field)
    preact = preact + spectral_part.astype(jnp.float32) + bias[None, None, :, None]
    for tile in range(S):
        preact = preact + mix_forward(kernel_weight[tile], shifted(features, offsets[tile], 1))
    _, pullback = jax.vjp(partial(jax.nn.gelu, approximate=True), preact)
    weighted = (pullback(cotangent.astype(jnp.float32))[0] * fluid_mask).astype(jnp.bfloat16)
    spec_grad = spectral(weighted, spec_weight, kept_modes, basis, True)
    lap_grad = laplace(weighted)
    input_grad = mix_back(point_weight, weighted) + mix_back(lap_weight, lap_grad) + spec_grad.astype(jnp.float32)
    scaling = float(NX * NY * NZ) ** (-0.5)
    tile_grads = []
    wide_weighted = weighted.astype(jnp.float32)
    for tile in range(S):
        input_grad = input_grad + mix_back(kernel_weight[tile], shifted(weighted, offsets[tile], -1))
        moved = shifted(features, offsets[tile], 1).astype(jnp.float32)
        tile_grads.append(jnp.einsum('xyoz,xycz->oc', wide_weighted, moved) * scaling)
    kernel_grad = jnp.stack(tile_grads, axis=0)
    return (input_grad.astype(jnp.bfloat16), kernel_grad)
```

```python
import functools
from functools import partial
import math

import jax
import jax.numpy as jnp
from jax import lax
from jax.experimental import pallas as pl
from jax.experimental.pallas import tpu as pltpu
from jax.sharding import PartitionSpec as P

RAD = 2
MESH = pl.DeviceIdType.MESH


def with_halo(cells, sides, width):
    for axis, dim in sides:
        count = lax.axis_size(axis)
        ends = count - 1
        head = lax.slice_in_dim(cells, 0, width, axis=dim)
        tail = lax.slice_in_dim(cells, cells.shape[dim] - width, cells.shape[dim], axis=dim)
        cells = jnp.concatenate(
            [
                lax.ppermute(tail, axis, [(i, (i + 1) % count) for i in range(ends)]),
                cells,
                lax.ppermute(head, axis, [((i + 1) % count, i) for i in range(ends)]),
            ],
            axis=dim,
        )
    return cells


def basis_table(mode_total, length):
    mode_index = jnp.arange(mode_total, dtype=jnp.float32)[:, None]
    cell_index = jnp.arange(length, dtype=jnp.float32)[None, :]
    phase_angle = math.pi / (2.0 * length) * mode_index * (2.0 * cell_index + 1.0)
    amplitude = jnp.where(mode_index == 0.0, math.sqrt(1.0 / length), math.sqrt(2.0 / length))
    return (amplitude * jnp.cos(phase_angle)).astype(jnp.bfloat16)


def pencil_work(pencil, spec_weight, kept_modes, adjoint):
    basis = basis_table(spec_weight.shape[0], pencil.shape[0])
    coefficients = jnp.einsum(
        "kx,xycz->kycz", basis, pencil, preferred_element_type=jnp.float32
    ).astype(jnp.bfloat16)
    if adjoint:
        masked = coefficients * kept_modes[:, None, :, None].astype(jnp.bfloat16)
        mixed_modes = jnp.einsum(
            "koc,kyoz->kycz", spec_weight, masked, preferred_element_type=jnp.float32
        ).astype(jnp.bfloat16)
    else:
        mixed_modes = jnp.einsum(
            "koc,kycz->kyoz", spec_weight, coefficients, preferred_element_type=jnp.float32
        )
        mixed_modes = (mixed_modes * kept_modes[:, None, :, None]).astype(jnp.bfloat16)
    return jnp.einsum(
        "kx,kyoz->xyoz", basis, mixed_modes, preferred_element_type=jnp.float32
    ).astype(jnp.bfloat16)


def spectral(slab, spec_weight, kept_modes, adjoint):
    result = pencil_work(
        lax.all_to_all(slab, "gx", split_axis=1, concat_axis=0, tiled=True),
        spec_weight,
        kept_modes,
        adjoint,
    )
    return lax.all_to_all(result, "gx", split_axis=0, concat_axis=1, tiled=True)


def laplace_ext(extended):
    padded = jnp.pad(extended, ((0, 0), (1, 1), (0, 0), (1, 1))).astype(jnp.float32)
    centre_cells = padded[1:-1, 1:-1, :, 1:-1]
    neighbours = padded[2:, 1:-1, :, 1:-1] + padded[:-2, 1:-1, :, 1:-1]
    neighbours = neighbours + padded[1:-1, 2:, :, 1:-1] + padded[1:-1, :-2, :, 1:-1]
    neighbours = neighbours + padded[1:-1, 1:-1, :, 2:] + padded[1:-1, 1:-1, :, :-2]
    return (neighbours - 6.0 * centre_cells).astype(jnp.bfloat16)


def pad_sides(extended):
    return jnp.pad(extended, ((0, 0), (RAD, RAD), (0, 0), (RAD, RAD)))


def window_of(padded, offset, direction, slab_shape):
    starts = (
        1 + direction * offset[0],
        RAD + direction * offset[1],
        0,
        RAD + direction * offset[2],
    )
    return lax.dynamic_slice(padded, starts, slab_shape)


def gelu_slope(preact, upstream):
    _, pullback = jax.vjp(partial(jax.nn.gelu, approximate=True), preact)
    return pullback(upstream)[0]


def sum_over_gx(terms):
    count = lax.axis_size("gx")
    if terms.size % count:
        return lax.psum(terms, "gx")
    pieces = lax.all_to_all(terms.reshape(count, -1), "gx", split_axis=0, concat_axis=0, tiled=True)
    mine = jnp.sum(pieces, axis=0)
    copies = jnp.broadcast_to(mine[None, :], pieces.shape)
    gathered = lax.all_to_all(copies, "gx", split_axis=0, concat_axis=0, tiled=True)
    return gathered.reshape(terms.shape)


def per_device(
    features,
    cotangent,
    wall_flags,
    mode_counts,
    offsets,
    point_weight,
    kernel_weight,
    lap_weight,
    spec_weight,
    bias,
):
    mode_total = spec_weight.shape[0]
    tile_total = kernel_weight.shape[0]
    kept_modes = (jnp.arange(mode_total, dtype=jnp.int32)[:, None] < mode_counts[None, :]).astype(
        jnp.float32
    )
    fluid_mask = (1 - wall_flags).astype(jnp.float32)[:, :, None, :]
    extended = with_halo(features, (("gx", 0),), 1)
    padded_field = pad_sides(extended)
    local_part = jnp.einsum(
        "oc,xycz->xyoz", point_weight, features, preferred_element_type=jnp.float32
    )
    local_part = local_part + jnp.einsum(
        "oc,xycz->xyoz", lap_weight, laplace_ext(extended), preferred_element_type=jnp.float32
    )
    for tile in range(tile_total):
        moved = window_of(padded_field, offsets[tile], 1, features.shape)
        local_part = local_part + jnp.einsum(
            "oc,xycz->xyoz", kernel_weight[tile], moved, preferred_element_type=jnp.float32
        )
    local_part = local_part + bias[:, None]
    spectral_part = spectral(features, spec_weight, kept_modes, False)
    preact = local_part + spectral_part.astype(jnp.float32)
    weighted = (gelu_slope(preact, cotangent.astype(jnp.float32)) * fluid_mask).astype(jnp.bfloat16)
    spec_grad = spectral(weighted, spec_weight, kept_modes, True)
    ext_grad = with_halo(weighted, (("gx", 0),), 1)
    padded_grad = pad_sides(ext_grad)
    input_grad = jnp.einsum(
        "oc,xyoz->xycz", point_weight, weighted, preferred_element_type=jnp.float32
    )
    input_grad = input_grad + jnp.einsum(
        "oc,xyoz->xycz", lap_weight, laplace_ext(ext_grad), preferred_element_type=jnp.float32
    )
    input_grad = input_grad + spec_grad.astype(jnp.float32)
    tile_grads = []
    for tile in range(tile_total):
        back_moved = window_of(padded_grad, offsets[tile], -1, weighted.shape)
        input_grad = input_grad + jnp.einsum(
            "oc,xyoz->xycz", kernel_weight[tile], back_moved, preferred_element_type=jnp.float32
        )
        tile_grads.append(
            jnp.einsum("xyoz,xycz->oc", back_moved, features, preferred_element_type=jnp.float32)
        )
    local_grad = jnp.stack(tile_grads, axis=0)
    scaling = float(
        lax.axis_size("gx") * features.shape[0] * features.shape[1] * features.shape[3]
    ) ** (-0.5)
    summed = sum_over_gx(local_grad)
    return (input_grad.astype(jnp.bfloat16), summed * scaling)


def fused_kernel(
    count,
    feat_in,
    cot_in,
    wall_in,
    mode_in,
    offs,
    basis,
    point_in,
    tile_in,
    lap_in,
    spec_in,
    bias_in,
    out,
    kout,
    feat,
    cot,
    wall,
    mode_row,
    bias_row,
    wst,
    wm,
    wmt,
    wf,
    wb,
    mode,
    bias,
    zs,
    cat,
    local,
    acc,
    vh,
    pen1,
    pen2,
    stage1,
    stage2,
    spec1,
    spec2,
    wgt,
    halo1,
    halo2,
    kacc,
    kpart,
    kmine,
    kother,
    shift,
    send,
    recv,
    hsend,
    hrecv,
    rsend,
    rrecv,
    ksend,
    krecv,
    xsend,
    xrecv,
    load,
):
    me = lax.axis_index("gx")
    grp = lax.axis_index("groups")
    xl, ny, ch, nz = feat.shape
    modes = wm.shape[0]
    tiles = offs.shape[0]
    half = count // 2
    quads = half // 2
    f32, bf16 = jnp.float32, jnp.bfloat16
    side = me // half
    inner = me % half
    chip = inner // 2

    def push(src, dst, ssem, rsem, peer):
        return pltpu.make_async_remote_copy(
            src_ref=src,
            dst_ref=dst,
            send_sem=ssem,
            recv_sem=rsem,
            device_id=(grp, peer),
            device_id_type=MESH,
        )

    def each(low, high, body):
        def step(i, carry):
            body(i)
            return carry

        lax.fori_loop(low, high, step, 0)

    def place(cross, turn, core):
        return ((side + cross) % 2) * half + ((chip + turn) % quads) * 2 + core

    def by_core(j):
        core = j // half
        rest = j % half
        return place(1 - rest // quads, rest % quads, core)

    def by_side(j):
        rest = j % half
        return place(1 - j // half, rest // 2, rest % 2)

    def from_side(j):
        rest = j % half
        return place(1 - j // half, quads - rest // 2, rest % 2)

    def from_core(j):
        core = j // half
        rest = j % half
        return place(1 - rest // quads, quads - rest % quads, core)

    def others(low, high, order, body):
        def visit(j):
            peer = order(j)

            @pl.when(peer != me)
            def _():
                body(peer)

        each(low, high, visit)

    def share1(peer):
        return push(
            feat_in.at[:, peer], pen1.at[me], send.at[0, peer], recv.at[0, me], peer
        )

    def land1(src):
        return push(feat_in.at[:, src], pen1.at[src], send.at[0, src], recv.at[0, src], src)

    def give1(peer):
        return push(stage1.at[peer], spec1.at[me], send.at[1, peer], recv.at[1, me], peer)

    def back1(src):
        return push(stage1.at[src], spec1.at[src], send.at[1, src], recv.at[1, src], src)

    def share2(peer):
        return push(wgt.at[peer], pen2.at[me], send.at[2, peer], recv.at[2, me], peer)

    def land2(src):
        return push(wgt.at[src], pen2.at[src], send.at[2, src], recv.at[2, src], src)

    def give2(peer):
        return push(stage2.at[peer], spec2.at[me], send.at[3, peer], recv.at[3, me], peer)

    def back2(src):
        return push(stage2.at[src], spec2.at[src], send.at[3, src], recv.at[3, src], src)

    loads = [
        pltpu.make_async_copy(feat_in, feat, load.at[0]),
        pltpu.make_async_copy(point_in, wst.at[0], load.at[1]),
        pltpu.make_async_copy(lap_in, wst.at[1], load.at[2]),
        pltpu.make_async_copy(tile_in, wst.at[pl.ds(2, tiles)], load.at[3]),
        pltpu.make_async_copy(spec_in, wm, load.at[4]),
        pltpu.make_async_copy(mode_in, mode_row, load.at[5]),
        pltpu.make_async_copy(bias_in, bias_row, load.at[6]),
        pltpu.make_async_copy(wall_in, wall, load.at[7]),
        pltpu.make_async_copy(cot_in, cot, load.at[8]),
    ]
    for piece in loads:
        piece.start()

    barrier = pltpu.get_barrier_semaphore()
    each(
        1,
        count,
        lambda d: pl.semaphore_signal(
            barrier, inc=1, device_id=(grp, lax.rem(me + d, count)), device_id_type=MESH
        ),
    )
    pl.semaphore_wait(barrier, count - 1)

    def low_copy(peer):
        return push(feat_in.at[0], halo1.at[1], hsend.at[0], hrecv.at[0], peer)

    def high_copy(peer):
        return push(feat_in.at[xl - 1], halo1.at[0], hsend.at[1], hrecv.at[1], peer)

    def low_row(y, peer):
        return push(wgt.at[y, 0], halo2.at[1, y], rsend.at[0, y], rrecv.at[0, y], peer)

    def high_row(y, peer):
        return push(wgt.at[y, xl - 1], halo2.at[0, y], rsend.at[1, y], rrecv.at[1, y], peer)

    def below(body):
        @pl.when(me > 0)
        def _():
            body(me - 1)

    def above(body):
        @pl.when(me < count - 1)
        def _():
            body(me + 1)

    below(lambda peer: low_copy(peer).start())
    above(lambda peer: high_copy(peer).start())
    others(0, count, by_core, lambda peer: share1(peer).start())

    from_z = lax.broadcasted_iota(jnp.int32, (nz, nz), 0)
    to_z = lax.broadcasted_iota(jnp.int32, (nz, nz), 1)
    for m, dz in enumerate([dz for dz in range(-RAD, RAD + 1) if dz]):
        shift[:, m * nz : (m + 1) * nz] = jnp.where(from_z == to_z + dz, 1.0, 0.0).astype(bf16)

    @pl.when(me == 0)
    def _():
        halo1[0] = jnp.zeros(halo1.shape[1:], bf16)
        halo2[0] = jnp.zeros(halo2.shape[1:], bf16)

    @pl.when(me == count - 1)
    def _():
        halo1[1] = jnp.zeros(halo1.shape[1:], bf16)
        halo2[1] = jnp.zeros(halo2.shape[1:], bf16)

    for edge in (0, RAD + ny):
        for dz in range(2 * RAD + 1):
            for x in range(xl + 2):
                zs[dz, x, edge : edge + RAD] = jnp.zeros((RAD, ch, nz), bf16)

    moves = [dz for dz in range(-RAD, RAD + 1) if dz]
    group = math.gcd(ny, 8)

    def spread(take, place_x):
        def body(i):
            y = i * group
            v = take(pl.ds(y, group))
            zs[RAD, place_x, pl.ds(y + RAD, group)] = v
            flat = v.reshape(group * ch, nz)
            moved = jnp.dot(flat, shift[...], preferred_element_type=f32).astype(bf16)
            for m, dz in enumerate(moves):
                piece = moved[:, m * nz : (m + 1) * nz].reshape(group, ch, nz)
                zs[RAD + dz, place_x, pl.ds(y + RAD, group)] = piece

        each(0, ny // group, body)

    def gather_rows(direction):
        def body(y):
            for x in range(xl):
                lanes = slice(x * nz, (x + 1) * nz)
                centre = zs[RAD, x + 1, y + RAD]
                cat[y, 0:ch, lanes] = centre
                total = zs[RAD, x + 2, y + RAD].astype(f32) + zs[RAD, x, y + RAD].astype(f32)
                total = total + zs[RAD, x + 1, y + RAD + 1].astype(f32)
                total = total + zs[RAD, x + 1, y + RAD - 1].astype(f32)
                total = total + zs[RAD + 1, x + 1, y + RAD].astype(f32)
                total = total + zs[RAD - 1, x + 1, y + RAD].astype(f32)
                cat[y, ch : 2 * ch, lanes] = (total - 6.0 * centre.astype(f32)).astype(bf16)
                for t in range(tiles):
                    moved = zs[
                        RAD + direction * offs[t, 2],
                        x + 1 + direction * offs[t, 0],
                        y + RAD + direction * offs[t, 1],
                    ]
                    cat[y, (2 + t) * ch : (3 + t) * ch, lanes] = moved

        each(0, ny, body)

    unroll = math.gcd(ny, 4)

    def each_row(body):
        def rows_at(i):
            for r in range(unroll):
                body(i * unroll + r)

        each(0, ny // unroll, rows_at)

    def mix(weights):
        def body(y):
            local[y] = jnp.dot(weights[...], cat[y], preferred_element_type=f32)

        each_row(body)

    def gain(planes, src):
        wide = [p.astype(f32) for p in planes]
        for k in range(modes):
            total = acc[k]
            for j in range(xl):
                total = total + basis[k, src * xl + j] * wide[j]
            acc[k] = total

    def forward_mix():
        for k in range(modes):
            v = jnp.dot(wm[k], acc[k].astype(bf16), preferred_element_type=f32)
            v = jnp.where(mode[...] > float(k), v, 0.0)
            vh[k] = v.astype(bf16).astype(f32)

    def backward_mix():
        for k in range(modes):
            u = jnp.where(mode[...] > float(k), acc[k], 0.0).astype(bf16)
            v = jnp.dot(wmt[k], u, preferred_element_type=f32)
            vh[k] = v.astype(bf16).astype(f32)

    def expand(stage, peer):
        for j in range(xl):
            total = basis[0, peer * xl + j] * vh[0]
            for k in range(1, modes):
                total = total + basis[k, peer * xl + j] * vh[k]
            stage[peer, j] = total.astype(bf16)

    loads[0].wait()
    for x in range(xl):
        spread(lambda y: feat[x, y], x + 1)
    for piece in loads[1:]:
        piece.wait()

    row_at = lax.broadcasted_iota(jnp.int32, (ch, ch), 0)
    col_at = lax.broadcasted_iota(jnp.int32, (ch, ch), 1)
    diagonal = row_at == col_at
    unit = jnp.where(diagonal, 1.0, 0.0).astype(bf16)

    def upright(row):
        spread_out = jnp.where(diagonal, jnp.broadcast_to(row, (ch, ch)), 0.0)
        column = jnp.sum(spread_out, axis=1, keepdims=True)
        return jnp.broadcast_to(column, (ch, nz))

    mode[...] = upright(mode_row[...].astype(f32))
    bias[...] = upright(bias_row[...])

    def flipped(block):
        return lax.dot_general(
            block, unit, (((0,), (0,)), ((), ())), preferred_element_type=f32
        ).astype(bf16)

    for t in range(2 + tiles):
        wf[:, t * ch : (t + 1) * ch] = wst[t]
        wb[:, t * ch : (t + 1) * ch] = flipped(wst[t])

    def flip_mode(k):
        wmt[k] = flipped(wm[k])

    each(0, modes, flip_mode)

    below(lambda peer: high_copy(peer).wait_recv())
    above(lambda peer: low_copy(peer).wait_recv())
    spread(lambda y: halo1[0, y], 0)
    spread(lambda y: halo1[1, y], xl + 1)
    gather_rows(1)
    mix(wf)

    acc[...] = jnp.zeros(acc.shape, f32)
    gain([feat[j, me] for j in range(xl)], me)

    def take1(src):
        land1(src).wait_recv()
        gain([pen1[src, j] for j in range(xl)], src)

    others(0, count, from_side, take1)
    forward_mix()

    def hand1(peer):
        expand(stage1, peer)
        give1(peer).start()

    others(0, count, by_side, hand1)
    expand(stage1, me)
    root = math.sqrt(2.0 / math.pi)

    def slope(y, planes):
        for x in range(xl):
            v = local[y, :, x * nz : (x + 1) * nz] + planes[x].astype(f32) + bias[...]
            square = v * v
            t = jnp.tanh(root * (v + 0.044715 * (square * v)))
            g = 0.5 * (1.0 + t)
            g = g + (0.5 * v) * ((1.0 - t * t) * (root * (1.0 + (3.0 * 0.044715) * square)))
            fluid = (1 - wall[x, pl.ds(y, 1), :]).astype(f32)
            wgt[y, x] = ((cot[x, y].astype(f32) * g) * fluid).astype(bf16)
        below(lambda peer: low_row(y, peer).start())
        above(lambda peer: high_row(y, peer).start())

    slope(me, [stage1[me, j] for j in range(xl)])

    def turn(src):
        back1(src).wait_recv()
        slope(src, [spec1[src, j] for j in range(xl)])
        share2(src).start()

    others(0, count, by_core, turn)

    for x in range(xl):
        spread(lambda y: wgt[y, x], x + 1)

    def halo_rows(y):
        below(lambda peer: high_row(y, peer).wait_recv())
        above(lambda peer: low_row(y, peer).wait_recv())

    each(0, ny, halo_rows)
    spread(lambda y: halo2[0, y], 0)
    spread(lambda y: halo2[1, y], xl + 1)
    gather_rows(-1)

    kacc[...] = jnp.zeros(kacc.shape, f32)

    def tile_grad(y):
        field = jnp.concatenate([feat[x, y] for x in range(xl)], axis=1)
        kacc[...] += lax.dot_general(
            cat[y, 2 * ch :, :], field, (((1,), (1,)), ((), ())), preferred_element_type=f32
        )

    each_row(tile_grad)
    rows = kpart.shape[1]

    def strip(p):
        return kacc.at[pl.ds(p * rows, rows)]

    def near(body):
        def visit(d):
            body((inner + d) % half)

        each(1, half, visit)

    def ksend_to(p):
        return push(
            strip(p), kpart.at[inner], ksend.at[0, p], krecv.at[0, inner], side * half + p
        )

    def kland(p):
        return push(strip(p), kpart.at[p], ksend.at[0, p], krecv.at[0, p], side * half + p)

    near(lambda p: ksend_to(p).start())
    mix(wb)

    acc[...] = jnp.zeros(acc.shape, f32)
    gain([wgt[me, j] for j in range(xl)], me)

    def take2(src):
        land2(src).wait_recv()
        gain([pen2[src, j] for j in range(xl)], src)

    others(0, count, from_side, take2)
    backward_mix()

    def hand2(peer):
        expand(stage2, peer)
        give2(peer).start()

    others(0, count, by_side, hand2)
    expand(stage2, me)

    kpart[inner] = kacc[pl.ds(inner * rows, rows)]
    near(lambda p: kland(p).wait_recv())
    part_sum = kpart[0]
    for p in range(1, half):
        part_sum = part_sum + kpart[p]
    kmine[...] = part_sum
    partner = ((side + 1) % 2) * half + inner
    across = push(kmine, kother, xsend.at[0], xrecv.at[0], partner)
    across.start()

    def finish(y, planes):
        for x in range(xl):
            total = local[y, :, x * nz : (x + 1) * nz] + planes[x].astype(f32)
            out[x, y] = total.astype(bf16)

    finish(me, [stage2[me, j] for j in range(xl)])

    def last(src):
        back2(src).wait_recv()
        finish(src, [spec2[src, j] for j in range(xl)])

    others(0, half, from_core, last)

    across.wait_recv()
    kout[inner] = (kmine[...] + kother[...]) * (float(count * xl * ny * nz) ** -0.5)

    def kspread(p):
        return push(
            kout.at[inner], kout.at[inner], ksend.at[1, p], krecv.at[1, inner], side * half + p
        )

    def kcollect(p):
        return push(kout.at[inner], kout.at[p], ksend.at[1, p], krecv.at[1, p], side * half + p)

    near(lambda p: kspread(p).start())
    others(half, count, from_core, last)
    near(lambda p: kcollect(p).wait_recv())

    below(lambda peer: low_copy(peer).wait_send())
    above(lambda peer: high_copy(peer).wait_send())

    def row_sent(y):
        below(lambda peer: low_row(y, peer).wait_send())
        above(lambda peer: high_row(y, peer).wait_send())

    each(0, ny, row_sent)
    across.wait_send()

    def near_sent(p):
        ksend_to(p).wait_send()
        kspread(p).wait_send()

    near(near_sent)

    def drain(peer):
        share1(peer).wait_send()
        give1(peer).wait_send()
        share2(peer).wait_send()
        give2(peer).wait_send()

    others(0, count, by_side, drain)


def fits_kernel(count, features, kernel_weight):
    xl, ny, ch, nz = features.shape
    cells = xl * ny * ch * nz
    tile_rows = kernel_weight.shape[0] * ch
    if ny != count or count % 4 or nz % 128 or ch % 16 or tile_rows % (8 * (count // 2)):
        return False
    return 80 * cells < 24 * 2**20


def fused_device(
    features,
    cotangent,
    wall_flags,
    mode_counts,
    offsets,
    point_weight,
    kernel_weight,
    lap_weight,
    spec_weight,
    bias,
):
    count = lax.axis_size("gx")
    if not fits_kernel(count, features, kernel_weight):
        return per_device(
            features,
            cotangent,
            wall_flags,
            mode_counts,
            offsets,
            point_weight,
            kernel_weight,
            lap_weight,
            spec_weight,
            bias,
        )
    xl, ny, ch, nz = features.shape
    modes, tiles = spec_weight.shape[0], kernel_weight.shape[0]
    half = count // 2
    rows = tiles * ch // half
    f32, bf16 = jnp.float32, jnp.bfloat16
    dma = pltpu.SemaphoreType.DMA
    hbm = pl.BlockSpec(memory_space=pltpu.HBM)
    vmem = pl.BlockSpec(memory_space=pltpu.VMEM)
    smem = pl.BlockSpec(memory_space=pltpu.SMEM)
    field_grad, tile_grad = pl.pallas_call(
        functools.partial(fused_kernel, count),
        out_shape=(
            jax.ShapeDtypeStruct(features.shape, bf16),
            jax.ShapeDtypeStruct((half, rows, ch), f32),
        ),
        in_specs=[hbm, hbm, hbm, hbm, smem, smem, hbm, hbm, hbm, hbm, hbm],
        out_specs=(vmem, vmem),
        scratch_shapes=[
            pltpu.VMEM((xl, ny, ch, nz), bf16),
            pltpu.VMEM((xl, ny, ch, nz), bf16),
            pltpu.VMEM((xl, ny, nz), jnp.int32),
            pltpu.VMEM((1, ch), jnp.int32),
            pltpu.VMEM((1, ch), f32),
            pltpu.VMEM((2 + tiles, ch, ch), bf16),
            pltpu.VMEM((modes, ch, ch), bf16),
            pltpu.VMEM((modes, ch, ch), bf16),
            pltpu.VMEM((ch, (2 + tiles) * ch), bf16),
            pltpu.VMEM((ch, (2 + tiles) * ch), bf16),
            pltpu.VMEM((ch, nz), f32),
            pltpu.VMEM((ch, nz), f32),
            pltpu.VMEM((2 * RAD + 1, xl + 2, ny + 2 * RAD, ch, nz), bf16),
            pltpu.VMEM((ny, (2 + tiles) * ch, xl * nz), bf16),
            pltpu.VMEM((ny, ch, xl * nz), f32),
            pltpu.VMEM((modes, ch, nz), f32),
            pltpu.VMEM((modes, ch, nz), f32),
            pltpu.VMEM((count, xl, ch, nz), bf16),
            pltpu.VMEM((count, xl, ch, nz), bf16),
            pltpu.VMEM((count, xl, ch, nz), bf16),
            pltpu.VMEM((count, xl, ch, nz), bf16),
            pltpu.VMEM((count, xl, ch, nz), bf16),
            pltpu.VMEM((count, xl, ch, nz), bf16),
            pltpu.VMEM((ny, xl, ch, nz), bf16),
            pltpu.VMEM((2, ny, ch, nz), bf16),
            pltpu.VMEM((2, ny, ch, nz), bf16),
            pltpu.VMEM((tiles * ch, ch), f32),
            pltpu.VMEM((half, rows, ch), f32),
            pltpu.VMEM((rows, ch), f32),
            pltpu.VMEM((rows, ch), f32),
            pltpu.VMEM((nz, 2 * RAD * nz), bf16),
            dma((4, count)),
            dma((4, count)),
            dma((2,)),
            dma((2,)),
            dma((2, ny)),
            dma((2, ny)),
            dma((2, half)),
            dma((2, half)),
            dma((1,)),
            dma((1,)),
            dma((9,)),
        ],
        compiler_params=pltpu.CompilerParams(
            collective_id=0, has_side_effects=True, vmem_limit_bytes=48 * 2**20
        ),
    )(
        features,
        cotangent,
        wall_flags,
        mode_counts.reshape(1, ch),
        offsets,
        basis_table(modes, count * xl).astype(f32),
        point_weight,
        kernel_weight,
        lap_weight,
        spec_weight,
        bias.reshape(1, ch),
    )
    return field_grad, tile_grad.reshape(kernel_weight.shape)


def solution(mesh):
    return jax.shard_map(
        fused_device,
        mesh=mesh,
        in_specs=(
            P(("groups", "gx"), None, None, None),
            P(("groups", "gx"), None, None, None),
            P(("groups", "gx"), None, None),
            P(),
            P(),
            P(),
            P(),
            P(),
            P(),
            P(),
        ),
        out_specs=(P(("groups", "gx"), None, None, None), P("groups", None, None)),
        check_vma=False,
    )
```

```python
import functools
from functools import partial
import math

import jax
import jax.numpy as jnp
from jax import lax
from jax.experimental import pallas as pl
from jax.experimental.pallas import tpu as pltpu
from jax.sharding import PartitionSpec as P

RAD = 2
MESH = pl.DeviceIdType.MESH


def with_halo(cells, sides, width):
    for axis, dim in sides:
        count = lax.axis_size(axis)
        ends = count - 1
        head = lax.slice_in_dim(cells, 0, width, axis=dim)
        tail = lax.slice_in_dim(cells, cells.shape[dim] - width, cells.shape[dim], axis=dim)
        cells = jnp.concatenate(
            [
                lax.ppermute(tail, axis, [(i, (i + 1) % count) for i in range(ends)]),
                cells,
                lax.ppermute(head, axis, [((i + 1) % count, i) for i in range(ends)]),
            ],
            axis=dim,
        )
    return cells


def basis_table(mode_total, length):
    mode_index = jnp.arange(mode_total, dtype=jnp.float32)[:, None]
    cell_index = jnp.arange(length, dtype=jnp.float32)[None, :]
    phase_angle = math.pi / (2.0 * length) * mode_index * (2.0 * cell_index + 1.0)
    amplitude = jnp.where(mode_index == 0.0, math.sqrt(1.0 / length), math.sqrt(2.0 / length))
    return (amplitude * jnp.cos(phase_angle)).astype(jnp.bfloat16)


def pencil_work(pencil, spec_weight, kept_modes, adjoint):
    basis = basis_table(spec_weight.shape[0], pencil.shape[0])
    coefficients = jnp.einsum(
        "kx,xycz->kycz", basis, pencil, preferred_element_type=jnp.float32
    ).astype(jnp.bfloat16)
    if adjoint:
        masked = coefficients * kept_modes[:, None, :, None].astype(jnp.bfloat16)
        mixed_modes = jnp.einsum(
            "koc,kyoz->kycz", spec_weight, masked, preferred_element_type=jnp.float32
        ).astype(jnp.bfloat16)
    else:
        mixed_modes = jnp.einsum(
            "koc,kycz->kyoz", spec_weight, coefficients, preferred_element_type=jnp.float32
        )
        mixed_modes = (mixed_modes * kept_modes[:, None, :, None]).astype(jnp.bfloat16)
    return jnp.einsum(
        "kx,kyoz->xyoz", basis, mixed_modes, preferred_element_type=jnp.float32
    ).astype(jnp.bfloat16)


def spectral(slab, spec_weight, kept_modes, adjoint):
    result = pencil_work(
        lax.all_to_all(slab, "gx", split_axis=1, concat_axis=0, tiled=True),
        spec_weight,
        kept_modes,
        adjoint,
    )
    return lax.all_to_all(result, "gx", split_axis=0, concat_axis=1, tiled=True)


def laplace_ext(extended):
    padded = jnp.pad(extended, ((0, 0), (1, 1), (0, 0), (1, 1))).astype(jnp.float32)
    centre_cells = padded[1:-1, 1:-1, :, 1:-1]
    neighbours = padded[2:, 1:-1, :, 1:-1] + padded[:-2, 1:-1, :, 1:-1]
    neighbours = neighbours + padded[1:-1, 2:, :, 1:-1] + padded[1:-1, :-2, :, 1:-1]
    neighbours = neighbours + padded[1:-1, 1:-1, :, 2:] + padded[1:-1, 1:-1, :, :-2]
    return (neighbours - 6.0 * centre_cells).astype(jnp.bfloat16)


def pad_sides(extended):
    return jnp.pad(extended, ((0, 0), (RAD, RAD), (0, 0), (RAD, RAD)))


def window_of(padded, offset, direction, slab_shape):
    starts = (
        1 + direction * offset[0],
        RAD + direction * offset[1],
        0,
        RAD + direction * offset[2],
    )
    return lax.dynamic_slice(padded, starts, slab_shape)


def gelu_slope(preact, upstream):
    _, pullback = jax.vjp(partial(jax.nn.gelu, approximate=True), preact)
    return pullback(upstream)[0]


def sum_over_gx(terms):
    count = lax.axis_size("gx")
    if terms.size % count:
        return lax.psum(terms, "gx")
    pieces = lax.all_to_all(terms.reshape(count, -1), "gx", split_axis=0, concat_axis=0, tiled=True)
    mine = jnp.sum(pieces, axis=0)
    copies = jnp.broadcast_to(mine[None, :], pieces.shape)
    gathered = lax.all_to_all(copies, "gx", split_axis=0, concat_axis=0, tiled=True)
    return gathered.reshape(terms.shape)


def per_device(
    features,
    cotangent,
    wall_flags,
    mode_counts,
    offsets,
    point_weight,
    kernel_weight,
    lap_weight,
    spec_weight,
    bias,
):
    mode_total = spec_weight.shape[0]
    tile_total = kernel_weight.shape[0]
    kept_modes = (jnp.arange(mode_total, dtype=jnp.int32)[:, None] < mode_counts[None, :]).astype(
        jnp.float32
    )
    fluid_mask = (1 - wall_flags).astype(jnp.float32)[:, :, None, :]
    extended = with_halo(features, (("gx", 0),), 1)
    padded_field = pad_sides(extended)
    local_part = jnp.einsum(
        "oc,xycz->xyoz", point_weight, features, preferred_element_type=jnp.float32
    )
    local_part = local_part + jnp.einsum(
        "oc,xycz->xyoz", lap_weight, laplace_ext(extended), preferred_element_type=jnp.float32
    )
    for tile in range(tile_total):
        moved = window_of(padded_field, offsets[tile], 1, features.shape)
        local_part = local_part + jnp.einsum(
            "oc,xycz->xyoz", kernel_weight[tile], moved, preferred_element_type=jnp.float32
        )
    local_part = local_part + bias[:, None]
    spectral_part = spectral(features, spec_weight, kept_modes, False)
    preact = local_part + spectral_part.astype(jnp.float32)
    weighted = (gelu_slope(preact, cotangent.astype(jnp.float32)) * fluid_mask).astype(jnp.bfloat16)
    spec_grad = spectral(weighted, spec_weight, kept_modes, True)
    ext_grad = with_halo(weighted, (("gx", 0),), 1)
    padded_grad = pad_sides(ext_grad)
    input_grad = jnp.einsum(
        "oc,xyoz->xycz", point_weight, weighted, preferred_element_type=jnp.float32
    )
    input_grad = input_grad + jnp.einsum(
        "oc,xyoz->xycz", lap_weight, laplace_ext(ext_grad), preferred_element_type=jnp.float32
    )
    input_grad = input_grad + spec_grad.astype(jnp.float32)
    tile_grads = []
    for tile in range(tile_total):
        back_moved = window_of(padded_grad, offsets[tile], -1, weighted.shape)
        input_grad = input_grad + jnp.einsum(
            "oc,xyoz->xycz", kernel_weight[tile], back_moved, preferred_element_type=jnp.float32
        )
        tile_grads.append(
            jnp.einsum("xyoz,xycz->oc", back_moved, features, preferred_element_type=jnp.float32)
        )
    local_grad = jnp.stack(tile_grads, axis=0)
    scaling = float(
        lax.axis_size("gx") * features.shape[0] * features.shape[1] * features.shape[3]
    ) ** (-0.5)
    summed = sum_over_gx(local_grad)
    return (input_grad.astype(jnp.bfloat16), summed * scaling)


def fused_kernel(
    count,
    feat_in,
    cot_in,
    wall_in,
    mode_in,
    offs_in,
    basis_in,
    point_in,
    tile_in,
    lap_in,
    spec_in,
    bias_in,
    out,
    kout,
    res,
    feat,
    cot,
    wall,
    mode_row,
    bias_row,
    offs,
    basis,
    wst,
    wm,
    wmt,
    wf,
    wb,
    mode,
    bias,
    zs,
    cat,
    local,
    acc,
    vh,
    pen1,
    pen2,
    stage1,
    stage2,
    spec1,
    spec2,
    wgt,
    halo1,
    halo2,
    kacc,
    kpart,
    kmine,
    kother,
    ksum,
    shift,
    send,
    recv,
    hsend,
    hrecv,
    rsend,
    rrecv,
    ksend,
    krecv,
    xsend,
    xrecv,
    fsend,
    frecv,
    store,
    load,
):
    me = lax.axis_index("gx")
    grp = lax.axis_index("groups")
    xl, ny, ch, nz = feat.shape
    modes = wm.shape[0]
    tiles = offs.shape[1]
    half = count // 2
    quads = half // 2
    f32, bf16 = jnp.float32, jnp.bfloat16
    side = me // half
    inner = me % half
    chip = inner // 2

    def push(src, dst, ssem, rsem, peer):
        return pltpu.make_async_remote_copy(
            src_ref=src,
            dst_ref=dst,
            send_sem=ssem,
            recv_sem=rsem,
            device_id=(grp, peer),
            device_id_type=MESH,
        )

    def each(low, high, body):
        def step(i, carry):
            body(i)
            return carry

        lax.fori_loop(low, high, step, 0)

    def place(cross, turn, core):
        return ((side + cross) % 2) * half + ((chip + turn) % quads) * 2 + core

    def by_core(j):
        core = j // half
        rest = j % half
        return place(1 - rest // quads, rest % quads, core)

    def by_side(j):
        rest = j % half
        return place(1 - j // half, rest // 2, rest % 2)

    def from_side(j):
        rest = j % half
        return place(1 - j // half, quads - rest // 2, rest % 2)

    def from_core(j):
        core = j // half
        rest = j % half
        return place(1 - rest // quads, quads - rest % quads, core)

    def others(low, high, order, body):
        def visit(j):
            peer = order(j)

            @pl.when(peer != me)
            def _():
                body(peer)

        each(low, high, visit)

    def share1(peer):
        return push(
            feat_in.at[:, peer], pen1.at[me], send.at[0, peer], recv.at[0, me], peer
        )

    def land1(src):
        return push(feat_in.at[:, src], pen1.at[src], send.at[0, src], recv.at[0, src], src)

    def give1(peer):
        return push(stage1.at[peer], spec1.at[me], send.at[1, peer], recv.at[1, me], peer)

    def back1(src):
        return push(stage1.at[src], spec1.at[src], send.at[1, src], recv.at[1, src], src)

    def share2(peer):
        return push(wgt.at[peer], pen2.at[me], send.at[2, peer], recv.at[2, me], peer)

    def land2(src):
        return push(wgt.at[src], pen2.at[src], send.at[2, src], recv.at[2, src], src)

    def give2(peer):
        return push(stage2.at[peer], spec2.at[me], send.at[3, peer], recv.at[3, me], peer)

    def back2(src):
        return push(stage2.at[src], spec2.at[src], send.at[3, src], recv.at[3, src], src)

    loads = [
        pltpu.make_async_copy(feat_in, feat, load.at[0]),
        pltpu.make_async_copy(point_in, wst.at[0], load.at[1]),
        pltpu.make_async_copy(lap_in, wst.at[1], load.at[2]),
        pltpu.make_async_copy(tile_in, wst.at[pl.ds(2, tiles)], load.at[3]),
        pltpu.make_async_copy(spec_in, wm, load.at[4]),
        pltpu.make_async_copy(mode_in, mode_row, load.at[5]),
        pltpu.make_async_copy(bias_in, bias_row, load.at[6]),
        pltpu.make_async_copy(wall_in, wall, load.at[7]),
        pltpu.make_async_copy(cot_in, cot, load.at[8]),
        pltpu.make_async_copy(offs_in, offs, load.at[9]),
        pltpu.make_async_copy(basis_in, basis, load.at[10]),
    ]
    for piece in loads:
        piece.start()

    barrier = pltpu.get_barrier_semaphore()
    each(
        1,
        count,
        lambda d: pl.semaphore_signal(
            barrier, inc=1, device_id=(grp, lax.rem(me + d, count)), device_id_type=MESH
        ),
    )
    pl.semaphore_wait(barrier, count - 1)

    low_edge = half - 1

    def low_copy(peer):
        return push(feat_in.at[0], halo1.at[1], hsend.at[0], hrecv.at[0], peer)

    def high_copy(peer):
        return push(feat_in.at[xl - 1], halo1.at[0], hsend.at[1], hrecv.at[1], peer)

    def low_cross():
        part = pl.ds(half - 1, half + 1)
        return push(feat_in.at[0, part], halo1.at[1, part], hsend.at[0], hrecv.at[0], low_edge)

    def high_cross():
        part = pl.ds(0, half + 1)
        return push(feat_in.at[xl - 1, part], halo1.at[0, part], hsend.at[1], hrecv.at[1], half)

    def low_pass():
        return push(pen1.at[half, 0], halo1.at[1, me], fsend.at[0], frecv.at[me], low_edge)

    def high_pass():
        return push(
            pen1.at[low_edge, xl - 1], halo1.at[0, me], fsend.at[0], frecv.at[me], half
        )

    def low_row(y, peer):
        return push(wgt.at[y, 0], halo2.at[1, y], rsend.at[0, y], rrecv.at[0, y], peer)

    def high_row(y, peer):
        return push(wgt.at[y, xl - 1], halo2.at[0, y], rsend.at[1, y], rrecv.at[1, y], peer)

    def low_relay():
        return push(
            pen2.at[half, 0], halo2.at[1, me], fsend.at[0], rrecv.at[0, me], low_edge
        )

    def high_relay():
        return push(
            pen2.at[low_edge, xl - 1], halo2.at[0, me], fsend.at[0], rrecv.at[1, me], half
        )

    def low_own(y):
        return (me > 0) & ((me != half) | (y >= low_edge))

    def high_own(y):
        return (me < count - 1) & ((me != low_edge) | (y <= half))

    def when(cond, body):
        @pl.when(cond)
        def _():
            body()

    inside_low = (me > 0) & (me != half)
    inside_high = (me < count - 1) & (me != low_edge)
    when(me == half, lambda: low_cross().start())
    when(me == low_edge, lambda: high_cross().start())
    when(inside_low, lambda: low_copy(me - 1).start())
    when(inside_high, lambda: high_copy(me + 1).start())
    others(0, count, by_core, lambda peer: share1(peer).start())

    from_z = lax.broadcasted_iota(jnp.int32, (nz, nz), 0)
    to_z = lax.broadcasted_iota(jnp.int32, (nz, nz), 1)
    for m, dz in enumerate([dz for dz in range(-RAD, RAD + 1) if dz]):
        shift[:, m * nz : (m + 1) * nz] = jnp.where(from_z == to_z + dz, 1.0, 0.0).astype(bf16)

    @pl.when(me == 0)
    def _():
        halo1[0] = jnp.zeros(halo1.shape[1:], bf16)
        halo2[0] = jnp.zeros(halo2.shape[1:], bf16)

    @pl.when(me == count - 1)
    def _():
        halo1[1] = jnp.zeros(halo1.shape[1:], bf16)
        halo2[1] = jnp.zeros(halo2.shape[1:], bf16)

    for edge in (0, RAD + ny):
        for dz in range(2 * RAD + 1):
            for x in range(xl + 2):
                zs[dz, x, edge : edge + RAD] = jnp.zeros((RAD, ch, nz), bf16)

    moves = [dz for dz in range(-RAD, RAD + 1) if dz]
    group = math.gcd(ny, 8)

    def spread(take, place_x):
        def body(i):
            y = i * group
            v = take(pl.ds(y, group))
            zs[RAD, place_x, pl.ds(y + RAD, group)] = v
            flat = v.reshape(group * ch, nz)
            moved = jnp.dot(flat, shift[...], preferred_element_type=f32).astype(bf16)
            for m, dz in enumerate(moves):
                piece = moved[:, m * nz : (m + 1) * nz].reshape(group, ch, nz)
                zs[RAD + dz, place_x, pl.ds(y + RAD, group)] = piece

        each(0, ny // group, body)

    def gather_rows(direction):
        def body(y):
            for x in range(xl):
                lanes = slice(x * nz, (x + 1) * nz)
                centre = zs[RAD, x + 1, y + RAD]
                cat[y, 0:ch, lanes] = centre
                total = zs[RAD, x + 2, y + RAD].astype(f32) + zs[RAD, x, y + RAD].astype(f32)
                total = total + zs[RAD, x + 1, y + RAD + 1].astype(f32)
                total = total + zs[RAD, x + 1, y + RAD - 1].astype(f32)
                total = total + zs[RAD + 1, x + 1, y + RAD].astype(f32)
                total = total + zs[RAD - 1, x + 1, y + RAD].astype(f32)
                cat[y, ch : 2 * ch, lanes] = (total - 6.0 * centre.astype(f32)).astype(bf16)
                for t in range(tiles):
                    moved = zs[
                        RAD + direction * offs[2, t],
                        x + 1 + direction * offs[0, t],
                        y + RAD + direction * offs[1, t],
                    ]
                    cat[y, (2 + t) * ch : (3 + t) * ch, lanes] = moved

        each(0, ny, body)

    unroll = math.gcd(ny, 4)

    def each_row(body):
        def rows_at(i):
            for r in range(unroll):
                body(i * unroll + r)

        each(0, ny // unroll, rows_at)

    def mix(weights):
        def body(y):
            local[y] = jnp.dot(weights[...], cat[y], preferred_element_type=f32)

        each_row(body)

    def gain(planes, src):
        wide = [p.astype(f32) for p in planes]
        for k in range(modes):
            total = acc[k]
            for j in range(xl):
                total = total + basis[k, src * xl + j] * wide[j]
            acc[k] = total

    def forward_mix():
        for k in range(modes):
            v = jnp.dot(wm[k], acc[k].astype(bf16), preferred_element_type=f32)
            v = jnp.where(mode[...] > float(k), v, 0.0)
            vh[k] = v.astype(bf16).astype(f32)

    def backward_mix():
        for k in range(modes):
            u = jnp.where(mode[...] > float(k), acc[k], 0.0).astype(bf16)
            v = jnp.dot(wmt[k], u, preferred_element_type=f32)
            vh[k] = v.astype(bf16).astype(f32)

    def expand(stage, peer):
        for j in range(xl):
            total = basis[0, peer * xl + j] * vh[0]
            for k in range(1, modes):
                total = total + basis[k, peer * xl + j] * vh[k]
            stage[peer, j] = total.astype(bf16)

    loads[0].wait()
    for x in range(xl):
        spread(lambda y: feat[x, y], x + 1)
    for piece in loads[1:]:
        piece.wait()

    row_at = lax.broadcasted_iota(jnp.int32, (ch, ch), 0)
    col_at = lax.broadcasted_iota(jnp.int32, (ch, ch), 1)
    diagonal = row_at == col_at
    unit = jnp.where(diagonal, 1.0, 0.0).astype(bf16)

    def upright(row):
        spread_out = jnp.where(diagonal, jnp.broadcast_to(row, (ch, ch)), 0.0)
        column = jnp.sum(spread_out, axis=1, keepdims=True)
        return jnp.broadcast_to(column, (ch, nz))

    mode[...] = upright(mode_row[...].astype(f32))
    bias[...] = upright(bias_row[...])

    def flipped(block):
        return lax.dot_general(
            block, unit, (((0,), (0,)), ((), ())), preferred_element_type=f32
        ).astype(bf16)

    for t in range(2 + tiles):
        wf[:, t * ch : (t + 1) * ch] = wst[t]
        wb[:, t * ch : (t + 1) * ch] = flipped(wst[t])

    def flip_mode(k):
        wmt[k] = flipped(wm[k])

    each(0, modes, flip_mode)

    def passed_low(i):
        push(
            pen1.at[low_edge, xl - 1], halo1.at[0, i], fsend.at[0], frecv.at[i], low_edge
        ).wait_recv()

    def passed_high(i):
        push(pen1.at[half, 0], halo1.at[1, i], fsend.at[0], frecv.at[i], half).wait_recv()

    def forward_stencil():
        when(inside_low, lambda: high_copy(me - 1).wait_recv())
        when(inside_high, lambda: low_copy(me + 1).wait_recv())

        @pl.when(me == half)
        def _():
            high_cross_here = push(
                feat_in.at[xl - 1, pl.ds(0, half + 1)],
                halo1.at[0, pl.ds(0, half + 1)],
                hsend.at[1],
                hrecv.at[1],
                low_edge,
            )
            high_cross_here.wait_recv()
            each(half + 1, count, passed_low)

        @pl.when(me == low_edge)
        def _():
            low_cross_here = push(
                feat_in.at[0, pl.ds(half - 1, half + 1)],
                halo1.at[1, pl.ds(half - 1, half + 1)],
                hsend.at[0],
                hrecv.at[0],
                half,
            )
            low_cross_here.wait_recv()
            each(0, half - 1, passed_high)

        spread(lambda y: halo1[0, y], 0)
        spread(lambda y: halo1[1, y], xl + 1)
        gather_rows(1)
        mix(wf)

    core = me % 2
    when(core == 1, forward_stencil)

    acc[...] = jnp.zeros(acc.shape, f32)
    gain([feat[j, me] for j in range(xl)], me)

    def take1(src):
        land1(src).wait_recv()
        when((src == half) & (me < low_edge), lambda: low_pass().start())
        when((src == low_edge) & (me > half), lambda: high_pass().start())
        gain([pen1[src, j] for j in range(xl)], src)

    others(0, count, from_side, take1)
    forward_mix()

    def hand1(peer):
        expand(stage1, peer)
        give1(peer).start()

    others(0, count, by_side, hand1)
    expand(stage1, me)
    when(core == 0, forward_stencil)
    root = math.sqrt(2.0 / math.pi)

    def slope(y, planes):
        for x in range(xl):
            v = local[y, :, x * nz : (x + 1) * nz] + planes[x].astype(f32) + bias[...]
            square = v * v
            t = jnp.tanh(root * (v + 0.044715 * (square * v)))
            g = 0.5 * (1.0 + t)
            g = g + (0.5 * v) * ((1.0 - t * t) * (root * (1.0 + (3.0 * 0.044715) * square)))
            fluid = (1 - wall[x, pl.ds(y, 1), :]).astype(f32)
            wgt[y, x] = ((cot[x, y].astype(f32) * g) * fluid).astype(bf16)
        when(low_own(y), lambda: low_row(y, me - 1).start())
        when(high_own(y), lambda: high_row(y, me + 1).start())

    kacc[...] = jnp.zeros(kacc.shape, f32)

    def row_work(y):
        planes = jnp.concatenate([wgt[y, x] for x in range(xl)], axis=1)
        kacc[...] += lax.dot_general(
            cat[y, 2 * ch :, :], planes, (((1,), (1,)), ((), ())), preferred_element_type=f32
        )
        flat = jnp.concatenate([wgt[y, x] for x in range(xl)], axis=0)
        moved = jnp.dot(flat, shift[...], preferred_element_type=f32).astype(bf16)
        for x in range(xl):
            zs[RAD, x + 1, y + RAD] = wgt[y, x]
            for m, dz in enumerate(moves):
                piece = moved[x * ch : (x + 1) * ch, m * nz : (m + 1) * nz]
                zs[RAD + dz, x + 1, y + RAD] = piece

    slope(me, [stage1[me, j] for j in range(xl)])
    row_work(me)

    def turn(src):
        back1(src).wait_recv()
        slope(src, [spec1[src, j] for j in range(xl)])
        share2(src).start()
        row_work(src)

    others(0, count, by_core, turn)

    for t in range(tiles):
        kacc[t * ch : (t + 1) * ch] = jnp.transpose(kacc[t * ch : (t + 1) * ch])

    rows = kpart.shape[1]

    def strip(p):
        return kacc.at[pl.ds(p * rows, rows)]

    def near(body):
        def visit(d):
            body((inner + d) % half)

        each(1, half, visit)

    def ksend_to(p):
        return push(
            strip(p), kpart.at[inner], ksend.at[0, p], krecv.at[0, inner], side * half + p
        )

    def kland(p):
        return push(strip(p), kpart.at[p], ksend.at[0, p], krecv.at[0, p], side * half + p)

    near(lambda p: ksend_to(p).start())

    acc[...] = jnp.zeros(acc.shape, f32)
    gain([wgt[me, j] for j in range(xl)], me)

    def take2(src):
        land2(src).wait_recv()
        when((src == half) & (me < low_edge), lambda: low_relay().start())
        when((src == low_edge) & (me > half), lambda: high_relay().start())
        gain([pen2[src, j] for j in range(xl)], src)

    when(me < low_edge, lambda: low_pass().wait_send())
    when(me > half, lambda: high_pass().wait_send())
    others(0, count, from_side, take2)
    kpart[inner] = kacc[pl.ds(inner * rows, rows)]
    near(lambda p: kland(p).wait_recv())
    part_sum = kpart[0]
    for p in range(1, half):
        part_sum = part_sum + kpart[p]
    kmine[...] = part_sum
    partner = ((side + 1) % 2) * half + inner
    across = push(kmine, kother, xsend.at[0], xrecv.at[0], partner)
    across.start()

    backward_mix()

    def hand2(peer):
        expand(stage2, peer)
        give2(peer).start()

    others(0, count, by_side, hand2)
    expand(stage2, me)

    def halo_rows(y):
        when(me > 0, lambda: high_row(y, me - 1).wait_recv())
        when(me < count - 1, lambda: low_row(y, me + 1).wait_recv())

    each(0, ny, halo_rows)
    spread(lambda y: halo2[0, y], 0)
    spread(lambda y: halo2[1, y], xl + 1)
    gather_rows(-1)

    mix(wb)

    def put(y):
        return pltpu.make_async_copy(res.at[:, y], out.at[:, y], store.at[y])

    def finish(y, planes):
        for x in range(xl):
            total = local[y, :, x * nz : (x + 1) * nz] + planes[x].astype(f32)
            res[x, y] = total.astype(bf16)
        put(y).start()

    finish(me, [stage2[me, j] for j in range(xl)])

    def last(src):
        back2(src).wait_recv()
        finish(src, [spec2[src, j] for j in range(xl)])

    others(0, half, from_core, last)

    across.wait_recv()
    ksum[...] = (kmine[...] + kother[...]) * (float(count * xl * ny * nz) ** -0.5)
    keep = pltpu.make_async_copy(ksum, kout.at[inner], store.at[ny])
    keep.start()

    def kspread(p):
        return push(ksum, kout.at[inner], ksend.at[1, p], krecv.at[1, inner], side * half + p)

    def kcollect(p):
        return push(ksum, kout.at[p], ksend.at[1, p], krecv.at[1, p], side * half + p)

    near(lambda p: kspread(p).start())
    others(half, count, from_core, last)
    near(lambda p: kcollect(p).wait_recv())

    keep.wait()
    each(0, ny, lambda y: put(y).wait())
    when(me == half, lambda: low_cross().wait_send())
    when(me == low_edge, lambda: high_cross().wait_send())
    when(inside_low, lambda: low_copy(me - 1).wait_send())
    when(inside_high, lambda: high_copy(me + 1).wait_send())

    def row_sent(y):
        when(low_own(y), lambda: low_row(y, me - 1).wait_send())
        when(high_own(y), lambda: high_row(y, me + 1).wait_send())

    each(0, ny, row_sent)
    when(me < low_edge, lambda: low_relay().wait_send())
    when(me > half, lambda: high_relay().wait_send())
    across.wait_send()

    def near_sent(p):
        ksend_to(p).wait_send()
        kspread(p).wait_send()

    near(near_sent)

    def drain(peer):
        share1(peer).wait_send()
        give1(peer).wait_send()
        share2(peer).wait_send()
        give2(peer).wait_send()

    others(0, count, by_side, drain)


def fits_kernel(count, features, kernel_weight):
    xl, ny, ch, nz = features.shape
    cells = xl * ny * ch * nz
    tile_rows = kernel_weight.shape[0] * ch
    if ny != count or count % 4 or nz % 128 or ch % 16 or tile_rows % (8 * (count // 2)):
        return False
    return 80 * cells < 24 * 2**20


def fused_device(
    features,
    cotangent,
    wall_flags,
    mode_counts,
    offsets,
    point_weight,
    kernel_weight,
    lap_weight,
    spec_weight,
    bias,
):
    count = lax.axis_size("gx")
    if not fits_kernel(count, features, kernel_weight):
        return per_device(
            features,
            cotangent,
            wall_flags,
            mode_counts,
            offsets,
            point_weight,
            kernel_weight,
            lap_weight,
            spec_weight,
            bias,
        )
    xl, ny, ch, nz = features.shape
    modes, tiles = spec_weight.shape[0], kernel_weight.shape[0]
    half = count // 2
    rows = tiles * ch // half
    f32, bf16 = jnp.float32, jnp.bfloat16
    dma = pltpu.SemaphoreType.DMA
    hbm = pl.BlockSpec(memory_space=pltpu.HBM)
    field_grad, tile_grad = pl.pallas_call(
        functools.partial(fused_kernel, count),
        out_shape=(
            jax.ShapeDtypeStruct(features.shape, bf16),
            jax.ShapeDtypeStruct((half, rows, ch), f32),
        ),
        in_specs=[hbm, hbm, hbm, hbm, hbm, hbm, hbm, hbm, hbm, hbm, hbm],
        out_specs=(hbm, hbm),
        scratch_shapes=[
            pltpu.VMEM((xl, ny, ch, nz), bf16),
            pltpu.VMEM((xl, ny, ch, nz), bf16),
            pltpu.VMEM((xl, ny, ch, nz), bf16),
            pltpu.VMEM((xl, ny, nz), jnp.int32),
            pltpu.VMEM((1, ch), jnp.int32),
            pltpu.VMEM((1, ch), f32),
            pltpu.SMEM((3, tiles), jnp.int32),
            pltpu.SMEM((modes, count * xl), f32),
            pltpu.VMEM((2 + tiles, ch, ch), bf16),
            pltpu.VMEM((modes, ch, ch), bf16),
            pltpu.VMEM((modes, ch, ch), bf16),
            pltpu.VMEM((ch, (2 + tiles) * ch), bf16),
            pltpu.VMEM((ch, (2 + tiles) * ch), bf16),
            pltpu.VMEM((ch, nz), f32),
            pltpu.VMEM((ch, nz), f32),
            pltpu.VMEM((2 * RAD + 1, xl + 2, ny + 2 * RAD, ch, nz), bf16),
            pltpu.VMEM((ny, (2 + tiles) * ch, xl * nz), bf16),
            pltpu.VMEM((ny, ch, xl * nz), f32),
            pltpu.VMEM((modes, ch, nz), f32),
            pltpu.VMEM((modes, ch, nz), f32),
            pltpu.VMEM((count, xl, ch, nz), bf16),
            pltpu.VMEM((count, xl, ch, nz), bf16),
            pltpu.VMEM((count, xl, ch, nz), bf16),
            pltpu.VMEM((count, xl, ch, nz), bf16),
            pltpu.VMEM((count, xl, ch, nz), bf16),
            pltpu.VMEM((count, xl, ch, nz), bf16),
            pltpu.VMEM((ny, xl, ch, nz), bf16),
            pltpu.VMEM((2, ny, ch, nz), bf16),
            pltpu.VMEM((2, ny, ch, nz), bf16),
            pltpu.VMEM((tiles * ch, ch), f32),
            pltpu.VMEM((half, rows, ch), f32),
            pltpu.VMEM((rows, ch), f32),
            pltpu.VMEM((rows, ch), f32),
            pltpu.VMEM((rows, ch), f32),
            pltpu.VMEM((nz, 2 * RAD * nz), bf16),
            dma((4, count)),
            dma((4, count)),
            dma((2,)),
            dma((2,)),
            dma((2, ny)),
            dma((2, ny)),
            dma((2, half)),
            dma((2, half)),
            dma((1,)),
            dma((1,)),
            dma((1,)),
            dma((ny,)),
            dma((ny + 1,)),
            dma((11,)),
        ],
        compiler_params=pltpu.CompilerParams(
            collective_id=0, has_side_effects=True, vmem_limit_bytes=62 * 2**20
        ),
    )(
        features,
        cotangent,
        wall_flags,
        mode_counts.reshape(1, ch),
        offsets.T,
        basis_table(modes, count * xl).astype(f32),
        point_weight,
        kernel_weight,
        lap_weight,
        spec_weight,
        bias.reshape(1, ch),
    )
    return field_grad, tile_grad.reshape(kernel_weight.shape)


def solution(mesh):
    return jax.shard_map(
        fused_device,
        mesh=mesh,
        in_specs=(
            P(("groups", "gx"), None, None, None),
            P(("groups", "gx"), None, None, None),
            P(("groups", "gx"), None, None),
            P(),
            P(),
            P(),
            P(),
            P(),
            P(),
            P(),
        ),
        out_specs=(P(("groups", "gx"), None, None, None), P("groups", None, None)),
        check_vma=False,
    )
```

```python
import functools
from functools import partial
import math

import jax
import ml_dtypes
import numpy as np
import jax.numpy as jnp
from jax import lax
from jax.experimental import pallas as pl
from jax.experimental.pallas import tpu as pltpu
from jax.sharding import PartitionSpec as P

RAD = 2
MESH = pl.DeviceIdType.MESH


def with_halo(cells, sides, width):
    for axis, dim in sides:
        count = lax.axis_size(axis)
        ends = count - 1
        head = lax.slice_in_dim(cells, 0, width, axis=dim)
        tail = lax.slice_in_dim(cells, cells.shape[dim] - width, cells.shape[dim], axis=dim)
        cells = jnp.concatenate(
            [
                lax.ppermute(tail, axis, [(i, (i + 1) % count) for i in range(ends)]),
                cells,
                lax.ppermute(head, axis, [((i + 1) % count, i) for i in range(ends)]),
            ],
            axis=dim,
        )
    return cells


def basis_table(mode_total, length):
    mode_index = jnp.arange(mode_total, dtype=jnp.float32)[:, None]
    cell_index = jnp.arange(length, dtype=jnp.float32)[None, :]
    phase_angle = math.pi / (2.0 * length) * mode_index * (2.0 * cell_index + 1.0)
    amplitude = jnp.where(mode_index == 0.0, math.sqrt(1.0 / length), math.sqrt(2.0 / length))
    return (amplitude * jnp.cos(phase_angle)).astype(jnp.bfloat16)


def basis_constant(mode_total, length):
    mode_index = np.arange(mode_total, dtype=np.float64)[:, None]
    cell_index = np.arange(length, dtype=np.float64)[None, :]
    phase_angle = math.pi / (2.0 * length) * mode_index * (2.0 * cell_index + 1.0)
    amplitude = np.where(mode_index == 0.0, math.sqrt(1.0 / length), math.sqrt(2.0 / length))
    table = (amplitude * np.cos(phase_angle)).astype(np.float32)
    return table.astype(ml_dtypes.bfloat16).astype(np.float32)


def pencil_work(pencil, spec_weight, kept_modes, adjoint):
    basis = basis_table(spec_weight.shape[0], pencil.shape[0])
    coefficients = jnp.einsum(
        "kx,xycz->kycz", basis, pencil, preferred_element_type=jnp.float32
    ).astype(jnp.bfloat16)
    if adjoint:
        masked = coefficients * kept_modes[:, None, :, None].astype(jnp.bfloat16)
        mixed_modes = jnp.einsum(
            "koc,kyoz->kycz", spec_weight, masked, preferred_element_type=jnp.float32
        ).astype(jnp.bfloat16)
    else:
        mixed_modes = jnp.einsum(
            "koc,kycz->kyoz", spec_weight, coefficients, preferred_element_type=jnp.float32
        )
        mixed_modes = (mixed_modes * kept_modes[:, None, :, None]).astype(jnp.bfloat16)
    return jnp.einsum(
        "kx,kyoz->xyoz", basis, mixed_modes, preferred_element_type=jnp.float32
    ).astype(jnp.bfloat16)


def spectral(slab, spec_weight, kept_modes, adjoint):
    result = pencil_work(
        lax.all_to_all(slab, "gx", split_axis=1, concat_axis=0, tiled=True),
        spec_weight,
        kept_modes,
        adjoint,
    )
    return lax.all_to_all(result, "gx", split_axis=0, concat_axis=1, tiled=True)


def laplace_ext(extended):
    padded = jnp.pad(extended, ((0, 0), (1, 1), (0, 0), (1, 1))).astype(jnp.float32)
    centre_cells = padded[1:-1, 1:-1, :, 1:-1]
    neighbours = padded[2:, 1:-1, :, 1:-1] + padded[:-2, 1:-1, :, 1:-1]
    neighbours = neighbours + padded[1:-1, 2:, :, 1:-1] + padded[1:-1, :-2, :, 1:-1]
    neighbours = neighbours + padded[1:-1, 1:-1, :, 2:] + padded[1:-1, 1:-1, :, :-2]
    return (neighbours - 6.0 * centre_cells).astype(jnp.bfloat16)


def pad_sides(extended):
    return jnp.pad(extended, ((0, 0), (RAD, RAD), (0, 0), (RAD, RAD)))


def window_of(padded, offset, direction, slab_shape):
    starts = (
        1 + direction * offset[0],
        RAD + direction * offset[1],
        0,
        RAD + direction * offset[2],
    )
    return lax.dynamic_slice(padded, starts, slab_shape)


def gelu_slope(preact, upstream):
    _, pullback = jax.vjp(partial(jax.nn.gelu, approximate=True), preact)
    return pullback(upstream)[0]


def sum_over_gx(terms):
    count = lax.axis_size("gx")
    if terms.size % count:
        return lax.psum(terms, "gx")
    pieces = lax.all_to_all(terms.reshape(count, -1), "gx", split_axis=0, concat_axis=0, tiled=True)
    mine = jnp.sum(pieces, axis=0)
    copies = jnp.broadcast_to(mine[None, :], pieces.shape)
    gathered = lax.all_to_all(copies, "gx", split_axis=0, concat_axis=0, tiled=True)
    return gathered.reshape(terms.shape)


def per_device(
    features,
    cotangent,
    wall_flags,
    mode_counts,
    offsets,
    point_weight,
    kernel_weight,
    lap_weight,
    spec_weight,
    bias,
):
    mode_total = spec_weight.shape[0]
    tile_total = kernel_weight.shape[0]
    kept_modes = (jnp.arange(mode_total, dtype=jnp.int32)[:, None] < mode_counts[None, :]).astype(
        jnp.float32
    )
    fluid_mask = (1 - wall_flags).astype(jnp.float32)[:, :, None, :]
    extended = with_halo(features, (("gx", 0),), 1)
    padded_field = pad_sides(extended)
    local_part = jnp.einsum(
        "oc,xycz->xyoz", point_weight, features, preferred_element_type=jnp.float32
    )
    local_part = local_part + jnp.einsum(
        "oc,xycz->xyoz", lap_weight, laplace_ext(extended), preferred_element_type=jnp.float32
    )
    for tile in range(tile_total):
        moved = window_of(padded_field, offsets[tile], 1, features.shape)
        local_part = local_part + jnp.einsum(
            "oc,xycz->xyoz", kernel_weight[tile], moved, preferred_element_type=jnp.float32
        )
    local_part = local_part + bias[:, None]
    spectral_part = spectral(features, spec_weight, kept_modes, False)
    preact = local_part + spectral_part.astype(jnp.float32)
    weighted = (gelu_slope(preact, cotangent.astype(jnp.float32)) * fluid_mask).astype(jnp.bfloat16)
    spec_grad = spectral(weighted, spec_weight, kept_modes, True)
    ext_grad = with_halo(weighted, (("gx", 0),), 1)
    padded_grad = pad_sides(ext_grad)
    input_grad = jnp.einsum(
        "oc,xyoz->xycz", point_weight, weighted, preferred_element_type=jnp.float32
    )
    input_grad = input_grad + jnp.einsum(
        "oc,xyoz->xycz", lap_weight, laplace_ext(ext_grad), preferred_element_type=jnp.float32
    )
    input_grad = input_grad + spec_grad.astype(jnp.float32)
    tile_grads = []
    for tile in range(tile_total):
        back_moved = window_of(padded_grad, offsets[tile], -1, weighted.shape)
        input_grad = input_grad + jnp.einsum(
            "oc,xyoz->xycz", kernel_weight[tile], back_moved, preferred_element_type=jnp.float32
        )
        tile_grads.append(
            jnp.einsum("xyoz,xycz->oc", back_moved, features, preferred_element_type=jnp.float32)
        )
    local_grad = jnp.stack(tile_grads, axis=0)
    scaling = float(
        lax.axis_size("gx") * features.shape[0] * features.shape[1] * features.shape[3]
    ) ** (-0.5)
    summed = sum_over_gx(local_grad)
    return (input_grad.astype(jnp.bfloat16), summed * scaling)


def fused_kernel(
    count,
    feat_in,
    cot_in,
    wall_in,
    mode_in,
    offs_in,
    basis_in,
    point_in,
    tile_in,
    lap_in,
    spec_in,
    bias_in,
    out,
    kout,
    feat,
    cot,
    wall,
    mode_row,
    bias_row,
    offs,
    basis,
    wst,
    wm,
    wmt,
    wf,
    wb,
    mode,
    bias,
    zs,
    cat,
    local,
    acc,
    vh,
    pen1,
    pen2,
    stage1,
    stage2,
    spec1,
    spec2,
    wgt,
    halo1,
    halo2,
    kacc,
    kpart,
    kmine,
    kother,
    ksum,
    shift,
    send,
    recv,
    hsend,
    hrecv,
    rsend,
    rrecv,
    ksend,
    krecv,
    xsend,
    xrecv,
    fsend,
    frecv,
    load,
):
    me = lax.axis_index("gx")
    grp = lax.axis_index("groups")
    xl, ny, ch, nz = feat.shape
    modes = wm.shape[0]
    tiles = offs.shape[1]
    half = count // 2
    quads = half // 2
    f32, bf16 = jnp.float32, jnp.bfloat16
    side = me // half
    inner = me % half
    chip = inner // 2

    def push(src, dst, ssem, rsem, peer):
        return pltpu.make_async_remote_copy(
            src_ref=src,
            dst_ref=dst,
            send_sem=ssem,
            recv_sem=rsem,
            device_id=(grp, peer),
            device_id_type=MESH,
        )

    def each(low, high, body):
        def step(i, carry):
            body(i)
            return carry

        lax.fori_loop(low, high, step, 0)

    def place(cross, turn, core):
        return ((side + cross) % 2) * half + ((chip + turn) % quads) * 2 + core

    def by_core(j):
        core = j // half
        rest = j % half
        return place(1 - rest // quads, rest % quads, core)

    def by_side(j):
        rest = j % half
        return place(1 - j // half, rest // 2, rest % 2)

    def from_side(j):
        rest = j % half
        return place(1 - j // half, quads - rest // 2, rest % 2)

    def from_core(j):
        core = j // half
        rest = j % half
        return place(1 - rest // quads, quads - rest % quads, core)

    def others(low, high, order, body):
        def visit(j):
            peer = order(j)

            @pl.when(peer != me)
            def _():
                body(peer)

        each(low, high, visit)

    def share1(peer):
        return push(
            feat_in.at[:, peer], pen1.at[me], send.at[0, peer], recv.at[0, me], peer
        )

    def land1(src):
        return push(feat_in.at[:, src], pen1.at[src], send.at[0, src], recv.at[0, src], src)

    def give1(peer):
        return push(stage1.at[peer], spec1.at[me], send.at[1, peer], recv.at[1, me], peer)

    def back1(src):
        return push(stage1.at[src], spec1.at[src], send.at[1, src], recv.at[1, src], src)

    def share2(peer):
        return push(wgt.at[peer], pen2.at[me], send.at[2, peer], recv.at[2, me], peer)

    def land2(src):
        return push(wgt.at[src], pen2.at[src], send.at[2, src], recv.at[2, src], src)

    def give2(peer):
        return push(stage2.at[peer], spec2.at[me], send.at[3, peer], recv.at[3, me], peer)

    def back2(src):
        return push(stage2.at[src], spec2.at[src], send.at[3, src], recv.at[3, src], src)

    loads = [
        pltpu.make_async_copy(feat_in, feat, load.at[0]),
        pltpu.make_async_copy(point_in, wst.at[0], load.at[1]),
        pltpu.make_async_copy(lap_in, wst.at[1], load.at[2]),
        pltpu.make_async_copy(tile_in, wst.at[pl.ds(2, tiles)], load.at[3]),
        pltpu.make_async_copy(spec_in, wm, load.at[4]),
        pltpu.make_async_copy(mode_in, mode_row, load.at[5]),
        pltpu.make_async_copy(bias_in, bias_row, load.at[6]),
        pltpu.make_async_copy(wall_in, wall, load.at[7]),
        pltpu.make_async_copy(cot_in, cot, load.at[8]),
        pltpu.make_async_copy(offs_in, offs, load.at[9]),
        pltpu.make_async_copy(basis_in, basis, load.at[10]),
    ]
    barrier = pltpu.get_barrier_semaphore()
    each(
        1,
        count,
        lambda d: pl.semaphore_signal(
            barrier, inc=1, device_id=(grp, lax.rem(me + d, count)), device_id_type=MESH
        ),
    )
    for piece in loads:
        piece.start()

    pl.semaphore_wait(barrier, count - 1)

    low_edge = half - 1

    def low_copy(peer):
        return push(feat_in.at[0], halo1.at[1], hsend.at[0], hrecv.at[0], peer)

    def high_copy(peer):
        return push(feat_in.at[xl - 1], halo1.at[0], hsend.at[1], hrecv.at[1], peer)

    def low_cross():
        part = pl.ds(half - 1, half + 1)
        return push(feat_in.at[0, part], halo1.at[1, part], hsend.at[0], hrecv.at[0], low_edge)

    def high_cross():
        part = pl.ds(0, half + 1)
        return push(feat_in.at[xl - 1, part], halo1.at[0, part], hsend.at[1], hrecv.at[1], half)

    def low_pass():
        return push(pen1.at[half, 0], halo1.at[1, me], fsend.at[0], frecv.at[me], low_edge)

    def high_pass():
        return push(
            pen1.at[low_edge, xl - 1], halo1.at[0, me], fsend.at[0], frecv.at[me], half
        )

    def low_row(y, peer):
        return push(wgt.at[y, 0], halo2.at[1, y], rsend.at[0, y], rrecv.at[0, y], peer)

    def high_row(y, peer):
        return push(wgt.at[y, xl - 1], halo2.at[0, y], rsend.at[1, y], rrecv.at[1, y], peer)

    def low_relay():
        return push(
            pen2.at[half, 0], halo2.at[1, me], fsend.at[0], rrecv.at[0, me], low_edge
        )

    def high_relay():
        return push(
            pen2.at[low_edge, xl - 1], halo2.at[0, me], fsend.at[0], rrecv.at[1, me], half
        )

    def low_own(y):
        return (me > 0) & ((me != half) | (y >= low_edge))

    def high_own(y):
        return (me < count - 1) & ((me != low_edge) | (y <= half))

    def when(cond, body):
        @pl.when(cond)
        def _():
            body()

    inside_low = (me > 0) & (me != half)
    inside_high = (me < count - 1) & (me != low_edge)
    when(me == half, lambda: low_cross().start())
    when(me == low_edge, lambda: high_cross().start())
    when(inside_low, lambda: low_copy(me - 1).start())
    when(inside_high, lambda: high_copy(me + 1).start())
    others(0, count, by_core, lambda peer: share1(peer).start())

    from_z = lax.broadcasted_iota(jnp.int32, (nz, nz), 0)
    to_z = lax.broadcasted_iota(jnp.int32, (nz, nz), 1)
    for m, dz in enumerate([dz for dz in range(-RAD, RAD + 1) if dz]):
        shift[:, m * nz : (m + 1) * nz] = jnp.where(from_z == to_z + dz, 1.0, 0.0).astype(bf16)

    @pl.when(me == 0)
    def _():
        halo1[0] = jnp.zeros(halo1.shape[1:], bf16)
        halo2[0] = jnp.zeros(halo2.shape[1:], bf16)

    @pl.when(me == count - 1)
    def _():
        halo1[1] = jnp.zeros(halo1.shape[1:], bf16)
        halo2[1] = jnp.zeros(halo2.shape[1:], bf16)

    for edge in (0, RAD + ny):
        for dz in range(2 * RAD + 1):
            for x in range(xl + 2):
                zs[dz, x, edge : edge + RAD] = jnp.zeros((RAD, ch, nz), bf16)

    moves = [dz for dz in range(-RAD, RAD + 1) if dz]
    group = math.gcd(ny, 8)

    def spread(take, place_x):
        def body(i):
            y = i * group
            v = take(pl.ds(y, group))
            zs[RAD, place_x, pl.ds(y + RAD, group)] = v
            flat = v.reshape(group * ch, nz)
            moved = jnp.dot(flat, shift[...], preferred_element_type=f32).astype(bf16)
            for m, dz in enumerate(moves):
                piece = moved[:, m * nz : (m + 1) * nz].reshape(group, ch, nz)
                zs[RAD + dz, place_x, pl.ds(y + RAD, group)] = piece

        each(0, ny // group, body)

    def gather_rows(direction):
        def body(y):
            for x in range(xl):
                lanes = slice(x * nz, (x + 1) * nz)
                centre = zs[RAD, x + 1, y + RAD]
                cat[y, 0:ch, lanes] = centre
                total = zs[RAD, x + 2, y + RAD].astype(f32) + zs[RAD, x, y + RAD].astype(f32)
                total = total + zs[RAD, x + 1, y + RAD + 1].astype(f32)
                total = total + zs[RAD, x + 1, y + RAD - 1].astype(f32)
                total = total + zs[RAD + 1, x + 1, y + RAD].astype(f32)
                total = total + zs[RAD - 1, x + 1, y + RAD].astype(f32)
                cat[y, ch : 2 * ch, lanes] = (total - 6.0 * centre.astype(f32)).astype(bf16)
                for t in range(tiles):
                    moved = zs[
                        RAD + direction * offs[2, t],
                        x + 1 + direction * offs[0, t],
                        y + RAD + direction * offs[1, t],
                    ]
                    cat[y, (2 + t) * ch : (3 + t) * ch, lanes] = moved

        each(0, ny, body)

    unroll = math.gcd(ny, 4)

    def each_row(body):
        def rows_at(i):
            for r in range(unroll):
                body(i * unroll + r)

        each(0, ny // unroll, rows_at)

    def mix(weights):
        def body(y):
            local[y] = jnp.dot(weights[...], cat[y], preferred_element_type=f32)

        each_row(body)

    def gain(planes, src):
        wide = [p.astype(f32) for p in planes]
        for k in range(modes):
            total = acc[k]
            for j in range(xl):
                total = total + basis[k, src * xl + j] * wide[j]
            acc[k] = total

    def forward_mix():
        for k in range(modes):
            v = jnp.dot(wm[k], acc[k].astype(bf16), preferred_element_type=f32)
            v = jnp.where(mode[...] > float(k), v, 0.0)
            vh[k] = v.astype(bf16).astype(f32)

    def backward_mix():
        for k in range(modes):
            u = jnp.where(mode[...] > float(k), acc[k], 0.0).astype(bf16)
            v = jnp.dot(wmt[k], u, preferred_element_type=f32)
            vh[k] = v.astype(bf16).astype(f32)

    def expand(stage, peer):
        for j in range(xl):
            total = basis[0, peer * xl + j] * vh[0]
            for k in range(1, modes):
                total = total + basis[k, peer * xl + j] * vh[k]
            stage[peer, j] = total.astype(bf16)

    loads[0].wait()
    for x in range(xl):
        spread(lambda y: feat[x, y], x + 1)
    for piece in loads[1:]:
        piece.wait()

    row_at = lax.broadcasted_iota(jnp.int32, (ch, ch), 0)
    col_at = lax.broadcasted_iota(jnp.int32, (ch, ch), 1)
    diagonal = row_at == col_at
    unit = jnp.where(diagonal, 1.0, 0.0).astype(bf16)

    def upright(row):
        spread_out = jnp.where(diagonal, jnp.broadcast_to(row, (ch, ch)), 0.0)
        column = jnp.sum(spread_out, axis=1, keepdims=True)
        return jnp.broadcast_to(column, (ch, nz))

    mode[...] = upright(mode_row[...].astype(f32))
    bias[...] = upright(bias_row[...])

    def flipped(block):
        return lax.dot_general(
            block, unit, (((0,), (0,)), ((), ())), preferred_element_type=f32
        ).astype(bf16)

    for t in range(2 + tiles):
        wf[:, t * ch : (t + 1) * ch] = wst[t]
        wb[:, t * ch : (t + 1) * ch] = flipped(wst[t])

    def flip_mode(k):
        wmt[k] = flipped(wm[k])

    each(0, modes, flip_mode)

    def passed_low(i):
        push(
            pen1.at[low_edge, xl - 1], halo1.at[0, i], fsend.at[0], frecv.at[i], low_edge
        ).wait_recv()

    def passed_high(i):
        push(pen1.at[half, 0], halo1.at[1, i], fsend.at[0], frecv.at[i], half).wait_recv()

    def forward_stencil():
        when(inside_low, lambda: high_copy(me - 1).wait_recv())
        when(inside_high, lambda: low_copy(me + 1).wait_recv())

        @pl.when(me == half)
        def _():
            high_cross_here = push(
                feat_in.at[xl - 1, pl.ds(0, half + 1)],
                halo1.at[0, pl.ds(0, half + 1)],
                hsend.at[1],
                hrecv.at[1],
                low_edge,
            )
            high_cross_here.wait_recv()
            each(half + 1, count, passed_low)

        @pl.when(me == low_edge)
        def _():
            low_cross_here = push(
                feat_in.at[0, pl.ds(half - 1, half + 1)],
                halo1.at[1, pl.ds(half - 1, half + 1)],
                hsend.at[0],
                hrecv.at[0],
                half,
            )
            low_cross_here.wait_recv()
            each(0, half - 1, passed_high)

        spread(lambda y: halo1[0, y], 0)
        spread(lambda y: halo1[1, y], xl + 1)
        gather_rows(1)
        mix(wf)

    core = me % 2
    when(core == 1, forward_stencil)

    acc[...] = jnp.zeros(acc.shape, f32)
    gain([feat[j, me] for j in range(xl)], me)

    def take1(src):
        land1(src).wait_recv()
        when((src == half) & (me < low_edge), lambda: low_pass().start())
        when((src == low_edge) & (me > half), lambda: high_pass().start())
        gain([pen1[src, j] for j in range(xl)], src)

    others(0, count, from_side, take1)
    forward_mix()

    def hand1(peer):
        expand(stage1, peer)
        give1(peer).start()

    others(0, count, by_side, hand1)
    expand(stage1, me)
    when(core == 0, forward_stencil)
    root = math.sqrt(2.0 / math.pi)

    def slope(y, planes):
        for x in range(xl):
            v = local[y, :, x * nz : (x + 1) * nz] + planes[x].astype(f32) + bias[...]
            square = v * v
            t = jnp.tanh(root * (v + 0.044715 * (square * v)))
            g = 0.5 * (1.0 + t)
            g = g + (0.5 * v) * ((1.0 - t * t) * (root * (1.0 + (3.0 * 0.044715) * square)))
            fluid = (1 - wall[x, pl.ds(y, 1), :]).astype(f32)
            wgt[y, x] = ((cot[x, y].astype(f32) * g) * fluid).astype(bf16)
        when(low_own(y), lambda: low_row(y, me - 1).start())
        when(high_own(y), lambda: high_row(y, me + 1).start())

    kacc[...] = jnp.zeros(kacc.shape, f32)

    def row_work(y):
        planes = jnp.concatenate([wgt[y, x] for x in range(xl)], axis=1)
        kacc[...] += lax.dot_general(
            cat[y, 2 * ch :, :], planes, (((1,), (1,)), ((), ())), preferred_element_type=f32
        )
        flat = jnp.concatenate([wgt[y, x] for x in range(xl)], axis=0)
        moved = jnp.dot(flat, shift[...], preferred_element_type=f32).astype(bf16)
        for x in range(xl):
            zs[RAD, x + 1, y + RAD] = wgt[y, x]
            for m, dz in enumerate(moves):
                piece = moved[x * ch : (x + 1) * ch, m * nz : (m + 1) * nz]
                zs[RAD + dz, x + 1, y + RAD] = piece

    slope(me, [stage1[me, j] for j in range(xl)])
    row_work(me)

    def turn(src):
        back1(src).wait_recv()
        slope(src, [spec1[src, j] for j in range(xl)])
        share2(src).start()
        row_work(src)

    others(0, count, by_core, turn)

    for t in range(tiles):
        kacc[t * ch : (t + 1) * ch] = jnp.transpose(kacc[t * ch : (t + 1) * ch])

    rows = kpart.shape[1]

    def strip(p):
        return kacc.at[pl.ds(p * rows, rows)]

    def near(body):
        def visit(d):
            body((inner + d) % half)

        each(1, half, visit)

    def ksend_to(p):
        return push(
            strip(p), kpart.at[inner], ksend.at[0, p], krecv.at[0, inner], side * half + p
        )

    def kland(p):
        return push(strip(p), kpart.at[p], ksend.at[0, p], krecv.at[0, p], side * half + p)

    near(lambda p: ksend_to(p).start())

    acc[...] = jnp.zeros(acc.shape, f32)
    gain([wgt[me, j] for j in range(xl)], me)

    def take2(src):
        land2(src).wait_recv()
        when((src == half) & (me < low_edge), lambda: low_relay().start())
        when((src == low_edge) & (me > half), lambda: high_relay().start())
        gain([pen2[src, j] for j in range(xl)], src)

    when(me < low_edge, lambda: low_pass().wait_send())
    when(me > half, lambda: high_pass().wait_send())
    others(0, count, from_side, take2)
    backward_mix()

    def hand2(peer):
        expand(stage2, peer)
        give2(peer).start()

    others(0, quads, by_side, hand2)
    kpart[inner] = kacc[pl.ds(inner * rows, rows)]
    near(lambda p: kland(p).wait_recv())
    part_sum = kpart[0]
    for p in range(1, half):
        part_sum = part_sum + kpart[p]
    kmine[...] = part_sum
    partner = ((side + 1) % 2) * half + inner
    across = push(kmine, kother, xsend.at[0], xrecv.at[0], partner)
    across.start()
    others(quads, count, by_side, hand2)
    expand(stage2, me)

    def halo_rows(y):
        when(me > 0, lambda: high_row(y, me - 1).wait_recv())
        when(me < count - 1, lambda: low_row(y, me + 1).wait_recv())

    each(0, ny, halo_rows)
    spread(lambda y: halo2[0, y], 0)
    spread(lambda y: halo2[1, y], xl + 1)
    gather_rows(-1)

    mix(wb)

    across.wait_recv()
    ksum[...] = (kmine[...] + kother[...]) * (float(count * xl * ny * nz) ** -0.5)
    kout[inner] = ksum[...]

    def kspread(p):
        return push(ksum, kout.at[inner], ksend.at[1, p], krecv.at[1, inner], side * half + p)

    def kcollect(p):
        return push(ksum, kout.at[p], ksend.at[1, p], krecv.at[1, p], side * half + p)

    near(lambda p: kspread(p).start())

    def finish(y, planes):
        for x in range(xl):
            total = local[y, :, x * nz : (x + 1) * nz] + planes[x].astype(f32)
            out[x, y] = total.astype(bf16)

    finish(me, [stage2[me, j] for j in range(xl)])

    def last(src):
        back2(src).wait_recv()
        finish(src, [spec2[src, j] for j in range(xl)])

    others(half, count, from_side, last)
    others(0, half, from_side, last)
    near(lambda p: kcollect(p).wait_recv())

    when(me == half, lambda: low_cross().wait_send())
    when(me == low_edge, lambda: high_cross().wait_send())
    when(inside_low, lambda: low_copy(me - 1).wait_send())
    when(inside_high, lambda: high_copy(me + 1).wait_send())

    def row_sent(y):
        when(low_own(y), lambda: low_row(y, me - 1).wait_send())
        when(high_own(y), lambda: high_row(y, me + 1).wait_send())

    each(0, ny, row_sent)
    when(me < low_edge, lambda: low_relay().wait_send())
    when(me > half, lambda: high_relay().wait_send())
    across.wait_send()

    def near_sent(p):
        ksend_to(p).wait_send()
        kspread(p).wait_send()

    near(near_sent)

    def drain(peer):
        share1(peer).wait_send()
        give1(peer).wait_send()
        share2(peer).wait_send()
        give2(peer).wait_send()

    others(0, count, by_side, drain)


def fits_kernel(count, features, kernel_weight):
    xl, ny, ch, nz = features.shape
    cells = xl * ny * ch * nz
    tile_rows = kernel_weight.shape[0] * ch
    if ny != count or count % 4 or nz % 128 or ch % 16 or tile_rows % (8 * (count // 2)):
        return False
    return 80 * cells < 24 * 2**20


def fused_device(
    features,
    cotangent,
    wall_flags,
    mode_counts,
    offsets,
    point_weight,
    kernel_weight,
    lap_weight,
    spec_weight,
    bias,
):
    count = lax.axis_size("gx")
    if not fits_kernel(count, features, kernel_weight):
        return per_device(
            features,
            cotangent,
            wall_flags,
            mode_counts,
            offsets,
            point_weight,
            kernel_weight,
            lap_weight,
            spec_weight,
            bias,
        )
    xl, ny, ch, nz = features.shape
    modes, tiles = spec_weight.shape[0], kernel_weight.shape[0]
    half = count // 2
    rows = tiles * ch // half
    f32, bf16 = jnp.float32, jnp.bfloat16
    dma = pltpu.SemaphoreType.DMA
    vmem = pl.BlockSpec(memory_space=pltpu.VMEM)
    hbm = pl.BlockSpec(memory_space=pltpu.HBM)
    field_grad, tile_grad = pl.pallas_call(
        functools.partial(fused_kernel, count),
        out_shape=(
            pltpu.VMEM(features.shape, bf16),
            pltpu.VMEM((half, rows, ch), f32),
        ),
        in_specs=[hbm, hbm, hbm, hbm, hbm, hbm, hbm, hbm, hbm, hbm, hbm],
        out_specs=(vmem, vmem),
        scratch_shapes=[
            pltpu.VMEM((xl, ny, ch, nz), bf16),
            pltpu.VMEM((xl, ny, ch, nz), bf16),
            pltpu.VMEM((xl, ny, nz), jnp.int32),
            pltpu.VMEM((1, ch), jnp.int32),
            pltpu.VMEM((1, ch), f32),
            pltpu.SMEM((3, tiles), jnp.int32),
            pltpu.SMEM((modes, count * xl), f32),
            pltpu.VMEM((2 + tiles, ch, ch), bf16),
            pltpu.VMEM((modes, ch, ch), bf16),
            pltpu.VMEM((modes, ch, ch), bf16),
            pltpu.VMEM((ch, (2 + tiles) * ch), bf16),
            pltpu.VMEM((ch, (2 + tiles) * ch), bf16),
            pltpu.VMEM((ch, nz), f32),
            pltpu.VMEM((ch, nz), f32),
            pltpu.VMEM((2 * RAD + 1, xl + 2, ny + 2 * RAD, ch, nz), bf16),
            pltpu.VMEM((ny, (2 + tiles) * ch, xl * nz), bf16),
            pltpu.VMEM((ny, ch, xl * nz), f32),
            pltpu.VMEM((modes, ch, nz), f32),
            pltpu.VMEM((modes, ch, nz), f32),
            pltpu.VMEM((count, xl, ch, nz), bf16),
            pltpu.VMEM((count, xl, ch, nz), bf16),
            pltpu.VMEM((count, xl, ch, nz), bf16),
            pltpu.VMEM((count, xl, ch, nz), bf16),
            pltpu.VMEM((count, xl, ch, nz), bf16),
            pltpu.VMEM((count, xl, ch, nz), bf16),
            pltpu.VMEM((ny, xl, ch, nz), bf16),
            pltpu.VMEM((2, ny, ch, nz), bf16),
            pltpu.VMEM((2, ny, ch, nz), bf16),
            pltpu.VMEM((tiles * ch, ch), f32),
            pltpu.VMEM((half, rows, ch), f32),
            pltpu.VMEM((rows, ch), f32),
            pltpu.VMEM((rows, ch), f32),
            pltpu.VMEM((rows, ch), f32),
            pltpu.VMEM((nz, 2 * RAD * nz), bf16),
            dma((4, count)),
            dma((4, count)),
            dma((2,)),
            dma((2,)),
            dma((2, ny)),
            dma((2, ny)),
            dma((2, half)),
            dma((2, half)),
            dma((1,)),
            dma((1,)),
            dma((1,)),
            dma((ny,)),
            dma((11,)),
        ],
        compiler_params=pltpu.CompilerParams(
            collective_id=0, has_side_effects=True, vmem_limit_bytes=56 * 2**20
        ),
    )(
        features,
        cotangent,
        wall_flags,
        mode_counts.reshape(1, ch),
        offsets.T,
        basis_constant(modes, count * xl),
        point_weight,
        kernel_weight,
        lap_weight,
        spec_weight,
        bias.reshape(1, ch),
    )
    return field_grad, tile_grad.reshape(kernel_weight.shape)


def solution(mesh):
    return jax.shard_map(
        fused_device,
        mesh=mesh,
        in_specs=(
            P(("groups", "gx"), None, None, None),
            P(("groups", "gx"), None, None, None),
            P(("groups", "gx"), None, None),
            P(),
            P(),
            P(),
            P(),
            P(),
            P(),
            P(),
        ),
        out_specs=(P(("groups", "gx"), None, None, None), P("groups", None, None)),
        check_vma=False,
    )
```

```python
import functools
from functools import partial
import math

import jax
import ml_dtypes
import numpy as np
import jax.numpy as jnp
from jax import lax
from jax.experimental import pallas as pl
from jax.experimental.pallas import tpu as pltpu
from jax.sharding import PartitionSpec as P

RAD = 2
MESH = pl.DeviceIdType.MESH


def with_halo(cells, sides, width):
    for axis, dim in sides:
        count = lax.axis_size(axis)
        ends = count - 1
        head = lax.slice_in_dim(cells, 0, width, axis=dim)
        tail = lax.slice_in_dim(cells, cells.shape[dim] - width, cells.shape[dim], axis=dim)
        cells = jnp.concatenate(
            [
                lax.ppermute(tail, axis, [(i, (i + 1) % count) for i in range(ends)]),
                cells,
                lax.ppermute(head, axis, [((i + 1) % count, i) for i in range(ends)]),
            ],
            axis=dim,
        )
    return cells


def basis_table(mode_total, length):
    mode_index = jnp.arange(mode_total, dtype=jnp.float32)[:, None]
    cell_index = jnp.arange(length, dtype=jnp.float32)[None, :]
    phase_angle = math.pi / (2.0 * length) * mode_index * (2.0 * cell_index + 1.0)
    amplitude = jnp.where(mode_index == 0.0, math.sqrt(1.0 / length), math.sqrt(2.0 / length))
    return (amplitude * jnp.cos(phase_angle)).astype(jnp.bfloat16)


def basis_constant(mode_total, length):
    mode_index = np.arange(mode_total, dtype=np.float64)[:, None]
    cell_index = np.arange(length, dtype=np.float64)[None, :]
    phase_angle = math.pi / (2.0 * length) * mode_index * (2.0 * cell_index + 1.0)
    amplitude = np.where(mode_index == 0.0, math.sqrt(1.0 / length), math.sqrt(2.0 / length))
    table = (amplitude * np.cos(phase_angle)).astype(np.float32)
    return table.astype(ml_dtypes.bfloat16).astype(np.float32)


def pencil_work(pencil, spec_weight, kept_modes, adjoint):
    basis = basis_table(spec_weight.shape[0], pencil.shape[0])
    coefficients = jnp.einsum(
        "kx,xycz->kycz", basis, pencil, preferred_element_type=jnp.float32
    ).astype(jnp.bfloat16)
    if adjoint:
        masked = coefficients * kept_modes[:, None, :, None].astype(jnp.bfloat16)
        mixed_modes = jnp.einsum(
            "koc,kyoz->kycz", spec_weight, masked, preferred_element_type=jnp.float32
        ).astype(jnp.bfloat16)
    else:
        mixed_modes = jnp.einsum(
            "koc,kycz->kyoz", spec_weight, coefficients, preferred_element_type=jnp.float32
        )
        mixed_modes = (mixed_modes * kept_modes[:, None, :, None]).astype(jnp.bfloat16)
    return jnp.einsum(
        "kx,kyoz->xyoz", basis, mixed_modes, preferred_element_type=jnp.float32
    ).astype(jnp.bfloat16)


def spectral(slab, spec_weight, kept_modes, adjoint):
    result = pencil_work(
        lax.all_to_all(slab, "gx", split_axis=1, concat_axis=0, tiled=True),
        spec_weight,
        kept_modes,
        adjoint,
    )
    return lax.all_to_all(result, "gx", split_axis=0, concat_axis=1, tiled=True)


def laplace_ext(extended):
    padded = jnp.pad(extended, ((0, 0), (1, 1), (0, 0), (1, 1))).astype(jnp.float32)
    centre_cells = padded[1:-1, 1:-1, :, 1:-1]
    neighbours = padded[2:, 1:-1, :, 1:-1] + padded[:-2, 1:-1, :, 1:-1]
    neighbours = neighbours + padded[1:-1, 2:, :, 1:-1] + padded[1:-1, :-2, :, 1:-1]
    neighbours = neighbours + padded[1:-1, 1:-1, :, 2:] + padded[1:-1, 1:-1, :, :-2]
    return (neighbours - 6.0 * centre_cells).astype(jnp.bfloat16)


def pad_sides(extended):
    return jnp.pad(extended, ((0, 0), (RAD, RAD), (0, 0), (RAD, RAD)))


def window_of(padded, offset, direction, slab_shape):
    starts = (
        1 + direction * offset[0],
        RAD + direction * offset[1],
        0,
        RAD + direction * offset[2],
    )
    return lax.dynamic_slice(padded, starts, slab_shape)


def gelu_slope(preact, upstream):
    _, pullback = jax.vjp(partial(jax.nn.gelu, approximate=True), preact)
    return pullback(upstream)[0]


def sum_over_gx(terms):
    count = lax.axis_size("gx")
    if terms.size % count:
        return lax.psum(terms, "gx")
    pieces = lax.all_to_all(terms.reshape(count, -1), "gx", split_axis=0, concat_axis=0, tiled=True)
    mine = jnp.sum(pieces, axis=0)
    copies = jnp.broadcast_to(mine[None, :], pieces.shape)
    gathered = lax.all_to_all(copies, "gx", split_axis=0, concat_axis=0, tiled=True)
    return gathered.reshape(terms.shape)


def per_device(
    features,
    cotangent,
    wall_flags,
    mode_counts,
    offsets,
    point_weight,
    kernel_weight,
    lap_weight,
    spec_weight,
    bias,
):
    mode_total = spec_weight.shape[0]
    tile_total = kernel_weight.shape[0]
    kept_modes = (jnp.arange(mode_total, dtype=jnp.int32)[:, None] < mode_counts[None, :]).astype(
        jnp.float32
    )
    fluid_mask = (1 - wall_flags).astype(jnp.float32)[:, :, None, :]
    extended = with_halo(features, (("gx", 0),), 1)
    padded_field = pad_sides(extended)
    local_part = jnp.einsum(
        "oc,xycz->xyoz", point_weight, features, preferred_element_type=jnp.float32
    )
    local_part = local_part + jnp.einsum(
        "oc,xycz->xyoz", lap_weight, laplace_ext(extended), preferred_element_type=jnp.float32
    )
    for tile in range(tile_total):
        moved = window_of(padded_field, offsets[tile], 1, features.shape)
        local_part = local_part + jnp.einsum(
            "oc,xycz->xyoz", kernel_weight[tile], moved, preferred_element_type=jnp.float32
        )
    local_part = local_part + bias[:, None]
    spectral_part = spectral(features, spec_weight, kept_modes, False)
    preact = local_part + spectral_part.astype(jnp.float32)
    weighted = (gelu_slope(preact, cotangent.astype(jnp.float32)) * fluid_mask).astype(jnp.bfloat16)
    spec_grad = spectral(weighted, spec_weight, kept_modes, True)
    ext_grad = with_halo(weighted, (("gx", 0),), 1)
    padded_grad = pad_sides(ext_grad)
    input_grad = jnp.einsum(
        "oc,xyoz->xycz", point_weight, weighted, preferred_element_type=jnp.float32
    )
    input_grad = input_grad + jnp.einsum(
        "oc,xyoz->xycz", lap_weight, laplace_ext(ext_grad), preferred_element_type=jnp.float32
    )
    input_grad = input_grad + spec_grad.astype(jnp.float32)
    tile_grads = []
    for tile in range(tile_total):
        back_moved = window_of(padded_grad, offsets[tile], -1, weighted.shape)
        input_grad = input_grad + jnp.einsum(
            "oc,xyoz->xycz", kernel_weight[tile], back_moved, preferred_element_type=jnp.float32
        )
        tile_grads.append(
            jnp.einsum("xyoz,xycz->oc", back_moved, features, preferred_element_type=jnp.float32)
        )
    local_grad = jnp.stack(tile_grads, axis=0)
    scaling = float(
        lax.axis_size("gx") * features.shape[0] * features.shape[1] * features.shape[3]
    ) ** (-0.5)
    summed = sum_over_gx(local_grad)
    return (input_grad.astype(jnp.bfloat16), summed * scaling)


def fused_kernel(
    count,
    feat_in,
    cot_in,
    wall_in,
    mode_in,
    offs_in,
    basis_in,
    point_in,
    tile_in,
    lap_in,
    spec_in,
    bias_in,
    out,
    kout,
    feat,
    cot,
    wall,
    mode_row,
    bias_row,
    offs,
    basis,
    wst,
    wm,
    wmt,
    wf,
    wb,
    mode,
    bias,
    zs,
    cat,
    local,
    acc,
    vh,
    pen1,
    pen2,
    stage1,
    stage2,
    spec1,
    spec2,
    wgt,
    halo1,
    halo2,
    kacc,
    kdense,
    kpart,
    kmine,
    kother,
    ksum,
    kall,
    shift,
    send,
    recv,
    hsend,
    hrecv,
    rsend,
    rrecv,
    ksend,
    krecv,
    xsend,
    xrecv,
    fsend,
    frecv,
    load,
):
    me = lax.axis_index("gx")
    grp = lax.axis_index("groups")
    xl, ny, ch, nz = feat.shape
    modes = wm.shape[0]
    tiles = offs.shape[1]
    half = count // 2
    quads = half // 2
    f32, bf16 = jnp.float32, jnp.bfloat16
    side = me // half
    inner = me % half
    chip = inner // 2

    def push(src, dst, ssem, rsem, peer):
        return pltpu.make_async_remote_copy(
            src_ref=src,
            dst_ref=dst,
            send_sem=ssem,
            recv_sem=rsem,
            device_id=(grp, peer),
            device_id_type=MESH,
        )

    def each(low, high, body):
        def step(i, carry):
            body(i)
            return carry

        lax.fori_loop(low, high, step, 0)

    def place(cross, turn, core):
        return ((side + cross) % 2) * half + ((chip + turn) % quads) * 2 + core

    def by_core(j):
        core = j // half
        rest = j % half
        return place(1 - rest // quads, rest % quads, core)

    def by_side(j):
        rest = j % half
        return place(1 - j // half, rest // 2, rest % 2)

    def from_side(j):
        rest = j % half
        return place(1 - j // half, quads - rest // 2, rest % 2)

    def from_core(j):
        core = j // half
        rest = j % half
        return place(1 - rest // quads, quads - rest % quads, core)

    def others(low, high, order, body):
        def visit(j):
            peer = order(j)

            @pl.when(peer != me)
            def _():
                body(peer)

        each(low, high, visit)

    def share1(peer):
        return push(
            feat.at[:, peer], pen1.at[me], send.at[0, peer], recv.at[0, me], peer
        )

    def land1(src):
        return push(feat.at[:, src], pen1.at[src], send.at[0, src], recv.at[0, src], src)

    def give1(peer):
        return push(stage1.at[peer], spec1.at[me], send.at[1, peer], recv.at[1, me], peer)

    def back1(src):
        return push(stage1.at[src], spec1.at[src], send.at[1, src], recv.at[1, src], src)

    def share2(peer):
        return push(wgt.at[peer], pen2.at[me], send.at[2, peer], recv.at[2, me], peer)

    def land2(src):
        return push(wgt.at[src], pen2.at[src], send.at[2, src], recv.at[2, src], src)

    def give2(peer):
        return push(stage2.at[peer], spec2.at[me], send.at[3, peer], recv.at[3, me], peer)

    def back2(src):
        return push(stage2.at[src], spec2.at[src], send.at[3, src], recv.at[3, src], src)

    loads = [
        pltpu.make_async_copy(feat_in, feat, load.at[0]),
        pltpu.make_async_copy(point_in, wst.at[0], load.at[1]),
        pltpu.make_async_copy(lap_in, wst.at[1], load.at[2]),
        pltpu.make_async_copy(tile_in, wst.at[pl.ds(2, tiles)], load.at[3]),
        pltpu.make_async_copy(spec_in, wm, load.at[4]),
        pltpu.make_async_copy(mode_in, mode_row, load.at[5]),
        pltpu.make_async_copy(bias_in, bias_row, load.at[6]),
        pltpu.make_async_copy(wall_in, wall, load.at[7]),
        pltpu.make_async_copy(cot_in, cot, load.at[8]),
        pltpu.make_async_copy(offs_in, offs, load.at[9]),
        pltpu.make_async_copy(basis_in, basis, load.at[10]),
    ]
    barrier = pltpu.get_barrier_semaphore()
    each(
        1,
        count,
        lambda d: pl.semaphore_signal(
            barrier, inc=1, device_id=(grp, lax.rem(me + d, count)), device_id_type=MESH
        ),
    )
    for piece in loads:
        piece.start()

    pl.semaphore_wait(barrier, count - 1)
    loads[0].wait()

    low_edge = half - 1

    def low_copy(peer):
        return push(feat.at[0], halo1.at[1], hsend.at[0], hrecv.at[0], peer)

    def high_copy(peer):
        return push(feat.at[xl - 1], halo1.at[0], hsend.at[1], hrecv.at[1], peer)

    def low_cross():
        part = pl.ds(half - 1, half + 1)
        return push(feat.at[0, part], halo1.at[1, part], hsend.at[0], hrecv.at[0], low_edge)

    def high_cross():
        part = pl.ds(0, half + 1)
        return push(feat.at[xl - 1, part], halo1.at[0, part], hsend.at[1], hrecv.at[1], half)

    def low_pass():
        return push(pen1.at[half, 0], halo1.at[1, me], fsend.at[0], frecv.at[me], low_edge)

    def high_pass():
        return push(
            pen1.at[low_edge, xl - 1], halo1.at[0, me], fsend.at[0], frecv.at[me], half
        )

    def low_row(y, peer):
        return push(wgt.at[y, 0], halo2.at[1, y], rsend.at[0, y], rrecv.at[0, y], peer)

    def high_row(y, peer):
        return push(wgt.at[y, xl - 1], halo2.at[0, y], rsend.at[1, y], rrecv.at[1, y], peer)

    def low_relay():
        return push(
            pen2.at[half, 0], halo2.at[1, me], fsend.at[0], rrecv.at[0, me], low_edge
        )

    def high_relay():
        return push(
            pen2.at[low_edge, xl - 1], halo2.at[0, me], fsend.at[0], rrecv.at[1, me], half
        )

    def low_own(y):
        return (me > 0) & ((me != half) | (y >= low_edge))

    def high_own(y):
        return (me < count - 1) & ((me != low_edge) | (y <= half))

    def when(cond, body):
        @pl.when(cond)
        def _():
            body()

    inside_low = (me > 0) & (me != half)
    inside_high = (me < count - 1) & (me != low_edge)
    when(me == half, lambda: low_cross().start())
    when(me == low_edge, lambda: high_cross().start())
    when(inside_low, lambda: low_copy(me - 1).start())
    when(inside_high, lambda: high_copy(me + 1).start())
    others(0, count, by_core, lambda peer: share1(peer).start())

    from_z = lax.broadcasted_iota(jnp.int32, (nz, nz), 0)
    to_z = lax.broadcasted_iota(jnp.int32, (nz, nz), 1)
    for m, dz in enumerate([dz for dz in range(-RAD, RAD + 1) if dz]):
        shift[:, m * nz : (m + 1) * nz] = jnp.where(from_z == to_z + dz, 1.0, 0.0).astype(bf16)

    @pl.when(me == 0)
    def _():
        halo1[0] = jnp.zeros(halo1.shape[1:], bf16)
        halo2[0] = jnp.zeros(halo2.shape[1:], bf16)

    @pl.when(me == count - 1)
    def _():
        halo1[1] = jnp.zeros(halo1.shape[1:], bf16)
        halo2[1] = jnp.zeros(halo2.shape[1:], bf16)

    for edge in (0, RAD + ny):
        for dz in range(2 * RAD + 1):
            for x in range(xl + 2):
                zs[dz, x, edge : edge + RAD] = jnp.zeros((RAD, ch, nz), bf16)

    moves = [dz for dz in range(-RAD, RAD + 1) if dz]
    group = math.gcd(ny, 8)

    def spread(take, place_x):
        def body(i):
            y = i * group
            v = take(pl.ds(y, group))
            zs[RAD, place_x, pl.ds(y + RAD, group)] = v
            flat = v.reshape(group * ch, nz)
            moved = jnp.dot(flat, shift[...], preferred_element_type=f32).astype(bf16)
            for m, dz in enumerate(moves):
                piece = moved[:, m * nz : (m + 1) * nz].reshape(group, ch, nz)
                zs[RAD + dz, place_x, pl.ds(y + RAD, group)] = piece

        each(0, ny // group, body)

    def gather_rows(direction):
        def body(y):
            for x in range(xl):
                lanes = slice(x * nz, (x + 1) * nz)
                centre = zs[RAD, x + 1, y + RAD]
                cat[y, 0:ch, lanes] = centre
                total = zs[RAD, x + 2, y + RAD].astype(f32) + zs[RAD, x, y + RAD].astype(f32)
                total = total + zs[RAD, x + 1, y + RAD + 1].astype(f32)
                total = total + zs[RAD, x + 1, y + RAD - 1].astype(f32)
                total = total + zs[RAD + 1, x + 1, y + RAD].astype(f32)
                total = total + zs[RAD - 1, x + 1, y + RAD].astype(f32)
                cat[y, ch : 2 * ch, lanes] = (total - 6.0 * centre.astype(f32)).astype(bf16)
                for t in range(tiles):
                    moved = zs[
                        RAD + direction * offs[2, t],
                        x + 1 + direction * offs[0, t],
                        y + RAD + direction * offs[1, t],
                    ]
                    cat[y, (2 + t) * ch : (3 + t) * ch, lanes] = moved

        each(0, ny, body)

    unroll = math.gcd(ny, 4)

    def each_row(body):
        def rows_at(i):
            for r in range(unroll):
                body(i * unroll + r)

        each(0, ny // unroll, rows_at)

    def mix(weights):
        def body(y):
            local[y] = jnp.dot(weights[...], cat[y], preferred_element_type=f32)

        each_row(body)

    def gain(planes, src):
        wide = [p.astype(f32) for p in planes]
        for k in range(modes):
            total = acc[k]
            for j in range(xl):
                total = total + basis[k, src * xl + j] * wide[j]
            acc[k] = total

    def forward_mix():
        for k in range(modes):
            v = jnp.dot(wm[k], acc[k].astype(bf16), preferred_element_type=f32)
            v = jnp.where(mode[...] > float(k), v, 0.0)
            vh[k] = v.astype(bf16).astype(f32)

    def backward_mix():
        for k in range(modes):
            u = jnp.where(mode[...] > float(k), acc[k], 0.0).astype(bf16)
            v = jnp.dot(wmt[k], u, preferred_element_type=f32)
            vh[k] = v.astype(bf16).astype(f32)

    def expand(stage, peer):
        for j in range(xl):
            total = basis[0, peer * xl + j] * vh[0]
            for k in range(1, modes):
                total = total + basis[k, peer * xl + j] * vh[k]
            stage[peer, j] = total.astype(bf16)

    for x in range(xl):
        spread(lambda y: feat[x, y], x + 1)
    for piece in loads[1:]:
        piece.wait()

    row_at = lax.broadcasted_iota(jnp.int32, (ch, ch), 0)
    col_at = lax.broadcasted_iota(jnp.int32, (ch, ch), 1)
    diagonal = row_at == col_at
    unit = jnp.where(diagonal, 1.0, 0.0).astype(bf16)

    def upright(row):
        spread_out = jnp.where(diagonal, jnp.broadcast_to(row, (ch, ch)), 0.0)
        column = jnp.sum(spread_out, axis=1, keepdims=True)
        return jnp.broadcast_to(column, (ch, nz))

    mode[...] = upright(mode_row[...].astype(f32))
    bias[...] = upright(bias_row[...])

    def flipped(block):
        return lax.dot_general(
            block, unit, (((0,), (0,)), ((), ())), preferred_element_type=f32
        ).astype(bf16)

    for t in range(2 + tiles):
        wf[:, t * ch : (t + 1) * ch] = wst[t]
        wb[:, t * ch : (t + 1) * ch] = flipped(wst[t])

    def flip_mode(k):
        wmt[k] = flipped(wm[k])

    each(0, modes, flip_mode)

    def passed_low(i):
        push(
            pen1.at[low_edge, xl - 1], halo1.at[0, i], fsend.at[0], frecv.at[i], low_edge
        ).wait_recv()

    def passed_high(i):
        push(pen1.at[half, 0], halo1.at[1, i], fsend.at[0], frecv.at[i], half).wait_recv()

    def forward_stencil():
        when(inside_low, lambda: high_copy(me - 1).wait_recv())
        when(inside_high, lambda: low_copy(me + 1).wait_recv())

        @pl.when(me == half)
        def _():
            high_cross_here = push(
                feat.at[xl - 1, pl.ds(0, half + 1)],
                halo1.at[0, pl.ds(0, half + 1)],
                hsend.at[1],
                hrecv.at[1],
                low_edge,
            )
            high_cross_here.wait_recv()
            each(half + 1, count, passed_low)

        @pl.when(me == low_edge)
        def _():
            low_cross_here = push(
                feat.at[0, pl.ds(half - 1, half + 1)],
                halo1.at[1, pl.ds(half - 1, half + 1)],
                hsend.at[0],
                hrecv.at[0],
                half,
            )
            low_cross_here.wait_recv()
            each(0, half - 1, passed_high)

        spread(lambda y: halo1[0, y], 0)
        spread(lambda y: halo1[1, y], xl + 1)
        gather_rows(1)
        mix(wf)

    core = me % 2
    when(core == 1, forward_stencil)

    acc[...] = jnp.zeros(acc.shape, f32)
    gain([feat[j, me] for j in range(xl)], me)

    def take1(src):
        land1(src).wait_recv()
        when((src == half) & (me < low_edge), lambda: low_pass().start())
        when((src == low_edge) & (me > half), lambda: high_pass().start())
        gain([pen1[src, j] for j in range(xl)], src)

    others(0, count, from_side, take1)
    forward_mix()

    def hand1(peer):
        expand(stage1, peer)
        give1(peer).start()

    others(0, count, by_side, hand1)
    expand(stage1, me)
    when(core == 0, forward_stencil)
    root = math.sqrt(2.0 / math.pi)

    def slope(y, planes):
        for x in range(xl):
            v = local[y, :, x * nz : (x + 1) * nz] + planes[x].astype(f32) + bias[...]
            square = v * v
            t = jnp.tanh(root * (v + 0.044715 * (square * v)))
            g = 0.5 * (1.0 + t)
            g = g + (0.5 * v) * ((1.0 - t * t) * (root * (1.0 + (3.0 * 0.044715) * square)))
            fluid = (1 - wall[x, pl.ds(y, 1), :]).astype(f32)
            wgt[y, x] = ((cot[x, y].astype(f32) * g) * fluid).astype(bf16)
        when(low_own(y), lambda: low_row(y, me - 1).start())
        when(high_own(y), lambda: high_row(y, me + 1).start())

    kacc[...] = jnp.zeros(kacc.shape, f32)

    def row_work(y):
        planes = jnp.concatenate([wgt[y, x] for x in range(xl)], axis=1)
        kacc[...] += lax.dot_general(
            cat[y, 2 * ch :, :], planes, (((1,), (1,)), ((), ())), preferred_element_type=f32
        )
        flat = jnp.concatenate([wgt[y, x] for x in range(xl)], axis=0)
        moved = jnp.dot(flat, shift[...], preferred_element_type=f32).astype(bf16)
        for x in range(xl):
            zs[RAD, x + 1, y + RAD] = wgt[y, x]
            for m, dz in enumerate(moves):
                piece = moved[x * ch : (x + 1) * ch, m * nz : (m + 1) * nz]
                zs[RAD + dz, x + 1, y + RAD] = piece

    slope(me, [stage1[me, j] for j in range(xl)])
    row_work(me)

    def turn(src):
        back1(src).wait_recv()
        slope(src, [spec1[src, j] for j in range(xl)])
        share2(src).start()
        row_work(src)

    others(0, count, by_core, turn)

    pairs = tiles // 2
    for t in range(pairs):
        kdense[t * ch : (t + 1) * ch] = jnp.concatenate(
            [
                jnp.transpose(kacc[p * ch : (p + 1) * ch])
                for p in (t, t + pairs)
            ],
            axis=1,
        )

    rows = kpart.shape[1]

    def strip(p):
        return kdense.at[pl.ds(p * rows, rows)]

    def near(body):
        def visit(d):
            body((inner + d) % half)

        each(1, half, visit)

    def ksend_to(p):
        return push(
            strip(p), kpart.at[inner], ksend.at[0, p], krecv.at[0, inner], side * half + p
        )

    def kland(p):
        return push(strip(p), kpart.at[p], ksend.at[0, p], krecv.at[0, p], side * half + p)

    near(lambda p: ksend_to(p).start())

    acc[...] = jnp.zeros(acc.shape, f32)
    gain([wgt[me, j] for j in range(xl)], me)

    def take2(src):
        land2(src).wait_recv()
        when((src == half) & (me < low_edge), lambda: low_relay().start())
        when((src == low_edge) & (me > half), lambda: high_relay().start())
        gain([pen2[src, j] for j in range(xl)], src)

    when(me < low_edge, lambda: low_pass().wait_send())
    when(me > half, lambda: high_pass().wait_send())
    others(0, count, from_side, take2)
    backward_mix()

    def hand2(peer):
        expand(stage2, peer)
        give2(peer).start()

    others(0, quads, by_side, hand2)
    kpart[inner] = kdense[pl.ds(inner * rows, rows)]
    near(lambda p: kland(p).wait_recv())
    part_sum = kpart[0]
    for p in range(1, half):
        part_sum = part_sum + kpart[p]
    kmine[...] = part_sum
    partner = ((side + 1) % 2) * half + inner
    across = push(kmine, kother, xsend.at[0], xrecv.at[0], partner)
    across.start()
    others(quads, count, by_side, hand2)
    expand(stage2, me)

    def halo_rows(y):
        when(me > 0, lambda: high_row(y, me - 1).wait_recv())
        when(me < count - 1, lambda: low_row(y, me + 1).wait_recv())

    each(0, ny, halo_rows)
    spread(lambda y: halo2[0, y], 0)
    spread(lambda y: halo2[1, y], xl + 1)
    gather_rows(-1)

    mix(wb)

    across.wait_recv()
    ksum[...] = (kmine[...] + kother[...]) * (float(count * xl * ny * nz) ** -0.5)
    kall[pl.ds(inner * rows, rows)] = ksum[...]

    def piece_of(p):
        return kall.at[pl.ds(p * rows, rows)]

    def kspread(p):
        return push(ksum, piece_of(inner), ksend.at[1, p], krecv.at[1, inner], side * half + p)

    def kcollect(p):
        return push(ksum, piece_of(p), ksend.at[1, p], krecv.at[1, p], side * half + p)

    near(lambda p: kspread(p).start())

    def finish(y, planes):
        for x in range(xl):
            total = local[y, :, x * nz : (x + 1) * nz] + planes[x].astype(f32)
            out[x, y] = total.astype(bf16)

    finish(me, [stage2[me, j] for j in range(xl)])

    def last(src):
        back2(src).wait_recv()
        finish(src, [spec2[src, j] for j in range(xl)])

    others(half, count, from_side, last)
    others(0, half, from_side, last)
    near(lambda p: kcollect(p).wait_recv())
    for t in range(pairs):
        kout[t] = kall[t * ch : (t + 1) * ch, 0:ch]
        kout[t + pairs] = kall[t * ch : (t + 1) * ch, ch : 2 * ch]

    when(me == half, lambda: low_cross().wait_send())
    when(me == low_edge, lambda: high_cross().wait_send())
    when(inside_low, lambda: low_copy(me - 1).wait_send())
    when(inside_high, lambda: high_copy(me + 1).wait_send())

    def row_sent(y):
        when(low_own(y), lambda: low_row(y, me - 1).wait_send())
        when(high_own(y), lambda: high_row(y, me + 1).wait_send())

    each(0, ny, row_sent)
    when(me < low_edge, lambda: low_relay().wait_send())
    when(me > half, lambda: high_relay().wait_send())
    across.wait_send()

    def near_sent(p):
        ksend_to(p).wait_send()
        kspread(p).wait_send()

    near(near_sent)

    def drain(peer):
        share1(peer).wait_send()
        give1(peer).wait_send()
        share2(peer).wait_send()
        give2(peer).wait_send()

    others(0, count, by_side, drain)


def fits_kernel(count, features, kernel_weight):
    xl, ny, ch, nz = features.shape
    cells = xl * ny * ch * nz
    tile_rows = kernel_weight.shape[0] * ch
    if ny != count or count % 4 or nz % 128 or ch % 64 or kernel_weight.shape[0] % 2:
        return False
    if tile_rows % (8 * count):
        return False
    return 80 * cells < 24 * 2**20


def fused_device(
    features,
    cotangent,
    wall_flags,
    mode_counts,
    offsets,
    point_weight,
    kernel_weight,
    lap_weight,
    spec_weight,
    bias,
):
    count = lax.axis_size("gx")
    if not fits_kernel(count, features, kernel_weight):
        return per_device(
            features,
            cotangent,
            wall_flags,
            mode_counts,
            offsets,
            point_weight,
            kernel_weight,
            lap_weight,
            spec_weight,
            bias,
        )
    xl, ny, ch, nz = features.shape
    modes, tiles = spec_weight.shape[0], kernel_weight.shape[0]
    half = count // 2
    rows = tiles * ch // (2 * half)
    f32, bf16 = jnp.float32, jnp.bfloat16
    dma = pltpu.SemaphoreType.DMA
    vmem = pl.BlockSpec(memory_space=pltpu.VMEM)
    hbm = pl.BlockSpec(memory_space=pltpu.HBM)
    field_grad, tile_grad = pl.pallas_call(
        functools.partial(fused_kernel, count),
        out_shape=(
            pltpu.VMEM(features.shape, bf16),
            pltpu.VMEM(kernel_weight.shape, f32),
        ),
        in_specs=[hbm, hbm, hbm, hbm, hbm, hbm, hbm, hbm, hbm, hbm, hbm],
        out_specs=(vmem, vmem),
        scratch_shapes=[
            pltpu.VMEM((xl, ny, ch, nz), bf16),
            pltpu.VMEM((xl, ny, ch, nz), bf16),
            pltpu.VMEM((xl, ny, nz), jnp.int32),
            pltpu.VMEM((1, ch), jnp.int32),
            pltpu.VMEM((1, ch), f32),
            pltpu.SMEM((3, tiles), jnp.int32),
            pltpu.SMEM((modes, count * xl), f32),
            pltpu.VMEM((2 + tiles, ch, ch), bf16),
            pltpu.VMEM((modes, ch, ch), bf16),
            pltpu.VMEM((modes, ch, ch), bf16),
            pltpu.VMEM((ch, (2 + tiles) * ch), bf16),
            pltpu.VMEM((ch, (2 + tiles) * ch), bf16),
            pltpu.VMEM((ch, nz), f32),
            pltpu.VMEM((ch, nz), f32),
            pltpu.VMEM((2 * RAD + 1, xl + 2, ny + 2 * RAD, ch, nz), bf16),
            pltpu.VMEM((ny, (2 + tiles) * ch, xl * nz), bf16),
            pltpu.VMEM((ny, ch, xl * nz), f32),
            pltpu.VMEM((modes, ch, nz), f32),
            pltpu.VMEM((modes, ch, nz), f32),
            pltpu.VMEM((count, xl, ch, nz), bf16),
            pltpu.VMEM((count, xl, ch, nz), bf16),
            pltpu.VMEM((count, xl, ch, nz), bf16),
            pltpu.VMEM((count, xl, ch, nz), bf16),
            pltpu.VMEM((count, xl, ch, nz), bf16),
            pltpu.VMEM((count, xl, ch, nz), bf16),
            pltpu.VMEM((ny, xl, ch, nz), bf16),
            pltpu.VMEM((2, ny, ch, nz), bf16),
            pltpu.VMEM((2, ny, ch, nz), bf16),
            pltpu.VMEM((tiles * ch, ch), f32),
            pltpu.VMEM((tiles * ch // 2, 2 * ch), f32),
            pltpu.VMEM((half, rows, 2 * ch), f32),
            pltpu.VMEM((rows, 2 * ch), f32),
            pltpu.VMEM((rows, 2 * ch), f32),
            pltpu.VMEM((rows, 2 * ch), f32),
            pltpu.VMEM((tiles * ch // 2, 2 * ch), f32),
            pltpu.VMEM((nz, 2 * RAD * nz), bf16),
            dma((4, count)),
            dma((4, count)),
            dma((2,)),
            dma((2,)),
            dma((2, ny)),
            dma((2, ny)),
            dma((2, half)),
            dma((2, half)),
            dma((1,)),
            dma((1,)),
            dma((1,)),
            dma((ny,)),
            dma((11,)),
        ],
        compiler_params=pltpu.CompilerParams(
            collective_id=0, has_side_effects=True, vmem_limit_bytes=56 * 2**20
        ),
    )(
        features,
        cotangent,
        wall_flags,
        mode_counts.reshape(1, ch),
        offsets.T,
        basis_constant(modes, count * xl),
        point_weight,
        kernel_weight,
        lap_weight,
        spec_weight,
        bias.reshape(1, ch),
    )
    return field_grad, tile_grad


def solution(mesh):
    return jax.shard_map(
        fused_device,
        mesh=mesh,
        in_specs=(
            P(("groups", "gx"), None, None, None),
            P(("groups", "gx"), None, None, None),
            P(("groups", "gx"), None, None),
            P(),
            P(),
            P(),
            P(),
            P(),
            P(),
            P(),
        ),
        out_specs=(P(("groups", "gx"), None, None, None), P("groups", None, None)),
        check_vma=False,
    )
```

```python
import functools
from functools import partial
import math

import jax
import ml_dtypes
import numpy as np
import jax.numpy as jnp
from jax import lax
from jax.experimental import pallas as pl
from jax.experimental.pallas import tpu as pltpu
from jax.sharding import PartitionSpec as P

RAD = 2
MESH = pl.DeviceIdType.MESH


def with_halo(cells, sides, width):
    for axis, dim in sides:
        count = lax.axis_size(axis)
        ends = count - 1
        head = lax.slice_in_dim(cells, 0, width, axis=dim)
        tail = lax.slice_in_dim(cells, cells.shape[dim] - width, cells.shape[dim], axis=dim)
        cells = jnp.concatenate(
            [
                lax.ppermute(tail, axis, [(i, (i + 1) % count) for i in range(ends)]),
                cells,
                lax.ppermute(head, axis, [((i + 1) % count, i) for i in range(ends)]),
            ],
            axis=dim,
        )
    return cells


def basis_table(mode_total, length):
    mode_index = jnp.arange(mode_total, dtype=jnp.float32)[:, None]
    cell_index = jnp.arange(length, dtype=jnp.float32)[None, :]
    phase_angle = math.pi / (2.0 * length) * mode_index * (2.0 * cell_index + 1.0)
    amplitude = jnp.where(mode_index == 0.0, math.sqrt(1.0 / length), math.sqrt(2.0 / length))
    return (amplitude * jnp.cos(phase_angle)).astype(jnp.bfloat16)


def basis_constant(mode_total, length):
    mode_index = np.arange(mode_total, dtype=np.float64)[:, None]
    cell_index = np.arange(length, dtype=np.float64)[None, :]
    phase_angle = math.pi / (2.0 * length) * mode_index * (2.0 * cell_index + 1.0)
    amplitude = np.where(mode_index == 0.0, math.sqrt(1.0 / length), math.sqrt(2.0 / length))
    table = (amplitude * np.cos(phase_angle)).astype(np.float32)
    return table.astype(ml_dtypes.bfloat16).astype(np.float32)


def pencil_work(pencil, spec_weight, kept_modes, adjoint):
    basis = basis_table(spec_weight.shape[0], pencil.shape[0])
    coefficients = jnp.einsum(
        "kx,xycz->kycz", basis, pencil, preferred_element_type=jnp.float32
    ).astype(jnp.bfloat16)
    if adjoint:
        masked = coefficients * kept_modes[:, None, :, None].astype(jnp.bfloat16)
        mixed_modes = jnp.einsum(
            "koc,kyoz->kycz", spec_weight, masked, preferred_element_type=jnp.float32
        ).astype(jnp.bfloat16)
    else:
        mixed_modes = jnp.einsum(
            "koc,kycz->kyoz", spec_weight, coefficients, preferred_element_type=jnp.float32
        )
        mixed_modes = (mixed_modes * kept_modes[:, None, :, None]).astype(jnp.bfloat16)
    return jnp.einsum(
        "kx,kyoz->xyoz", basis, mixed_modes, preferred_element_type=jnp.float32
    ).astype(jnp.bfloat16)


def spectral(slab, spec_weight, kept_modes, adjoint):
    result = pencil_work(
        lax.all_to_all(slab, "gx", split_axis=1, concat_axis=0, tiled=True),
        spec_weight,
        kept_modes,
        adjoint,
    )
    return lax.all_to_all(result, "gx", split_axis=0, concat_axis=1, tiled=True)


def laplace_ext(extended):
    padded = jnp.pad(extended, ((0, 0), (1, 1), (0, 0), (1, 1))).astype(jnp.float32)
    centre_cells = padded[1:-1, 1:-1, :, 1:-1]
    neighbours = padded[2:, 1:-1, :, 1:-1] + padded[:-2, 1:-1, :, 1:-1]
    neighbours = neighbours + padded[1:-1, 2:, :, 1:-1] + padded[1:-1, :-2, :, 1:-1]
    neighbours = neighbours + padded[1:-1, 1:-1, :, 2:] + padded[1:-1, 1:-1, :, :-2]
    return (neighbours - 6.0 * centre_cells).astype(jnp.bfloat16)


def pad_sides(extended):
    return jnp.pad(extended, ((0, 0), (RAD, RAD), (0, 0), (RAD, RAD)))


def window_of(padded, offset, direction, slab_shape):
    starts = (
        1 + direction * offset[0],
        RAD + direction * offset[1],
        0,
        RAD + direction * offset[2],
    )
    return lax.dynamic_slice(padded, starts, slab_shape)


def gelu_slope(preact, upstream):
    _, pullback = jax.vjp(partial(jax.nn.gelu, approximate=True), preact)
    return pullback(upstream)[0]


def sum_over_gx(terms):
    count = lax.axis_size("gx")
    if terms.size % count:
        return lax.psum(terms, "gx")
    pieces = lax.all_to_all(terms.reshape(count, -1), "gx", split_axis=0, concat_axis=0, tiled=True)
    mine = jnp.sum(pieces, axis=0)
    copies = jnp.broadcast_to(mine[None, :], pieces.shape)
    gathered = lax.all_to_all(copies, "gx", split_axis=0, concat_axis=0, tiled=True)
    return gathered.reshape(terms.shape)


def per_device(
    features,
    cotangent,
    wall_flags,
    mode_counts,
    offsets,
    point_weight,
    kernel_weight,
    lap_weight,
    spec_weight,
    bias,
):
    mode_total = spec_weight.shape[0]
    tile_total = kernel_weight.shape[0]
    kept_modes = (jnp.arange(mode_total, dtype=jnp.int32)[:, None] < mode_counts[None, :]).astype(
        jnp.float32
    )
    fluid_mask = (1 - wall_flags).astype(jnp.float32)[:, :, None, :]
    extended = with_halo(features, (("gx", 0),), 1)
    padded_field = pad_sides(extended)
    local_part = jnp.einsum(
        "oc,xycz->xyoz", point_weight, features, preferred_element_type=jnp.float32
    )
    local_part = local_part + jnp.einsum(
        "oc,xycz->xyoz", lap_weight, laplace_ext(extended), preferred_element_type=jnp.float32
    )
    for tile in range(tile_total):
        moved = window_of(padded_field, offsets[tile], 1, features.shape)
        local_part = local_part + jnp.einsum(
            "oc,xycz->xyoz", kernel_weight[tile], moved, preferred_element_type=jnp.float32
        )
    local_part = local_part + bias[:, None]
    spectral_part = spectral(features, spec_weight, kept_modes, False)
    preact = local_part + spectral_part.astype(jnp.float32)
    weighted = (gelu_slope(preact, cotangent.astype(jnp.float32)) * fluid_mask).astype(jnp.bfloat16)
    spec_grad = spectral(weighted, spec_weight, kept_modes, True)
    ext_grad = with_halo(weighted, (("gx", 0),), 1)
    padded_grad = pad_sides(ext_grad)
    input_grad = jnp.einsum(
        "oc,xyoz->xycz", point_weight, weighted, preferred_element_type=jnp.float32
    )
    input_grad = input_grad + jnp.einsum(
        "oc,xyoz->xycz", lap_weight, laplace_ext(ext_grad), preferred_element_type=jnp.float32
    )
    input_grad = input_grad + spec_grad.astype(jnp.float32)
    tile_grads = []
    for tile in range(tile_total):
        back_moved = window_of(padded_grad, offsets[tile], -1, weighted.shape)
        input_grad = input_grad + jnp.einsum(
            "oc,xyoz->xycz", kernel_weight[tile], back_moved, preferred_element_type=jnp.float32
        )
        tile_grads.append(
            jnp.einsum("xyoz,xycz->oc", back_moved, features, preferred_element_type=jnp.float32)
        )
    local_grad = jnp.stack(tile_grads, axis=0)
    scaling = float(
        lax.axis_size("gx") * features.shape[0] * features.shape[1] * features.shape[3]
    ) ** (-0.5)
    summed = sum_over_gx(local_grad)
    return (input_grad.astype(jnp.bfloat16), summed * scaling)


def fused_kernel(
    count,
    feat_in,
    cot_in,
    wall_in,
    mode_in,
    offs_in,
    basis_in,
    point_in,
    tile_in,
    lap_in,
    spec_in,
    bias_in,
    out,
    kout,
    feat,
    cot,
    wall,
    mode_row,
    bias_row,
    offs,
    basis,
    wst,
    wm,
    wmt,
    wf,
    wb,
    mode,
    bias,
    zs,
    cat,
    local,
    acc,
    vh,
    pen1,
    pen2,
    stage1,
    stage2,
    spec1,
    spec2,
    wgt,
    halo1,
    halo2,
    kacc,
    kdense,
    kpart,
    kmine,
    kother,
    ksum,
    kall,
    shift,
    send,
    recv,
    hsend,
    hrecv,
    rsend,
    rrecv,
    ksend,
    krecv,
    xsend,
    xrecv,
    fsend,
    frecv,
    load,
):
    me = lax.axis_index("gx")
    grp = lax.axis_index("groups")
    xl, ny, ch, nz = feat.shape
    modes = wm.shape[0]
    tiles = offs.shape[1]
    half = count // 2
    quads = half // 2
    f32, bf16 = jnp.float32, jnp.bfloat16
    side = me // half
    inner = me % half
    chip = inner // 2

    def push(src, dst, ssem, rsem, peer):
        return pltpu.make_async_remote_copy(
            src_ref=src,
            dst_ref=dst,
            send_sem=ssem,
            recv_sem=rsem,
            device_id=(grp, peer),
            device_id_type=MESH,
        )

    def each(low, high, body):
        def step(i, carry):
            body(i)
            return carry

        lax.fori_loop(low, high, step, 0)

    def place(cross, turn, core):
        return ((side + cross) % 2) * half + ((chip + turn) % quads) * 2 + core

    def by_core(j):
        core = j // half
        rest = j % half
        return place(1 - rest // quads, rest % quads, core)

    def by_side(j):
        rest = j % half
        return place(1 - j // half, rest // 2, rest % 2)

    def from_side(j):
        rest = j % half
        return place(1 - j // half, quads - rest // 2, rest % 2)

    def from_core(j):
        core = j // half
        rest = j % half
        return place(1 - rest // quads, quads - rest % quads, core)

    def others(low, high, order, body):
        def visit(j):
            peer = order(j)

            @pl.when(peer != me)
            def _():
                body(peer)

        each(low, high, visit)

    def share1(peer):
        return push(
            feat.at[:, peer], pen1.at[me], send.at[0, peer], recv.at[0, me], peer
        )

    def land1(src):
        return push(feat.at[:, src], pen1.at[src], send.at[0, src], recv.at[0, src], src)

    def give1(peer):
        return push(stage1.at[peer], spec1.at[me], send.at[1, peer], recv.at[1, me], peer)

    def back1(src):
        return push(stage1.at[src], spec1.at[src], send.at[1, src], recv.at[1, src], src)

    def share2(peer):
        return push(wgt.at[peer], pen2.at[me], send.at[2, peer], recv.at[2, me], peer)

    def land2(src):
        return push(wgt.at[src], pen2.at[src], send.at[2, src], recv.at[2, src], src)

    def give2(peer):
        return push(stage2.at[peer], spec2.at[me], send.at[3, peer], recv.at[3, me], peer)

    def back2(src):
        return push(stage2.at[src], spec2.at[src], send.at[3, src], recv.at[3, src], src)

    loads = [
        pltpu.make_async_copy(feat_in, feat, load.at[0]),
        pltpu.make_async_copy(point_in, wst.at[0], load.at[1]),
        pltpu.make_async_copy(lap_in, wst.at[1], load.at[2]),
        pltpu.make_async_copy(tile_in, wst.at[pl.ds(2, tiles)], load.at[3]),
        pltpu.make_async_copy(spec_in, wm, load.at[4]),
        pltpu.make_async_copy(mode_in, mode_row, load.at[5]),
        pltpu.make_async_copy(bias_in, bias_row, load.at[6]),
        pltpu.make_async_copy(wall_in, wall, load.at[7]),
        pltpu.make_async_copy(cot_in, cot, load.at[8]),
        pltpu.make_async_copy(offs_in, offs, load.at[9]),
        pltpu.make_async_copy(basis_in, basis, load.at[10]),
    ]
    barrier = pltpu.get_barrier_semaphore()
    each(
        1,
        count,
        lambda d: pl.semaphore_signal(
            barrier, inc=1, device_id=(grp, lax.rem(me + d, count)), device_id_type=MESH
        ),
    )
    for piece in loads:
        piece.start()

    pl.semaphore_wait(barrier, count - 1)
    loads[0].wait()

    low_edge = half - 1

    def low_copy(peer):
        return push(feat.at[0], halo1.at[1], hsend.at[0], hrecv.at[0], peer)

    def high_copy(peer):
        return push(feat.at[xl - 1], halo1.at[0], hsend.at[1], hrecv.at[1], peer)

    def low_cross():
        part = pl.ds(half - 1, half + 1)
        return push(feat.at[0, part], halo1.at[1, part], hsend.at[0], hrecv.at[0], low_edge)

    def high_cross():
        part = pl.ds(0, half + 1)
        return push(feat.at[xl - 1, part], halo1.at[0, part], hsend.at[1], hrecv.at[1], half)

    def low_pass():
        return push(pen1.at[half, 0], halo1.at[1, me], fsend.at[0], frecv.at[me], low_edge)

    def high_pass():
        return push(
            pen1.at[low_edge, xl - 1], halo1.at[0, me], fsend.at[0], frecv.at[me], half
        )

    def low_row(y, peer):
        return push(wgt.at[y, 0], halo2.at[1, y], rsend.at[0, y], rrecv.at[0, y], peer)

    def high_row(y, peer):
        return push(wgt.at[y, xl - 1], halo2.at[0, y], rsend.at[1, y], rrecv.at[1, y], peer)

    def low_relay():
        return push(
            pen2.at[half, 0], halo2.at[1, me], fsend.at[0], rrecv.at[0, me], low_edge
        )

    def high_relay():
        return push(
            pen2.at[low_edge, xl - 1], halo2.at[0, me], fsend.at[0], rrecv.at[1, me], half
        )

    def low_own(y):
        return (me > 0) & ((me != half) | (y >= low_edge))

    def high_own(y):
        return (me < count - 1) & ((me != low_edge) | (y <= half))

    def when(cond, body):
        @pl.when(cond)
        def _():
            body()

    inside_low = (me > 0) & (me != half)
    inside_high = (me < count - 1) & (me != low_edge)
    when(me == half, lambda: low_cross().start())
    when(me == low_edge, lambda: high_cross().start())
    when(inside_low, lambda: low_copy(me - 1).start())
    when(inside_high, lambda: high_copy(me + 1).start())
    others(0, count, by_core, lambda peer: share1(peer).start())

    from_z = lax.broadcasted_iota(jnp.int32, (nz, nz), 0)
    to_z = lax.broadcasted_iota(jnp.int32, (nz, nz), 1)
    for m, dz in enumerate([dz for dz in range(-RAD, RAD + 1) if dz]):
        shift[:, m * nz : (m + 1) * nz] = jnp.where(from_z == to_z + dz, 1.0, 0.0).astype(bf16)

    @pl.when(me == 0)
    def _():
        halo1[0] = jnp.zeros(halo1.shape[1:], bf16)
        halo2[0] = jnp.zeros(halo2.shape[1:], bf16)

    @pl.when(me == count - 1)
    def _():
        halo1[1] = jnp.zeros(halo1.shape[1:], bf16)
        halo2[1] = jnp.zeros(halo2.shape[1:], bf16)

    for edge in (0, RAD + ny):
        for dz in range(2 * RAD + 1):
            for x in range(xl + 2):
                zs[dz, x, edge : edge + RAD] = jnp.zeros((RAD, ch, nz), bf16)

    moves = [dz for dz in range(-RAD, RAD + 1) if dz]
    group = math.gcd(ny, 8)

    def spread(take, place_x):
        def body(i):
            y = i * group
            v = take(pl.ds(y, group))
            zs[RAD, place_x, pl.ds(y + RAD, group)] = v
            flat = v.reshape(group * ch, nz)
            moved = jnp.dot(flat, shift[...], preferred_element_type=f32).astype(bf16)
            for m, dz in enumerate(moves):
                piece = moved[:, m * nz : (m + 1) * nz].reshape(group, ch, nz)
                zs[RAD + dz, place_x, pl.ds(y + RAD, group)] = piece

        each(0, ny // group, body)

    def gather_rows(direction):
        def body(y):
            for x in range(xl):
                lanes = slice(x * nz, (x + 1) * nz)
                centre = zs[RAD, x + 1, y + RAD]
                cat[y, 0:ch, lanes] = centre
                total = zs[RAD, x + 2, y + RAD].astype(f32) + zs[RAD, x, y + RAD].astype(f32)
                total = total + zs[RAD, x + 1, y + RAD + 1].astype(f32)
                total = total + zs[RAD, x + 1, y + RAD - 1].astype(f32)
                total = total + zs[RAD + 1, x + 1, y + RAD].astype(f32)
                total = total + zs[RAD - 1, x + 1, y + RAD].astype(f32)
                cat[y, ch : 2 * ch, lanes] = (total - 6.0 * centre.astype(f32)).astype(bf16)
                for t in range(tiles):
                    moved = zs[
                        RAD + direction * offs[2, t],
                        x + 1 + direction * offs[0, t],
                        y + RAD + direction * offs[1, t],
                    ]
                    cat[y, (2 + t) * ch : (3 + t) * ch, lanes] = moved

        each(0, ny, body)

    unroll = math.gcd(ny, 4)

    def each_row(body):
        def rows_at(i):
            for r in range(unroll):
                body(i * unroll + r)

        each(0, ny // unroll, rows_at)

    def mix(weights):
        def body(y):
            local[y] = jnp.dot(weights[...], cat[y], preferred_element_type=f32)

        each_row(body)

    def gain(planes, src):
        wide = [p.astype(f32) for p in planes]
        for k in range(modes):
            total = acc[k]
            for j in range(xl):
                total = total + basis[k, src * xl + j] * wide[j]
            acc[k] = total

    def forward_mix():
        for k in range(modes):
            v = jnp.dot(wm[k], acc[k].astype(bf16), preferred_element_type=f32)
            v = jnp.where(mode[...] > float(k), v, 0.0)
            vh[k] = v.astype(bf16).astype(f32)

    def backward_mix():
        for k in range(modes):
            u = jnp.where(mode[...] > float(k), acc[k], 0.0).astype(bf16)
            v = jnp.dot(wmt[k], u, preferred_element_type=f32)
            vh[k] = v.astype(bf16).astype(f32)

    def expand(stage, peer):
        for j in range(xl):
            total = basis[0, peer * xl + j] * vh[0]
            for k in range(1, modes):
                total = total + basis[k, peer * xl + j] * vh[k]
            stage[peer, j] = total.astype(bf16)

    for x in range(xl):
        spread(lambda y: feat[x, y], x + 1)
    for piece in loads[1:]:
        piece.wait()

    row_at = lax.broadcasted_iota(jnp.int32, (ch, ch), 0)
    col_at = lax.broadcasted_iota(jnp.int32, (ch, ch), 1)
    diagonal = row_at == col_at
    unit = jnp.where(diagonal, 1.0, 0.0).astype(bf16)

    def upright(row):
        spread_out = jnp.where(diagonal, jnp.broadcast_to(row, (ch, ch)), 0.0)
        column = jnp.sum(spread_out, axis=1, keepdims=True)
        return jnp.broadcast_to(column, (ch, nz))

    mode[...] = upright(mode_row[...].astype(f32))
    bias[...] = upright(bias_row[...])

    def flipped(block):
        return lax.dot_general(
            block, unit, (((0,), (0,)), ((), ())), preferred_element_type=f32
        ).astype(bf16)

    for t in range(2 + tiles):
        wf[:, t * ch : (t + 1) * ch] = wst[t]
        wb[:, t * ch : (t + 1) * ch] = flipped(wst[t])

    def flip_mode(k):
        wmt[k] = flipped(wm[k])

    each(0, modes, flip_mode)

    def passed_low(i):
        push(
            pen1.at[low_edge, xl - 1], halo1.at[0, i], fsend.at[0], frecv.at[i], low_edge
        ).wait_recv()

    def passed_high(i):
        push(pen1.at[half, 0], halo1.at[1, i], fsend.at[0], frecv.at[i], half).wait_recv()

    def forward_stencil():
        when(inside_low, lambda: high_copy(me - 1).wait_recv())
        when(inside_high, lambda: low_copy(me + 1).wait_recv())

        @pl.when(me == half)
        def _():
            high_cross_here = push(
                feat.at[xl - 1, pl.ds(0, half + 1)],
                halo1.at[0, pl.ds(0, half + 1)],
                hsend.at[1],
                hrecv.at[1],
                low_edge,
            )
            high_cross_here.wait_recv()
            each(half + 1, count, passed_low)

        @pl.when(me == low_edge)
        def _():
            low_cross_here = push(
                feat.at[0, pl.ds(half - 1, half + 1)],
                halo1.at[1, pl.ds(half - 1, half + 1)],
                hsend.at[0],
                hrecv.at[0],
                half,
            )
            low_cross_here.wait_recv()
            each(0, half - 1, passed_high)

        spread(lambda y: halo1[0, y], 0)
        spread(lambda y: halo1[1, y], xl + 1)
        gather_rows(1)
        mix(wf)

    core = me % 2
    early = (core == 1) & (me != low_edge)
    when(early, forward_stencil)

    acc[...] = jnp.zeros(acc.shape, f32)
    gain([feat[j, me] for j in range(xl)], me)

    def take1(src):
        land1(src).wait_recv()
        when((src == half) & (me < low_edge), lambda: low_pass().start())
        when((src == low_edge) & (me > half), lambda: high_pass().start())
        gain([pen1[src, j] for j in range(xl)], src)

    others(0, count, from_side, take1)
    forward_mix()

    def hand1(peer):
        expand(stage1, peer)
        give1(peer).start()

    others(0, count, by_core, hand1)
    expand(stage1, me)
    when(jnp.logical_not(early), forward_stencil)
    root = math.sqrt(2.0 / math.pi)

    def slope(y, planes):
        for x in range(xl):
            v = local[y, :, x * nz : (x + 1) * nz] + planes[x].astype(f32) + bias[...]
            square = v * v
            t = jnp.tanh(root * (v + 0.044715 * (square * v)))
            g = 0.5 * (1.0 + t)
            g = g + (0.5 * v) * ((1.0 - t * t) * (root * (1.0 + (3.0 * 0.044715) * square)))
            fluid = (1 - wall[x, pl.ds(y, 1), :]).astype(f32)
            wgt[y, x] = ((cot[x, y].astype(f32) * g) * fluid).astype(bf16)
        when(low_own(y), lambda: low_row(y, me - 1).start())
        when(high_own(y), lambda: high_row(y, me + 1).start())

    kacc[...] = jnp.zeros(kacc.shape, f32)

    def row_work(y):
        planes = jnp.concatenate([wgt[y, x] for x in range(xl)], axis=1)
        kacc[...] += lax.dot_general(
            cat[y, 2 * ch :, :], planes, (((1,), (1,)), ((), ())), preferred_element_type=f32
        )
        flat = jnp.concatenate([wgt[y, x] for x in range(xl)], axis=0)
        moved = jnp.dot(flat, shift[...], preferred_element_type=f32).astype(bf16)
        for x in range(xl):
            zs[RAD, x + 1, y + RAD] = wgt[y, x]
            for m, dz in enumerate(moves):
                piece = moved[x * ch : (x + 1) * ch, m * nz : (m + 1) * nz]
                zs[RAD + dz, x + 1, y + RAD] = piece

    slope(me, [stage1[me, j] for j in range(xl)])
    row_work(me)

    def turn(src):
        back1(src).wait_recv()
        slope(src, [spec1[src, j] for j in range(xl)])
        share2(src).start()
        row_work(src)

    others(0, count, by_core, turn)

    pairs = tiles // 2
    for t in range(pairs):
        kdense[t * ch : (t + 1) * ch] = jnp.concatenate(
            [
                jnp.transpose(kacc[p * ch : (p + 1) * ch])
                for p in (t, t + pairs)
            ],
            axis=1,
        )

    rows = kpart.shape[1]

    def strip(p):
        return kdense.at[pl.ds(p * rows, rows)]

    def near(body):
        def visit(d):
            body((inner + d) % half)

        each(1, half, visit)

    def ksend_to(p):
        return push(
            strip(p), kpart.at[inner], ksend.at[0, p], krecv.at[0, inner], side * half + p
        )

    def kland(p):
        return push(strip(p), kpart.at[p], ksend.at[0, p], krecv.at[0, p], side * half + p)

    near(lambda p: ksend_to(p).start())

    acc[...] = jnp.zeros(acc.shape, f32)
    gain([wgt[me, j] for j in range(xl)], me)

    def take2(src):
        land2(src).wait_recv()
        when((src == half) & (me < low_edge), lambda: low_relay().start())
        when((src == low_edge) & (me > half), lambda: high_relay().start())
        gain([pen2[src, j] for j in range(xl)], src)

    when(me < low_edge, lambda: low_pass().wait_send())
    when(me > half, lambda: high_pass().wait_send())
    others(0, count, from_side, take2)
    backward_mix()

    def hand2(peer):
        expand(stage2, peer)
        give2(peer).start()

    others(0, quads, by_core, hand2)
    kpart[inner] = kdense[pl.ds(inner * rows, rows)]
    near(lambda p: kland(p).wait_recv())
    part_sum = kpart[0]
    for p in range(1, half):
        part_sum = part_sum + kpart[p]
    kmine[...] = part_sum
    partner = ((side + 1) % 2) * half + inner
    across = push(kmine, kother, xsend.at[0], xrecv.at[0], partner)
    across.start()
    others(quads, count, by_core, hand2)
    expand(stage2, me)

    def halo_rows(y):
        when(me > 0, lambda: high_row(y, me - 1).wait_recv())
        when(me < count - 1, lambda: low_row(y, me + 1).wait_recv())

    each(0, ny, halo_rows)
    spread(lambda y: halo2[0, y], 0)
    spread(lambda y: halo2[1, y], xl + 1)
    gather_rows(-1)

    mix(wb)

    across.wait_recv()
    ksum[...] = (kmine[...] + kother[...]) * (float(count * xl * ny * nz) ** -0.5)
    kall[pl.ds(inner * rows, rows)] = ksum[...]

    def piece_of(p):
        return kall.at[pl.ds(p * rows, rows)]

    def kspread(p):
        return push(ksum, piece_of(inner), ksend.at[1, p], krecv.at[1, inner], side * half + p)

    def kcollect(p):
        return push(ksum, piece_of(p), ksend.at[1, p], krecv.at[1, p], side * half + p)

    near(lambda p: kspread(p).start())

    def finish(y, planes):
        for x in range(xl):
            total = local[y, :, x * nz : (x + 1) * nz] + planes[x].astype(f32)
            out[x, y] = total.astype(bf16)

    finish(me, [stage2[me, j] for j in range(xl)])

    def last(src):
        back2(src).wait_recv()
        finish(src, [spec2[src, j] for j in range(xl)])

    others(half, count, from_side, last)
    others(0, half, from_side, last)
    near(lambda p: kcollect(p).wait_recv())
    for t in range(pairs):
        kout[t] = kall[t * ch : (t + 1) * ch, 0:ch]
        kout[t + pairs] = kall[t * ch : (t + 1) * ch, ch : 2 * ch]

    when(me == half, lambda: low_cross().wait_send())
    when(me == low_edge, lambda: high_cross().wait_send())
    when(inside_low, lambda: low_copy(me - 1).wait_send())
    when(inside_high, lambda: high_copy(me + 1).wait_send())

    def row_sent(y):
        when(low_own(y), lambda: low_row(y, me - 1).wait_send())
        when(high_own(y), lambda: high_row(y, me + 1).wait_send())

    each(0, ny, row_sent)
    when(me < low_edge, lambda: low_relay().wait_send())
    when(me > half, lambda: high_relay().wait_send())
    across.wait_send()

    def near_sent(p):
        ksend_to(p).wait_send()
        kspread(p).wait_send()

    near(near_sent)

    def drain(peer):
        share1(peer).wait_send()
        give1(peer).wait_send()
        share2(peer).wait_send()
        give2(peer).wait_send()

    others(0, count, by_side, drain)


def fits_kernel(count, features, kernel_weight):
    xl, ny, ch, nz = features.shape
    cells = xl * ny * ch * nz
    tile_rows = kernel_weight.shape[0] * ch
    if ny != count or count % 4 or nz % 128 or ch % 64 or kernel_weight.shape[0] % 2:
        return False
    if tile_rows % (8 * count):
        return False
    return 80 * cells < 24 * 2**20


def fused_device(
    features,
    cotangent,
    wall_flags,
    mode_counts,
    offsets,
    point_weight,
    kernel_weight,
    lap_weight,
    spec_weight,
    bias,
):
    count = lax.axis_size("gx")
    if not fits_kernel(count, features, kernel_weight):
        return per_device(
            features,
            cotangent,
            wall_flags,
            mode_counts,
            offsets,
            point_weight,
            kernel_weight,
            lap_weight,
            spec_weight,
            bias,
        )
    xl, ny, ch, nz = features.shape
    modes, tiles = spec_weight.shape[0], kernel_weight.shape[0]
    half = count // 2
    rows = tiles * ch // (2 * half)
    f32, bf16 = jnp.float32, jnp.bfloat16
    dma = pltpu.SemaphoreType.DMA
    vmem = pl.BlockSpec(memory_space=pltpu.VMEM)
    hbm = pl.BlockSpec(memory_space=pltpu.HBM)
    field_grad, tile_grad = pl.pallas_call(
        functools.partial(fused_kernel, count),
        out_shape=(
            pltpu.VMEM(features.shape, bf16),
            pltpu.VMEM(kernel_weight.shape, f32),
        ),
        in_specs=[hbm, hbm, hbm, hbm, hbm, hbm, hbm, hbm, hbm, hbm, hbm],
        out_specs=(vmem, vmem),
        scratch_shapes=[
            pltpu.VMEM((xl, ny, ch, nz), bf16),
            pltpu.VMEM((xl, ny, ch, nz), bf16),
            pltpu.VMEM((xl, ny, nz), jnp.int32),
            pltpu.VMEM((1, ch), jnp.int32),
            pltpu.VMEM((1, ch), f32),
            pltpu.SMEM((3, tiles), jnp.int32),
            pltpu.SMEM((modes, count * xl), f32),
            pltpu.VMEM((2 + tiles, ch, ch), bf16),
            pltpu.VMEM((modes, ch, ch), bf16),
            pltpu.VMEM((modes, ch, ch), bf16),
            pltpu.VMEM((ch, (2 + tiles) * ch), bf16),
            pltpu.VMEM((ch, (2 + tiles) * ch), bf16),
            pltpu.VMEM((ch, nz), f32),
            pltpu.VMEM((ch, nz), f32),
            pltpu.VMEM((2 * RAD + 1, xl + 2, ny + 2 * RAD, ch, nz), bf16),
            pltpu.VMEM((ny, (2 + tiles) * ch, xl * nz), bf16),
            pltpu.VMEM((ny, ch, xl * nz), f32),
            pltpu.VMEM((modes, ch, nz), f32),
            pltpu.VMEM((modes, ch, nz), f32),
            pltpu.VMEM((count, xl, ch, nz), bf16),
            pltpu.VMEM((count, xl, ch, nz), bf16),
            pltpu.VMEM((count, xl, ch, nz), bf16),
            pltpu.VMEM((count, xl, ch, nz), bf16),
            pltpu.VMEM((count, xl, ch, nz), bf16),
            pltpu.VMEM((count, xl, ch, nz), bf16),
            pltpu.VMEM((ny, xl, ch, nz), bf16),
            pltpu.VMEM((2, ny, ch, nz), bf16),
            pltpu.VMEM((2, ny, ch, nz), bf16),
            pltpu.VMEM((tiles * ch, ch), f32),
            pltpu.VMEM((tiles * ch // 2, 2 * ch), f32),
            pltpu.VMEM((half, rows, 2 * ch), f32),
            pltpu.VMEM((rows, 2 * ch), f32),
            pltpu.VMEM((rows, 2 * ch), f32),
            pltpu.VMEM((rows, 2 * ch), f32),
            pltpu.VMEM((tiles * ch // 2, 2 * ch), f32),
            pltpu.VMEM((nz, 2 * RAD * nz), bf16),
            dma((4, count)),
            dma((4, count)),
            dma((2,)),
            dma((2,)),
            dma((2, ny)),
            dma((2, ny)),
            dma((2, half)),
            dma((2, half)),
            dma((1,)),
            dma((1,)),
            dma((1,)),
            dma((ny,)),
            dma((11,)),
        ],
        compiler_params=pltpu.CompilerParams(
            collective_id=0, has_side_effects=True, vmem_limit_bytes=56 * 2**20
        ),
    )(
        features,
        cotangent,
        wall_flags,
        mode_counts.reshape(1, ch),
        offsets.T,
        basis_constant(modes, count * xl),
        point_weight,
        kernel_weight,
        lap_weight,
        spec_weight,
        bias.reshape(1, ch),
    )
    return field_grad, tile_grad


def solution(mesh):
    return jax.shard_map(
        fused_device,
        mesh=mesh,
        in_specs=(
            P(("groups", "gx"), None, None, None),
            P(("groups", "gx"), None, None, None),
            P(("groups", "gx"), None, None),
            P(),
            P(),
            P(),
            P(),
            P(),
            P(),
            P(),
        ),
        out_specs=(P(("groups", "gx"), None, None, None), P("groups", None, None)),
        check_vma=False,
    )
```

```python
import functools
from functools import partial
import math

import jax
import ml_dtypes
import numpy as np
import jax.numpy as jnp
from jax import lax
from jax.experimental import pallas as pl
from jax.experimental.pallas import tpu as pltpu
from jax.sharding import PartitionSpec as P

RAD = 2
MESH = pl.DeviceIdType.MESH


def with_halo(cells, sides, width):
    for axis, dim in sides:
        count = lax.axis_size(axis)
        ends = count - 1
        head = lax.slice_in_dim(cells, 0, width, axis=dim)
        tail = lax.slice_in_dim(cells, cells.shape[dim] - width, cells.shape[dim], axis=dim)
        cells = jnp.concatenate(
            [
                lax.ppermute(tail, axis, [(i, (i + 1) % count) for i in range(ends)]),
                cells,
                lax.ppermute(head, axis, [((i + 1) % count, i) for i in range(ends)]),
            ],
            axis=dim,
        )
    return cells


def basis_table(mode_total, length):
    mode_index = jnp.arange(mode_total, dtype=jnp.float32)[:, None]
    cell_index = jnp.arange(length, dtype=jnp.float32)[None, :]
    phase_angle = math.pi / (2.0 * length) * mode_index * (2.0 * cell_index + 1.0)
    amplitude = jnp.where(mode_index == 0.0, math.sqrt(1.0 / length), math.sqrt(2.0 / length))
    return (amplitude * jnp.cos(phase_angle)).astype(jnp.bfloat16)


def basis_constant(mode_total, length):
    mode_index = np.arange(mode_total, dtype=np.float64)[:, None]
    cell_index = np.arange(length, dtype=np.float64)[None, :]
    phase_angle = math.pi / (2.0 * length) * mode_index * (2.0 * cell_index + 1.0)
    amplitude = np.where(mode_index == 0.0, math.sqrt(1.0 / length), math.sqrt(2.0 / length))
    table = (amplitude * np.cos(phase_angle)).astype(np.float32)
    return table.astype(ml_dtypes.bfloat16).astype(np.float32)


def pencil_work(pencil, spec_weight, kept_modes, adjoint):
    basis = basis_table(spec_weight.shape[0], pencil.shape[0])
    coefficients = jnp.einsum(
        "kx,xycz->kycz", basis, pencil, preferred_element_type=jnp.float32
    ).astype(jnp.bfloat16)
    if adjoint:
        masked = coefficients * kept_modes[:, None, :, None].astype(jnp.bfloat16)
        mixed_modes = jnp.einsum(
            "koc,kyoz->kycz", spec_weight, masked, preferred_element_type=jnp.float32
        ).astype(jnp.bfloat16)
    else:
        mixed_modes = jnp.einsum(
            "koc,kycz->kyoz", spec_weight, coefficients, preferred_element_type=jnp.float32
        )
        mixed_modes = (mixed_modes * kept_modes[:, None, :, None]).astype(jnp.bfloat16)
    return jnp.einsum(
        "kx,kyoz->xyoz", basis, mixed_modes, preferred_element_type=jnp.float32
    ).astype(jnp.bfloat16)


def spectral(slab, spec_weight, kept_modes, adjoint):
    result = pencil_work(
        lax.all_to_all(slab, "gx", split_axis=1, concat_axis=0, tiled=True),
        spec_weight,
        kept_modes,
        adjoint,
    )
    return lax.all_to_all(result, "gx", split_axis=0, concat_axis=1, tiled=True)


def laplace_ext(extended):
    padded = jnp.pad(extended, ((0, 0), (1, 1), (0, 0), (1, 1))).astype(jnp.float32)
    centre_cells = padded[1:-1, 1:-1, :, 1:-1]
    neighbours = padded[2:, 1:-1, :, 1:-1] + padded[:-2, 1:-1, :, 1:-1]
    neighbours = neighbours + padded[1:-1, 2:, :, 1:-1] + padded[1:-1, :-2, :, 1:-1]
    neighbours = neighbours + padded[1:-1, 1:-1, :, 2:] + padded[1:-1, 1:-1, :, :-2]
    return (neighbours - 6.0 * centre_cells).astype(jnp.bfloat16)


def pad_sides(extended):
    return jnp.pad(extended, ((0, 0), (RAD, RAD), (0, 0), (RAD, RAD)))


def window_of(padded, offset, direction, slab_shape):
    starts = (
        1 + direction * offset[0],
        RAD + direction * offset[1],
        0,
        RAD + direction * offset[2],
    )
    return lax.dynamic_slice(padded, starts, slab_shape)


def gelu_slope(preact, upstream):
    _, pullback = jax.vjp(partial(jax.nn.gelu, approximate=True), preact)
    return pullback(upstream)[0]


def sum_over_gx(terms):
    count = lax.axis_size("gx")
    if terms.size % count:
        return lax.psum(terms, "gx")
    pieces = lax.all_to_all(terms.reshape(count, -1), "gx", split_axis=0, concat_axis=0, tiled=True)
    mine = jnp.sum(pieces, axis=0)
    copies = jnp.broadcast_to(mine[None, :], pieces.shape)
    gathered = lax.all_to_all(copies, "gx", split_axis=0, concat_axis=0, tiled=True)
    return gathered.reshape(terms.shape)


def per_device(
    features,
    cotangent,
    wall_flags,
    mode_counts,
    offsets,
    point_weight,
    kernel_weight,
    lap_weight,
    spec_weight,
    bias,
):
    mode_total = spec_weight.shape[0]
    tile_total = kernel_weight.shape[0]
    kept_modes = (jnp.arange(mode_total, dtype=jnp.int32)[:, None] < mode_counts[None, :]).astype(
        jnp.float32
    )
    fluid_mask = (1 - wall_flags).astype(jnp.float32)[:, :, None, :]
    extended = with_halo(features, (("gx", 0),), 1)
    padded_field = pad_sides(extended)
    local_part = jnp.einsum(
        "oc,xycz->xyoz", point_weight, features, preferred_element_type=jnp.float32
    )
    local_part = local_part + jnp.einsum(
        "oc,xycz->xyoz", lap_weight, laplace_ext(extended), preferred_element_type=jnp.float32
    )
    for tile in range(tile_total):
        moved = window_of(padded_field, offsets[tile], 1, features.shape)
        local_part = local_part + jnp.einsum(
            "oc,xycz->xyoz", kernel_weight[tile], moved, preferred_element_type=jnp.float32
        )
    local_part = local_part + bias[:, None]
    spectral_part = spectral(features, spec_weight, kept_modes, False)
    preact = local_part + spectral_part.astype(jnp.float32)
    weighted = (gelu_slope(preact, cotangent.astype(jnp.float32)) * fluid_mask).astype(jnp.bfloat16)
    spec_grad = spectral(weighted, spec_weight, kept_modes, True)
    ext_grad = with_halo(weighted, (("gx", 0),), 1)
    padded_grad = pad_sides(ext_grad)
    input_grad = jnp.einsum(
        "oc,xyoz->xycz", point_weight, weighted, preferred_element_type=jnp.float32
    )
    input_grad = input_grad + jnp.einsum(
        "oc,xyoz->xycz", lap_weight, laplace_ext(ext_grad), preferred_element_type=jnp.float32
    )
    input_grad = input_grad + spec_grad.astype(jnp.float32)
    tile_grads = []
    for tile in range(tile_total):
        back_moved = window_of(padded_grad, offsets[tile], -1, weighted.shape)
        input_grad = input_grad + jnp.einsum(
            "oc,xyoz->xycz", kernel_weight[tile], back_moved, preferred_element_type=jnp.float32
        )
        tile_grads.append(
            jnp.einsum("xyoz,xycz->oc", back_moved, features, preferred_element_type=jnp.float32)
        )
    local_grad = jnp.stack(tile_grads, axis=0)
    scaling = float(
        lax.axis_size("gx") * features.shape[0] * features.shape[1] * features.shape[3]
    ) ** (-0.5)
    summed = sum_over_gx(local_grad)
    return (input_grad.astype(jnp.bfloat16), summed * scaling)


def fused_kernel(
    count,
    feat_in,
    cot_in,
    wall_in,
    mode_in,
    offs_in,
    basis_in,
    point_in,
    tile_in,
    lap_in,
    spec_in,
    bias_in,
    out,
    kout,
    feat,
    cot,
    wall,
    mode_row,
    bias_row,
    offs,
    basis,
    wst,
    wm,
    wmt,
    wf,
    wb,
    mode,
    bias,
    zs,
    cat,
    local,
    acc,
    vh,
    pen1,
    pen2,
    stage1,
    stage2,
    spec1,
    spec2,
    wgt,
    halo1,
    halo2,
    rel1,
    rel2,
    kacc,
    kdense,
    kpart,
    kmine,
    kother,
    ksum,
    kall,
    shift,
    send,
    recv,
    hsend,
    hrecv,
    vsend,
    vrecv,
    rsend,
    rrecv,
    ksend,
    krecv,
    xsend,
    xrecv,
    fsend,
    frecv,
    load,
):
    me = lax.axis_index("gx")
    grp = lax.axis_index("groups")
    xl, ny, ch, nz = feat.shape
    modes = wm.shape[0]
    tiles = offs.shape[1]
    half = count // 2
    quads = half // 2
    f32, bf16 = jnp.float32, jnp.bfloat16
    side = me // half
    inner = me % half
    chip = inner // 2

    def push(src, dst, ssem, rsem, peer):
        return pltpu.make_async_remote_copy(
            src_ref=src,
            dst_ref=dst,
            send_sem=ssem,
            recv_sem=rsem,
            device_id=(grp, peer),
            device_id_type=MESH,
        )

    def each(low, high, body):
        def step(i, carry):
            body(i)
            return carry

        lax.fori_loop(low, high, step, 0)

    def place(cross, turn, core):
        return ((side + cross) % 2) * half + ((chip + turn) % quads) * 2 + core

    def by_core(j):
        core = j // half
        rest = j % half
        return place(1 - rest // quads, rest % quads, core)

    def by_side(j):
        rest = j % half
        return place(1 - j // half, rest // 2, rest % 2)

    def from_side(j):
        rest = j % half
        return place(1 - j // half, quads - rest // 2, rest % 2)

    def from_core(j):
        core = j // half
        rest = j % half
        return place(1 - rest // quads, quads - rest % quads, core)

    def others(low, high, order, body):
        def visit(j):
            peer = order(j)

            @pl.when(peer != me)
            def _():
                body(peer)

        each(low, high, visit)

    def share1(peer):
        return push(
            feat.at[:, peer], pen1.at[me], send.at[0, peer], recv.at[0, me], peer
        )

    def land1(src):
        return push(feat.at[:, src], pen1.at[src], send.at[0, src], recv.at[0, src], src)

    def give1(peer):
        return push(stage1.at[peer], spec1.at[me], send.at[1, peer], recv.at[1, me], peer)

    def back1(src):
        return push(stage1.at[src], spec1.at[src], send.at[1, src], recv.at[1, src], src)

    def share2(peer):
        return push(wgt.at[peer], pen2.at[me], send.at[2, peer], recv.at[2, me], peer)

    def land2(src):
        return push(wgt.at[src], pen2.at[src], send.at[2, src], recv.at[2, src], src)

    def give2(peer):
        return push(stage2.at[peer], spec2.at[me], send.at[3, peer], recv.at[3, me], peer)

    def back2(src):
        return push(stage2.at[src], spec2.at[src], send.at[3, src], recv.at[3, src], src)

    loads = [
        pltpu.make_async_copy(feat_in, feat, load.at[0]),
        pltpu.make_async_copy(point_in, wst.at[0], load.at[1]),
        pltpu.make_async_copy(lap_in, wst.at[1], load.at[2]),
        pltpu.make_async_copy(tile_in, wst.at[pl.ds(2, tiles)], load.at[3]),
        pltpu.make_async_copy(spec_in, wm, load.at[4]),
        pltpu.make_async_copy(mode_in, mode_row, load.at[5]),
        pltpu.make_async_copy(bias_in, bias_row, load.at[6]),
        pltpu.make_async_copy(wall_in, wall, load.at[7]),
        pltpu.make_async_copy(cot_in, cot, load.at[8]),
        pltpu.make_async_copy(offs_in, offs, load.at[9]),
        pltpu.make_async_copy(basis_in, basis, load.at[10]),
    ]
    barrier = pltpu.get_barrier_semaphore()
    each(
        1,
        count,
        lambda d: pl.semaphore_signal(
            barrier, inc=1, device_id=(grp, lax.rem(me + d, count)), device_id_type=MESH
        ),
    )
    for piece in loads:
        piece.start()

    pl.semaphore_wait(barrier, count - 1)
    loads[0].wait()

    low_edge = half - 1
    via = rel1.shape[0]
    up_relay = low_edge - 2
    down_relay = half + 2

    def low_copy(peer):
        return push(feat.at[0], halo1.at[1], hsend.at[0], hrecv.at[0], peer)

    def high_copy(peer):
        return push(feat.at[xl - 1], halo1.at[0], hsend.at[1], hrecv.at[1], peer)

    def low_cross():
        part = pl.ds(half - 1 + via, half + 1 - via)
        return push(feat.at[0, part], halo1.at[1, part], hsend.at[0], hrecv.at[0], low_edge)

    def high_cross():
        part = pl.ds(0, half + 1 - via)
        return push(feat.at[xl - 1, part], halo1.at[0, part], hsend.at[1], hrecv.at[1], half)

    def up_first(peer):
        part = pl.ds(half + 1 - via, via)
        return push(feat.at[xl - 1, part], rel1, hsend.at[2], hrecv.at[2], peer)

    def down_first(peer):
        return push(feat.at[0, pl.ds(half - 1, via)], rel1, hsend.at[2], hrecv.at[2], peer)

    def up_second(peer):
        part = pl.ds(half + 1 - via, via)
        return push(rel1, halo1.at[0, part], hsend.at[3], hrecv.at[3], peer)

    def down_second(peer):
        part = pl.ds(half - 1, via)
        return push(rel1, halo1.at[1, part], hsend.at[3], hrecv.at[3], peer)

    def low_pass():
        return push(pen1.at[half, 0], halo1.at[1, me], fsend.at[0], frecv.at[me], low_edge)

    def high_pass():
        return push(
            pen1.at[low_edge, xl - 1], halo1.at[0, me], fsend.at[0], frecv.at[me], half
        )

    def low_row(y, peer):
        return push(wgt.at[y, 0], halo2.at[1, y], rsend.at[0, y], rrecv.at[0, y], peer)

    def high_row(y, peer):
        return push(wgt.at[y, xl - 1], halo2.at[0, y], rsend.at[1, y], rrecv.at[1, y], peer)

    def low_relay():
        return push(
            pen2.at[half, 0], halo2.at[1, me], fsend.at[0], rrecv.at[0, me], low_edge
        )

    def high_relay():
        return push(
            pen2.at[low_edge, xl - 1], halo2.at[0, me], fsend.at[0], rrecv.at[1, me], half
        )

    def low_detour(y, peer):
        slot = y - (half - 1)
        return push(wgt.at[y, 0], rel2.at[slot], rsend.at[0, y], vrecv.at[slot], peer)

    def high_detour(y, peer):
        slot = y - (half + 1 - via)
        return push(wgt.at[y, xl - 1], rel2.at[slot], rsend.at[1, y], vrecv.at[slot], peer)

    def low_onward(slot, peer):
        y = slot + half - 1
        return push(rel2.at[slot], halo2.at[1, y], vsend.at[slot], rrecv.at[0, y], peer)

    def high_onward(slot, peer):
        y = slot + half + 1 - via
        return push(rel2.at[slot], halo2.at[0, y], vsend.at[slot], rrecv.at[1, y], peer)

    def low_turned(y):
        return (me == half) & (y >= low_edge) & (y < low_edge + via)

    def high_turned(y):
        return (me == low_edge) & (y > half - via) & (y <= half)

    def low_straight(y):
        return (me > 0) & ((me != half) | (y >= low_edge + via))

    def high_straight(y):
        return (me < count - 1) & ((me != low_edge) | (y <= half - via))

    def low_own(y):
        return (me > 0) & ((me != half) | (y >= low_edge))

    def high_own(y):
        return (me < count - 1) & ((me != low_edge) | (y <= half))

    def when(cond, body):
        @pl.when(cond)
        def _():
            body()

    inside_low = (me > 0) & (me != half)
    inside_high = (me < count - 1) & (me != low_edge)
    others(0, half, by_core, lambda peer: share1(peer).start())
    when(me == half, lambda: low_cross().start())
    when(me == low_edge, lambda: high_cross().start())
    when(me == half, lambda: down_first(down_relay).start())
    when(me == low_edge, lambda: up_first(up_relay).start())
    when(inside_low, lambda: low_copy(me - 1).start())
    when(inside_high, lambda: high_copy(me + 1).start())
    others(half, count, by_core, lambda peer: share1(peer).start())

    from_z = lax.broadcasted_iota(jnp.int32, (nz, nz), 0)
    to_z = lax.broadcasted_iota(jnp.int32, (nz, nz), 1)
    for m, dz in enumerate([dz for dz in range(-RAD, RAD + 1) if dz]):
        shift[:, m * nz : (m + 1) * nz] = jnp.where(from_z == to_z + dz, 1.0, 0.0).astype(bf16)

    @pl.when(me == 0)
    def _():
        halo1[0] = jnp.zeros(halo1.shape[1:], bf16)
        halo2[0] = jnp.zeros(halo2.shape[1:], bf16)

    @pl.when(me == count - 1)
    def _():
        halo1[1] = jnp.zeros(halo1.shape[1:], bf16)
        halo2[1] = jnp.zeros(halo2.shape[1:], bf16)

    for edge in (0, RAD + ny):
        for dz in range(2 * RAD + 1):
            for x in range(xl + 2):
                zs[dz, x, edge : edge + RAD] = jnp.zeros((RAD, ch, nz), bf16)

    moves = [dz for dz in range(-RAD, RAD + 1) if dz]
    group = math.gcd(ny, 8)

    def spread(take, place_x):
        def body(i):
            y = i * group
            v = take(pl.ds(y, group))
            zs[RAD, place_x, pl.ds(y + RAD, group)] = v
            flat = v.reshape(group * ch, nz)
            moved = jnp.dot(flat, shift[...], preferred_element_type=f32).astype(bf16)
            for m, dz in enumerate(moves):
                piece = moved[:, m * nz : (m + 1) * nz].reshape(group, ch, nz)
                zs[RAD + dz, place_x, pl.ds(y + RAD, group)] = piece

        each(0, ny // group, body)

    def gather_rows(direction):
        def body(y):
            for x in range(xl):
                lanes = slice(x * nz, (x + 1) * nz)
                centre = zs[RAD, x + 1, y + RAD]
                cat[y, 0:ch, lanes] = centre
                total = zs[RAD, x + 2, y + RAD].astype(f32) + zs[RAD, x, y + RAD].astype(f32)
                total = total + zs[RAD, x + 1, y + RAD + 1].astype(f32)
                total = total + zs[RAD, x + 1, y + RAD - 1].astype(f32)
                total = total + zs[RAD + 1, x + 1, y + RAD].astype(f32)
                total = total + zs[RAD - 1, x + 1, y + RAD].astype(f32)
                cat[y, ch : 2 * ch, lanes] = (total - 6.0 * centre.astype(f32)).astype(bf16)
                for t in range(tiles):
                    moved = zs[
                        RAD + direction * offs[2, t],
                        x + 1 + direction * offs[0, t],
                        y + RAD + direction * offs[1, t],
                    ]
                    cat[y, (2 + t) * ch : (3 + t) * ch, lanes] = moved

        each(0, ny, body)

    unroll = math.gcd(ny, 4)

    def each_row(body):
        def rows_at(i):
            for r in range(unroll):
                body(i * unroll + r)

        each(0, ny // unroll, rows_at)

    def mix(weights):
        def body(y):
            local[y] = jnp.dot(weights[...], cat[y], preferred_element_type=f32)

        each_row(body)

    def gain(planes, src):
        wide = [p.astype(f32) for p in planes]
        for k in range(modes):
            total = acc[k]
            for j in range(xl):
                total = total + basis[k, src * xl + j] * wide[j]
            acc[k] = total

    def forward_mix():
        for k in range(modes):
            v = jnp.dot(wm[k], acc[k].astype(bf16), preferred_element_type=f32)
            v = jnp.where(mode[...] > float(k), v, 0.0)
            vh[k] = v.astype(bf16).astype(f32)

    def backward_mix():
        for k in range(modes):
            u = jnp.where(mode[...] > float(k), acc[k], 0.0).astype(bf16)
            v = jnp.dot(wmt[k], u, preferred_element_type=f32)
            vh[k] = v.astype(bf16).astype(f32)

    def expand(stage, peer):
        for j in range(xl):
            total = basis[0, peer * xl + j] * vh[0]
            for k in range(1, modes):
                total = total + basis[k, peer * xl + j] * vh[k]
            stage[peer, j] = total.astype(bf16)

    for x in range(xl):
        spread(lambda y: feat[x, y], x + 1)
    for piece in loads[1:]:
        piece.wait()

    row_at = lax.broadcasted_iota(jnp.int32, (ch, ch), 0)
    col_at = lax.broadcasted_iota(jnp.int32, (ch, ch), 1)
    diagonal = row_at == col_at
    unit = jnp.where(diagonal, 1.0, 0.0).astype(bf16)

    def upright(row):
        spread_out = jnp.where(diagonal, jnp.broadcast_to(row, (ch, ch)), 0.0)
        column = jnp.sum(spread_out, axis=1, keepdims=True)
        return jnp.broadcast_to(column, (ch, nz))

    mode[...] = upright(mode_row[...].astype(f32))
    bias[...] = upright(bias_row[...])

    def flipped(block):
        return lax.dot_general(
            block, unit, (((0,), (0,)), ((), ())), preferred_element_type=f32
        ).astype(bf16)

    for t in range(2 + tiles):
        wf[:, t * ch : (t + 1) * ch] = wst[t]
        wb[:, t * ch : (t + 1) * ch] = flipped(wst[t])

    def flip_mode(k):
        wmt[k] = flipped(wm[k])

    each(0, modes, flip_mode)

    def passed_low(i):
        push(
            pen1.at[low_edge, xl - 1], halo1.at[0, i], fsend.at[0], frecv.at[i], low_edge
        ).wait_recv()

    def passed_high(i):
        push(pen1.at[half, 0], halo1.at[1, i], fsend.at[0], frecv.at[i], half).wait_recv()

    def forward_stencil():
        when(inside_low, lambda: high_copy(me - 1).wait_recv())
        when(inside_high, lambda: low_copy(me + 1).wait_recv())

        @pl.when(me == half)
        def _():
            high_cross_here = push(
                feat.at[xl - 1, pl.ds(0, half + 1 - via)],
                halo1.at[0, pl.ds(0, half + 1 - via)],
                hsend.at[1],
                hrecv.at[1],
                low_edge,
            )
            high_cross_here.wait_recv()
            up_second(up_relay).wait_recv()
            each(half + 1, count, passed_low)

        @pl.when(me == low_edge)
        def _():
            low_cross_here = push(
                feat.at[0, pl.ds(half - 1 + via, half + 1 - via)],
                halo1.at[1, pl.ds(half - 1 + via, half + 1 - via)],
                hsend.at[0],
                hrecv.at[0],
                half,
            )
            low_cross_here.wait_recv()
            down_second(down_relay).wait_recv()
            each(0, half - 1, passed_high)

        spread(lambda y: halo1[0, y], 0)
        spread(lambda y: halo1[1, y], xl + 1)
        gather_rows(1)
        mix(wf)

    core = me % 2

    @pl.when(me == up_relay)
    def _():
        up_first(low_edge).wait_recv()
        up_second(half).start()

    @pl.when(me == down_relay)
    def _():
        down_first(half).wait_recv()
        down_second(low_edge).start()

    early = (core == 1) & (me != low_edge)
    when(early, forward_stencil)

    acc[...] = jnp.zeros(acc.shape, f32)
    gain([feat[j, me] for j in range(xl)], me)

    def take1(src):
        land1(src).wait_recv()
        when((src == half) & (me < low_edge), lambda: low_pass().start())
        when((src == low_edge) & (me > half), lambda: high_pass().start())
        gain([pen1[src, j] for j in range(xl)], src)

    others(0, count, from_side, take1)
    forward_mix()

    def hand1(peer):
        expand(stage1, peer)
        give1(peer).start()

    others(0, count, by_core, hand1)
    expand(stage1, me)
    when(jnp.logical_not(early), forward_stencil)
    root = math.sqrt(2.0 / math.pi)

    def slope(y, planes):
        for x in range(xl):
            v = local[y, :, x * nz : (x + 1) * nz] + planes[x].astype(f32) + bias[...]
            square = v * v
            t = jnp.tanh(root * (v + 0.044715 * (square * v)))
            g = 0.5 * (1.0 + t)
            g = g + (0.5 * v) * ((1.0 - t * t) * (root * (1.0 + (3.0 * 0.044715) * square)))
            fluid = (1 - wall[x, pl.ds(y, 1), :]).astype(f32)
            wgt[y, x] = ((cot[x, y].astype(f32) * g) * fluid).astype(bf16)
        when(low_straight(y), lambda: low_row(y, me - 1).start())
        when(high_straight(y), lambda: high_row(y, me + 1).start())
        when(low_turned(y), lambda: low_detour(y, down_relay).start())
        when(high_turned(y), lambda: high_detour(y, up_relay).start())

    kacc[...] = jnp.zeros(kacc.shape, f32)

    def row_work(y):
        planes = jnp.concatenate([wgt[y, x] for x in range(xl)], axis=1)
        kacc[...] += lax.dot_general(
            cat[y, 2 * ch :, :], planes, (((1,), (1,)), ((), ())), preferred_element_type=f32
        )
        flat = jnp.concatenate([wgt[y, x] for x in range(xl)], axis=0)
        moved = jnp.dot(flat, shift[...], preferred_element_type=f32).astype(bf16)
        for x in range(xl):
            zs[RAD, x + 1, y + RAD] = wgt[y, x]
            for m, dz in enumerate(moves):
                piece = moved[x * ch : (x + 1) * ch, m * nz : (m + 1) * nz]
                zs[RAD + dz, x + 1, y + RAD] = piece

    slope(me, [stage1[me, j] for j in range(xl)])
    row_work(me)

    def turn(src):
        back1(src).wait_recv()
        slope(src, [spec1[src, j] for j in range(xl)])
        share2(src).start()
        row_work(src)

    others(0, count, by_core, turn)

    pairs = tiles // 2
    for t in range(pairs):
        kdense[t * ch : (t + 1) * ch] = jnp.concatenate(
            [
                jnp.transpose(kacc[p * ch : (p + 1) * ch])
                for p in (t, t + pairs)
            ],
            axis=1,
        )

    rows = kpart.shape[1]

    def strip(p):
        return kdense.at[pl.ds(p * rows, rows)]

    def near(body):
        def visit(d):
            body((inner + d) % half)

        each(1, half, visit)

    def ksend_to(p):
        return push(
            strip(p), kpart.at[inner], ksend.at[0, p], krecv.at[0, inner], side * half + p
        )

    def kland(p):
        return push(strip(p), kpart.at[p], ksend.at[0, p], krecv.at[0, p], side * half + p)

    near(lambda p: ksend_to(p).start())
    def pass_up(slot):
        high_detour(slot + half + 1 - via, low_edge).wait_recv()
        high_onward(slot, half).start()

    def pass_down(slot):
        low_detour(slot + half - 1, half).wait_recv()
        low_onward(slot, low_edge).start()

    when(me == up_relay, lambda: each(0, via, pass_up))
    when(me == down_relay, lambda: each(0, via, pass_down))

    acc[...] = jnp.zeros(acc.shape, f32)
    gain([wgt[me, j] for j in range(xl)], me)

    def take2(src):
        land2(src).wait_recv()
        when((src == half) & (me < low_edge), lambda: low_relay().start())
        when((src == low_edge) & (me > half), lambda: high_relay().start())
        gain([pen2[src, j] for j in range(xl)], src)

    when(me < low_edge, lambda: low_pass().wait_send())
    when(me > half, lambda: high_pass().wait_send())
    others(0, count, from_side, take2)
    backward_mix()

    def hand2(peer):
        expand(stage2, peer)
        give2(peer).start()

    others(0, quads, by_core, hand2)
    kpart[inner] = kdense[pl.ds(inner * rows, rows)]
    near(lambda p: kland(p).wait_recv())
    part_sum = kpart[0]
    for p in range(1, half):
        part_sum = part_sum + kpart[p]
    kmine[...] = part_sum
    partner = ((side + 1) % 2) * half + inner
    across = push(kmine, kother, xsend.at[0], xrecv.at[0], partner)
    across.start()
    others(quads, count, by_core, hand2)
    expand(stage2, me)

    def halo_rows(y):
        when(me > 0, lambda: high_row(y, me - 1).wait_recv())
        when(me < count - 1, lambda: low_row(y, me + 1).wait_recv())

    each(0, ny, halo_rows)
    spread(lambda y: halo2[0, y], 0)
    spread(lambda y: halo2[1, y], xl + 1)
    gather_rows(-1)

    mix(wb)

    across.wait_recv()
    ksum[...] = (kmine[...] + kother[...]) * (float(count * xl * ny * nz) ** -0.5)
    kall[pl.ds(inner * rows, rows)] = ksum[...]

    def piece_of(p):
        return kall.at[pl.ds(p * rows, rows)]

    def kspread(p):
        return push(ksum, piece_of(inner), ksend.at[1, p], krecv.at[1, inner], side * half + p)

    def kcollect(p):
        return push(ksum, piece_of(p), ksend.at[1, p], krecv.at[1, p], side * half + p)

    near(lambda p: kspread(p).start())

    def finish(y, planes):
        for x in range(xl):
            total = local[y, :, x * nz : (x + 1) * nz] + planes[x].astype(f32)
            out[x, y] = total.astype(bf16)

    finish(me, [stage2[me, j] for j in range(xl)])

    def last(src):
        back2(src).wait_recv()
        finish(src, [spec2[src, j] for j in range(xl)])

    others(half, count, from_side, last)
    others(0, half, from_side, last)
    near(lambda p: kcollect(p).wait_recv())
    for t in range(pairs):
        kout[t] = kall[t * ch : (t + 1) * ch, 0:ch]
        kout[t + pairs] = kall[t * ch : (t + 1) * ch, ch : 2 * ch]

    when(me == half, lambda: low_cross().wait_send())
    when(me == low_edge, lambda: high_cross().wait_send())
    when(me == half, lambda: down_first(down_relay).wait_send())
    when(me == low_edge, lambda: up_first(up_relay).wait_send())
    when(me == up_relay, lambda: up_second(half).wait_send())
    when(me == down_relay, lambda: down_second(low_edge).wait_send())
    when(me == up_relay, lambda: each(0, via, lambda i: high_onward(i, half).wait_send()))
    when(me == down_relay, lambda: each(0, via, lambda i: low_onward(i, low_edge).wait_send()))
    when(inside_low, lambda: low_copy(me - 1).wait_send())
    when(inside_high, lambda: high_copy(me + 1).wait_send())

    def row_sent(y):
        when(low_own(y), lambda: low_row(y, me - 1).wait_send())
        when(high_own(y), lambda: high_row(y, me + 1).wait_send())

    each(0, ny, row_sent)
    when(me < low_edge, lambda: low_relay().wait_send())
    when(me > half, lambda: high_relay().wait_send())
    across.wait_send()

    def near_sent(p):
        ksend_to(p).wait_send()
        kspread(p).wait_send()

    near(near_sent)

    def drain(peer):
        share1(peer).wait_send()
        give1(peer).wait_send()
        share2(peer).wait_send()
        give2(peer).wait_send()

    others(0, count, by_side, drain)


def flush_kernel(field, tile, field_out, tile_out, sems):
    first = pltpu.make_async_copy(field, field_out, sems.at[0])
    second = pltpu.make_async_copy(tile, tile_out, sems.at[1])
    first.start()
    second.start()
    first.wait()
    second.wait()


def fits_kernel(count, features, kernel_weight):
    xl, ny, ch, nz = features.shape
    cells = xl * ny * ch * nz
    tile_rows = kernel_weight.shape[0] * ch
    if ny != count or count % 4 or nz % 128 or ch % 64 or kernel_weight.shape[0] % 2:
        return False
    if tile_rows % (8 * count):
        return False
    return 80 * cells < 24 * 2**20


def fused_device(
    features,
    cotangent,
    wall_flags,
    mode_counts,
    offsets,
    point_weight,
    kernel_weight,
    lap_weight,
    spec_weight,
    bias,
):
    count = lax.axis_size("gx")
    if not fits_kernel(count, features, kernel_weight):
        return per_device(
            features,
            cotangent,
            wall_flags,
            mode_counts,
            offsets,
            point_weight,
            kernel_weight,
            lap_weight,
            spec_weight,
            bias,
        )
    xl, ny, ch, nz = features.shape
    modes, tiles = spec_weight.shape[0], kernel_weight.shape[0]
    half = count // 2
    rows = tiles * ch // (2 * half)
    f32, bf16 = jnp.float32, jnp.bfloat16
    dma = pltpu.SemaphoreType.DMA
    vmem = pl.BlockSpec(memory_space=pltpu.VMEM)
    hbm = pl.BlockSpec(memory_space=pltpu.HBM)
    field_grad, tile_grad = pl.pallas_call(
        functools.partial(fused_kernel, count),
        out_shape=(
            pltpu.VMEM(features.shape, bf16),
            pltpu.VMEM(kernel_weight.shape, f32),
        ),
        in_specs=[hbm, hbm, hbm, hbm, hbm, hbm, hbm, hbm, hbm, hbm, hbm],
        out_specs=(vmem, vmem),
        scratch_shapes=[
            pltpu.VMEM((xl, ny, ch, nz), bf16),
            pltpu.VMEM((xl, ny, ch, nz), bf16),
            pltpu.VMEM((xl, ny, nz), jnp.int32),
            pltpu.VMEM((1, ch), jnp.int32),
            pltpu.VMEM((1, ch), f32),
            pltpu.SMEM((3, tiles), jnp.int32),
            pltpu.SMEM((modes, count * xl), f32),
            pltpu.VMEM((2 + tiles, ch, ch), bf16),
            pltpu.VMEM((modes, ch, ch), bf16),
            pltpu.VMEM((modes, ch, ch), bf16),
            pltpu.VMEM((ch, (2 + tiles) * ch), bf16),
            pltpu.VMEM((ch, (2 + tiles) * ch), bf16),
            pltpu.VMEM((ch, nz), f32),
            pltpu.VMEM((ch, nz), f32),
            pltpu.VMEM((2 * RAD + 1, xl + 2, ny + 2 * RAD, ch, nz), bf16),
            pltpu.VMEM((ny, (2 + tiles) * ch, xl * nz), bf16),
            pltpu.VMEM((ny, ch, xl * nz), f32),
            pltpu.VMEM((modes, ch, nz), f32),
            pltpu.VMEM((modes, ch, nz), f32),
            pltpu.VMEM((count, xl, ch, nz), bf16),
            pltpu.VMEM((count, xl, ch, nz), bf16),
            pltpu.VMEM((count, xl, ch, nz), bf16),
            pltpu.VMEM((count, xl, ch, nz), bf16),
            pltpu.VMEM((count, xl, ch, nz), bf16),
            pltpu.VMEM((count, xl, ch, nz), bf16),
            pltpu.VMEM((ny, xl, ch, nz), bf16),
            pltpu.VMEM((2, ny, ch, nz), bf16),
            pltpu.VMEM((2, ny, ch, nz), bf16),
            pltpu.VMEM((half // 2, ch, nz), bf16),
            pltpu.VMEM((half // 2, ch, nz), bf16),
            pltpu.VMEM((tiles * ch, ch), f32),
            pltpu.VMEM((tiles * ch // 2, 2 * ch), f32),
            pltpu.VMEM((half, rows, 2 * ch), f32),
            pltpu.VMEM((rows, 2 * ch), f32),
            pltpu.VMEM((rows, 2 * ch), f32),
            pltpu.VMEM((rows, 2 * ch), f32),
            pltpu.VMEM((tiles * ch // 2, 2 * ch), f32),
            pltpu.VMEM((nz, 2 * RAD * nz), bf16),
            dma((4, count)),
            dma((4, count)),
            dma((4,)),
            dma((4,)),
            dma((half // 2,)),
            dma((half // 2,)),
            dma((2, ny)),
            dma((2, ny)),
            dma((2, half)),
            dma((2, half)),
            dma((1,)),
            dma((1,)),
            dma((1,)),
            dma((ny,)),
            dma((11,)),
        ],
        compiler_params=pltpu.CompilerParams(
            collective_id=0, has_side_effects=True, vmem_limit_bytes=56 * 2**20
        ),
    )(
        features,
        cotangent,
        wall_flags,
        mode_counts.reshape(1, ch),
        offsets.T,
        basis_constant(modes, count * xl),
        point_weight,
        kernel_weight,
        lap_weight,
        spec_weight,
        bias.reshape(1, ch),
    )
    field_grad, tile_grad = pl.pallas_call(
        flush_kernel,
        out_shape=(
            jax.ShapeDtypeStruct(features.shape, bf16),
            jax.ShapeDtypeStruct(kernel_weight.shape, f32),
        ),
        in_specs=[vmem] * 2,
        out_specs=(hbm,) * 2,
        scratch_shapes=[dma((2,))],
    )(
        pltpu.with_memory_space_constraint(field_grad, pltpu.VMEM),
        pltpu.with_memory_space_constraint(tile_grad, pltpu.VMEM),
    )
    return field_grad, tile_grad


def solution(mesh):
    return jax.shard_map(
        fused_device,
        mesh=mesh,
        in_specs=(
            P(("groups", "gx"), None, None, None),
            P(("groups", "gx"), None, None, None),
            P(("groups", "gx"), None, None),
            P(),
            P(),
            P(),
            P(),
            P(),
            P(),
            P(),
        ),
        out_specs=(P(("groups", "gx"), None, None, None), P("groups", None, None)),
        check_vma=False,
    )
```

```python
import functools
from functools import partial
import math

import jax
import ml_dtypes
import numpy as np
import jax.numpy as jnp
from jax import lax
from jax.experimental import pallas as pl
from jax.experimental.pallas import tpu as pltpu
from jax.sharding import PartitionSpec as P

RAD = 2
MESH = pl.DeviceIdType.MESH


def with_halo(cells, sides, width):
    for axis, dim in sides:
        count = lax.axis_size(axis)
        ends = count - 1
        head = lax.slice_in_dim(cells, 0, width, axis=dim)
        tail = lax.slice_in_dim(cells, cells.shape[dim] - width, cells.shape[dim], axis=dim)
        cells = jnp.concatenate(
            [
                lax.ppermute(tail, axis, [(i, (i + 1) % count) for i in range(ends)]),
                cells,
                lax.ppermute(head, axis, [((i + 1) % count, i) for i in range(ends)]),
            ],
            axis=dim,
        )
    return cells


def basis_table(mode_total, length):
    mode_index = jnp.arange(mode_total, dtype=jnp.float32)[:, None]
    cell_index = jnp.arange(length, dtype=jnp.float32)[None, :]
    phase_angle = math.pi / (2.0 * length) * mode_index * (2.0 * cell_index + 1.0)
    amplitude = jnp.where(mode_index == 0.0, math.sqrt(1.0 / length), math.sqrt(2.0 / length))
    return (amplitude * jnp.cos(phase_angle)).astype(jnp.bfloat16)


def basis_constant(mode_total, length):
    mode_index = np.arange(mode_total, dtype=np.float64)[:, None]
    cell_index = np.arange(length, dtype=np.float64)[None, :]
    phase_angle = math.pi / (2.0 * length) * mode_index * (2.0 * cell_index + 1.0)
    amplitude = np.where(mode_index == 0.0, math.sqrt(1.0 / length), math.sqrt(2.0 / length))
    table = (amplitude * np.cos(phase_angle)).astype(np.float32)
    return table.astype(ml_dtypes.bfloat16).astype(np.float32)


def pencil_work(pencil, spec_weight, kept_modes, adjoint):
    basis = basis_table(spec_weight.shape[0], pencil.shape[0])
    coefficients = jnp.einsum(
        "kx,xycz->kycz", basis, pencil, preferred_element_type=jnp.float32
    ).astype(jnp.bfloat16)
    if adjoint:
        masked = coefficients * kept_modes[:, None, :, None].astype(jnp.bfloat16)
        mixed_modes = jnp.einsum(
            "koc,kyoz->kycz", spec_weight, masked, preferred_element_type=jnp.float32
        ).astype(jnp.bfloat16)
    else:
        mixed_modes = jnp.einsum(
            "koc,kycz->kyoz", spec_weight, coefficients, preferred_element_type=jnp.float32
        )
        mixed_modes = (mixed_modes * kept_modes[:, None, :, None]).astype(jnp.bfloat16)
    return jnp.einsum(
        "kx,kyoz->xyoz", basis, mixed_modes, preferred_element_type=jnp.float32
    ).astype(jnp.bfloat16)


def spectral(slab, spec_weight, kept_modes, adjoint):
    result = pencil_work(
        lax.all_to_all(slab, "gx", split_axis=1, concat_axis=0, tiled=True),
        spec_weight,
        kept_modes,
        adjoint,
    )
    return lax.all_to_all(result, "gx", split_axis=0, concat_axis=1, tiled=True)


def laplace_ext(extended):
    padded = jnp.pad(extended, ((0, 0), (1, 1), (0, 0), (1, 1))).astype(jnp.float32)
    centre_cells = padded[1:-1, 1:-1, :, 1:-1]
    neighbours = padded[2:, 1:-1, :, 1:-1] + padded[:-2, 1:-1, :, 1:-1]
    neighbours = neighbours + padded[1:-1, 2:, :, 1:-1] + padded[1:-1, :-2, :, 1:-1]
    neighbours = neighbours + padded[1:-1, 1:-1, :, 2:] + padded[1:-1, 1:-1, :, :-2]
    return (neighbours - 6.0 * centre_cells).astype(jnp.bfloat16)


def pad_sides(extended):
    return jnp.pad(extended, ((0, 0), (RAD, RAD), (0, 0), (RAD, RAD)))


def window_of(padded, offset, direction, slab_shape):
    starts = (
        1 + direction * offset[0],
        RAD + direction * offset[1],
        0,
        RAD + direction * offset[2],
    )
    return lax.dynamic_slice(padded, starts, slab_shape)


def gelu_slope(preact, upstream):
    _, pullback = jax.vjp(partial(jax.nn.gelu, approximate=True), preact)
    return pullback(upstream)[0]


def sum_over_gx(terms):
    count = lax.axis_size("gx")
    if terms.size % count:
        return lax.psum(terms, "gx")
    pieces = lax.all_to_all(terms.reshape(count, -1), "gx", split_axis=0, concat_axis=0, tiled=True)
    mine = jnp.sum(pieces, axis=0)
    copies = jnp.broadcast_to(mine[None, :], pieces.shape)
    gathered = lax.all_to_all(copies, "gx", split_axis=0, concat_axis=0, tiled=True)
    return gathered.reshape(terms.shape)


def per_device(
    features,
    cotangent,
    wall_flags,
    mode_counts,
    offsets,
    point_weight,
    kernel_weight,
    lap_weight,
    spec_weight,
    bias,
):
    mode_total = spec_weight.shape[0]
    tile_total = kernel_weight.shape[0]
    kept_modes = (jnp.arange(mode_total, dtype=jnp.int32)[:, None] < mode_counts[None, :]).astype(
        jnp.float32
    )
    fluid_mask = (1 - wall_flags).astype(jnp.float32)[:, :, None, :]
    extended = with_halo(features, (("gx", 0),), 1)
    padded_field = pad_sides(extended)
    local_part = jnp.einsum(
        "oc,xycz->xyoz", point_weight, features, preferred_element_type=jnp.float32
    )
    local_part = local_part + jnp.einsum(
        "oc,xycz->xyoz", lap_weight, laplace_ext(extended), preferred_element_type=jnp.float32
    )
    for tile in range(tile_total):
        moved = window_of(padded_field, offsets[tile], 1, features.shape)
        local_part = local_part + jnp.einsum(
            "oc,xycz->xyoz", kernel_weight[tile], moved, preferred_element_type=jnp.float32
        )
    local_part = local_part + bias[:, None]
    spectral_part = spectral(features, spec_weight, kept_modes, False)
    preact = local_part + spectral_part.astype(jnp.float32)
    weighted = (gelu_slope(preact, cotangent.astype(jnp.float32)) * fluid_mask).astype(jnp.bfloat16)
    spec_grad = spectral(weighted, spec_weight, kept_modes, True)
    ext_grad = with_halo(weighted, (("gx", 0),), 1)
    padded_grad = pad_sides(ext_grad)
    input_grad = jnp.einsum(
        "oc,xyoz->xycz", point_weight, weighted, preferred_element_type=jnp.float32
    )
    input_grad = input_grad + jnp.einsum(
        "oc,xyoz->xycz", lap_weight, laplace_ext(ext_grad), preferred_element_type=jnp.float32
    )
    input_grad = input_grad + spec_grad.astype(jnp.float32)
    tile_grads = []
    for tile in range(tile_total):
        back_moved = window_of(padded_grad, offsets[tile], -1, weighted.shape)
        input_grad = input_grad + jnp.einsum(
            "oc,xyoz->xycz", kernel_weight[tile], back_moved, preferred_element_type=jnp.float32
        )
        tile_grads.append(
            jnp.einsum("xyoz,xycz->oc", back_moved, features, preferred_element_type=jnp.float32)
        )
    local_grad = jnp.stack(tile_grads, axis=0)
    scaling = float(
        lax.axis_size("gx") * features.shape[0] * features.shape[1] * features.shape[3]
    ) ** (-0.5)
    summed = sum_over_gx(local_grad)
    return (input_grad.astype(jnp.bfloat16), summed * scaling)


def fused_kernel(
    count,
    feat_in,
    cot_in,
    wall_in,
    mode_in,
    offs_in,
    basis_in,
    point_in,
    tile_in,
    lap_in,
    spec_in,
    bias_in,
    out,
    kout,
    feat,
    cot,
    wall,
    mode_row,
    bias_row,
    offs,
    basis,
    wst,
    wm,
    wmt,
    wf,
    wb,
    mode,
    bias,
    zs,
    cat,
    local,
    acc,
    vh,
    pen1,
    pen2,
    stage1,
    stage2,
    spec1,
    spec2,
    wgt,
    halo1,
    halo2,
    rel1,
    rel2,
    kacc,
    kdense,
    kpart,
    kmine,
    kother,
    ksum,
    kall,
    shift,
    send,
    recv,
    hsend,
    hrecv,
    vsend,
    vrecv,
    rsend,
    rrecv,
    ksend,
    krecv,
    xsend,
    xrecv,
    fsend,
    frecv,
    load,
):
    me = lax.axis_index("gx")
    grp = lax.axis_index("groups")
    xl, ny, ch, nz = feat.shape
    modes = wm.shape[0]
    tiles = offs.shape[1]
    half = count // 2
    quads = half // 2
    f32, bf16 = jnp.float32, jnp.bfloat16
    side = me // half
    inner = me % half
    chip = inner // 2

    def push(src, dst, ssem, rsem, peer):
        return pltpu.make_async_remote_copy(
            src_ref=src,
            dst_ref=dst,
            send_sem=ssem,
            recv_sem=rsem,
            device_id=(grp, peer),
            device_id_type=MESH,
        )

    def each(low, high, body):
        def step(i, carry):
            body(i)
            return carry

        lax.fori_loop(low, high, step, 0)

    def place(cross, turn, core):
        return ((side + cross) % 2) * half + ((chip + turn) % quads) * 2 + core

    def by_core(j):
        core = j // half
        rest = j % half
        return place(1 - rest // quads, rest % quads, core)

    def by_side(j):
        rest = j % half
        return place(1 - j // half, rest // 2, rest % 2)

    def from_side(j):
        rest = j % half
        return place(1 - j // half, quads - rest // 2, rest % 2)

    def from_core(j):
        core = j // half
        rest = j % half
        return place(1 - rest // quads, quads - rest % quads, core)

    def others(low, high, order, body):
        def visit(j):
            peer = order(j)

            @pl.when(peer != me)
            def _():
                body(peer)

        each(low, high, visit)

    def share1(peer):
        return push(
            feat.at[:, peer], pen1.at[me], send.at[0, peer], recv.at[0, me], peer
        )

    def land1(src):
        return push(feat.at[:, src], pen1.at[src], send.at[0, src], recv.at[0, src], src)

    def give1(peer):
        return push(stage1.at[peer], spec1.at[me], send.at[1, peer], recv.at[1, me], peer)

    def back1(src):
        return push(stage1.at[src], spec1.at[src], send.at[1, src], recv.at[1, src], src)

    def share2(peer):
        return push(wgt.at[peer], pen2.at[me], send.at[2, peer], recv.at[2, me], peer)

    def land2(src):
        return push(wgt.at[src], pen2.at[src], send.at[2, src], recv.at[2, src], src)

    def give2(peer):
        return push(stage2.at[peer], spec2.at[me], send.at[3, peer], recv.at[3, me], peer)

    def back2(src):
        return push(stage2.at[src], spec2.at[src], send.at[3, src], recv.at[3, src], src)

    loads = [
        pltpu.make_async_copy(feat_in, feat, load.at[0]),
        pltpu.make_async_copy(point_in, wst.at[0], load.at[1]),
        pltpu.make_async_copy(lap_in, wst.at[1], load.at[2]),
        pltpu.make_async_copy(tile_in, wst.at[pl.ds(2, tiles)], load.at[3]),
        pltpu.make_async_copy(spec_in, wm, load.at[4]),
        pltpu.make_async_copy(mode_in, mode_row, load.at[5]),
        pltpu.make_async_copy(bias_in, bias_row, load.at[6]),
        pltpu.make_async_copy(wall_in, wall, load.at[7]),
        pltpu.make_async_copy(cot_in, cot, load.at[8]),
        pltpu.make_async_copy(offs_in, offs, load.at[9]),
        pltpu.make_async_copy(basis_in, basis, load.at[10]),
    ]
    barrier = pltpu.get_barrier_semaphore()
    each(
        1,
        count,
        lambda d: pl.semaphore_signal(
            barrier, inc=1, device_id=(grp, lax.rem(me + d, count)), device_id_type=MESH
        ),
    )
    for piece in loads:
        piece.start()

    pl.semaphore_wait(barrier, count - 1)
    loads[0].wait()

    low_edge = half - 1
    via = rel1.shape[0]
    up_relay = low_edge - 2
    down_relay = half + 2

    def low_copy(peer):
        return push(feat.at[0], halo1.at[1], hsend.at[0], hrecv.at[0], peer)

    def high_copy(peer):
        return push(feat.at[xl - 1], halo1.at[0], hsend.at[1], hrecv.at[1], peer)

    def low_cross():
        part = pl.ds(half - 1 + via, half + 1 - via)
        return push(feat.at[0, part], halo1.at[1, part], hsend.at[0], hrecv.at[0], low_edge)

    def high_cross():
        part = pl.ds(0, half + 1 - via)
        return push(feat.at[xl - 1, part], halo1.at[0, part], hsend.at[1], hrecv.at[1], half)

    def up_first(peer):
        part = pl.ds(half + 1 - via, via)
        return push(feat.at[xl - 1, part], rel1, hsend.at[2], hrecv.at[2], peer)

    def down_first(peer):
        return push(feat.at[0, pl.ds(half - 1, via)], rel1, hsend.at[2], hrecv.at[2], peer)

    def up_second(peer):
        part = pl.ds(half + 1 - via, via)
        return push(rel1, halo1.at[0, part], hsend.at[3], hrecv.at[3], peer)

    def down_second(peer):
        part = pl.ds(half - 1, via)
        return push(rel1, halo1.at[1, part], hsend.at[3], hrecv.at[3], peer)

    def low_pass():
        return push(pen1.at[half, 0], halo1.at[1, me], fsend.at[0], frecv.at[me], low_edge)

    def high_pass():
        return push(
            pen1.at[low_edge, xl - 1], halo1.at[0, me], fsend.at[0], frecv.at[me], half
        )

    def low_row(y, peer):
        return push(wgt.at[y, 0], halo2.at[1, y], rsend.at[0, y], rrecv.at[0, y], peer)

    def high_row(y, peer):
        return push(wgt.at[y, xl - 1], halo2.at[0, y], rsend.at[1, y], rrecv.at[1, y], peer)

    def low_relay():
        return push(
            pen2.at[half, 0], halo2.at[1, me], fsend.at[0], rrecv.at[0, me], low_edge
        )

    def high_relay():
        return push(
            pen2.at[low_edge, xl - 1], halo2.at[0, me], fsend.at[0], rrecv.at[1, me], half
        )

    def low_detour(y, peer):
        slot = y - (half - 1)
        return push(wgt.at[y, 0], rel2.at[slot], rsend.at[0, y], vrecv.at[slot], peer)

    def high_detour(y, peer):
        slot = y - (half + 1 - via)
        return push(wgt.at[y, xl - 1], rel2.at[slot], rsend.at[1, y], vrecv.at[slot], peer)

    def low_onward(slot, peer):
        y = slot + half - 1
        return push(rel2.at[slot], halo2.at[1, y], vsend.at[slot], rrecv.at[0, y], peer)

    def high_onward(slot, peer):
        y = slot + half + 1 - via
        return push(rel2.at[slot], halo2.at[0, y], vsend.at[slot], rrecv.at[1, y], peer)

    def low_turned(y):
        return (me == half) & (y >= low_edge) & (y < low_edge + via)

    def high_turned(y):
        return (me == low_edge) & (y > half - via) & (y <= half)

    def low_straight(y):
        return (me > 0) & ((me != half) | (y >= low_edge + via))

    def high_straight(y):
        return (me < count - 1) & ((me != low_edge) | (y <= half - via))

    def low_own(y):
        return (me > 0) & ((me != half) | (y >= low_edge))

    def high_own(y):
        return (me < count - 1) & ((me != low_edge) | (y <= half))

    def when(cond, body):
        @pl.when(cond)
        def _():
            body()

    inside_low = (me > 0) & (me != half)
    inside_high = (me < count - 1) & (me != low_edge)
    others(0, half, by_core, lambda peer: share1(peer).start())
    when(me == half, lambda: low_cross().start())
    when(me == low_edge, lambda: high_cross().start())
    when(me == half, lambda: down_first(down_relay).start())
    when(me == low_edge, lambda: up_first(up_relay).start())
    when(inside_low, lambda: low_copy(me - 1).start())
    when(inside_high, lambda: high_copy(me + 1).start())
    others(half, count, by_core, lambda peer: share1(peer).start())

    from_z = lax.broadcasted_iota(jnp.int32, (nz, nz), 0)
    to_z = lax.broadcasted_iota(jnp.int32, (nz, nz), 1)
    for m, dz in enumerate([dz for dz in range(-RAD, RAD + 1) if dz]):
        shift[:, m * nz : (m + 1) * nz] = jnp.where(from_z == to_z + dz, 1.0, 0.0).astype(bf16)

    @pl.when(me == 0)
    def _():
        halo1[0] = jnp.zeros(halo1.shape[1:], bf16)
        halo2[0] = jnp.zeros(halo2.shape[1:], bf16)

    @pl.when(me == count - 1)
    def _():
        halo1[1] = jnp.zeros(halo1.shape[1:], bf16)
        halo2[1] = jnp.zeros(halo2.shape[1:], bf16)

    for edge in (0, RAD + ny):
        for dz in range(2 * RAD + 1):
            for x in range(xl + 2):
                zs[dz, x, edge : edge + RAD] = jnp.zeros((RAD, ch, nz), bf16)

    moves = [dz for dz in range(-RAD, RAD + 1) if dz]
    group = math.gcd(ny, 8)

    def spread(take, place_x):
        def body(i):
            y = i * group
            v = take(pl.ds(y, group))
            zs[RAD, place_x, pl.ds(y + RAD, group)] = v
            flat = v.reshape(group * ch, nz)
            moved = jnp.dot(flat, shift[...], preferred_element_type=f32).astype(bf16)
            for m, dz in enumerate(moves):
                piece = moved[:, m * nz : (m + 1) * nz].reshape(group, ch, nz)
                zs[RAD + dz, place_x, pl.ds(y + RAD, group)] = piece

        each(0, ny // group, body)

    def gather_rows(direction):
        def body(y):
            for x in range(xl):
                lanes = slice(x * nz, (x + 1) * nz)
                centre = zs[RAD, x + 1, y + RAD]
                cat[y, 0:ch, lanes] = centre
                total = zs[RAD, x + 2, y + RAD].astype(f32) + zs[RAD, x, y + RAD].astype(f32)
                total = total + zs[RAD, x + 1, y + RAD + 1].astype(f32)
                total = total + zs[RAD, x + 1, y + RAD - 1].astype(f32)
                total = total + zs[RAD + 1, x + 1, y + RAD].astype(f32)
                total = total + zs[RAD - 1, x + 1, y + RAD].astype(f32)
                cat[y, ch : 2 * ch, lanes] = (total - 6.0 * centre.astype(f32)).astype(bf16)
                for t in range(tiles):
                    moved = zs[
                        RAD + direction * offs[2, t],
                        x + 1 + direction * offs[0, t],
                        y + RAD + direction * offs[1, t],
                    ]
                    cat[y, (2 + t) * ch : (3 + t) * ch, lanes] = moved

        each(0, ny, body)

    unroll = math.gcd(ny, 4)

    def each_row(body):
        def rows_at(i):
            for r in range(unroll):
                body(i * unroll + r)

        each(0, ny // unroll, rows_at)

    def mix(weights):
        def body(y):
            local[y] = jnp.dot(weights[...], cat[y], preferred_element_type=f32)

        each_row(body)

    def gain(planes, src):
        wide = [p.astype(f32) for p in planes]
        for k in range(modes):
            total = acc[k]
            for j in range(xl):
                total = total + basis[k, src * xl + j] * wide[j]
            acc[k] = total

    def forward_mix():
        for k in range(modes):
            v = jnp.dot(wm[k], acc[k].astype(bf16), preferred_element_type=f32)
            v = jnp.where(mode[...] > float(k), v, 0.0)
            vh[k] = v.astype(bf16).astype(f32)

    def backward_mix():
        for k in range(modes):
            u = jnp.where(mode[...] > float(k), acc[k], 0.0).astype(bf16)
            v = jnp.dot(wmt[k], u, preferred_element_type=f32)
            vh[k] = v.astype(bf16).astype(f32)

    def expand(stage, peer):
        for j in range(xl):
            total = basis[0, peer * xl + j] * vh[0]
            for k in range(1, modes):
                total = total + basis[k, peer * xl + j] * vh[k]
            stage[peer, j] = total.astype(bf16)

    for x in range(xl):
        spread(lambda y: feat[x, y], x + 1)
    for piece in loads[1:]:
        piece.wait()

    row_at = lax.broadcasted_iota(jnp.int32, (ch, ch), 0)
    col_at = lax.broadcasted_iota(jnp.int32, (ch, ch), 1)
    diagonal = row_at == col_at
    unit = jnp.where(diagonal, 1.0, 0.0).astype(bf16)

    def upright(row):
        spread_out = jnp.where(diagonal, jnp.broadcast_to(row, (ch, ch)), 0.0)
        column = jnp.sum(spread_out, axis=1, keepdims=True)
        return jnp.broadcast_to(column, (ch, nz))

    mode[...] = upright(mode_row[...].astype(f32))
    bias[...] = upright(bias_row[...])

    def flipped(block):
        return lax.dot_general(
            block, unit, (((0,), (0,)), ((), ())), preferred_element_type=f32
        ).astype(bf16)

    for t in range(2 + tiles):
        wf[:, t * ch : (t + 1) * ch] = wst[t]
        wb[:, t * ch : (t + 1) * ch] = flipped(wst[t])

    def flip_mode(k):
        wmt[k] = flipped(wm[k])

    each(0, modes, flip_mode)

    def passed_low(i):
        push(
            pen1.at[low_edge, xl - 1], halo1.at[0, i], fsend.at[0], frecv.at[i], low_edge
        ).wait_recv()

    def passed_high(i):
        push(pen1.at[half, 0], halo1.at[1, i], fsend.at[0], frecv.at[i], half).wait_recv()

    def forward_stencil():
        when(inside_low, lambda: high_copy(me - 1).wait_recv())
        when(inside_high, lambda: low_copy(me + 1).wait_recv())

        @pl.when(me == half)
        def _():
            high_cross_here = push(
                feat.at[xl - 1, pl.ds(0, half + 1 - via)],
                halo1.at[0, pl.ds(0, half + 1 - via)],
                hsend.at[1],
                hrecv.at[1],
                low_edge,
            )
            high_cross_here.wait_recv()
            up_second(up_relay).wait_recv()
            each(half + 1, count, passed_low)

        @pl.when(me == low_edge)
        def _():
            low_cross_here = push(
                feat.at[0, pl.ds(half - 1 + via, half + 1 - via)],
                halo1.at[1, pl.ds(half - 1 + via, half + 1 - via)],
                hsend.at[0],
                hrecv.at[0],
                half,
            )
            low_cross_here.wait_recv()
            down_second(down_relay).wait_recv()
            each(0, half - 1, passed_high)

        spread(lambda y: halo1[0, y], 0)
        spread(lambda y: halo1[1, y], xl + 1)
        gather_rows(1)
        mix(wf)

    core = me % 2

    @pl.when(me == up_relay)
    def _():
        up_first(low_edge).wait_recv()
        up_second(half).start()

    @pl.when(me == down_relay)
    def _():
        down_first(half).wait_recv()
        down_second(low_edge).start()

    early = (core == 1) & (me != low_edge)
    when(early, forward_stencil)

    acc[...] = jnp.zeros(acc.shape, f32)
    gain([feat[j, me] for j in range(xl)], me)

    def take1(src):
        land1(src).wait_recv()
        when((src == half) & (me < low_edge), lambda: low_pass().start())
        when((src == low_edge) & (me > half), lambda: high_pass().start())
        gain([pen1[src, j] for j in range(xl)], src)

    others(0, count, from_side, take1)
    forward_mix()

    def hand1(peer):
        expand(stage1, peer)
        give1(peer).start()

    others(0, count, by_core, hand1)
    expand(stage1, me)
    when(jnp.logical_not(early), forward_stencil)
    root = math.sqrt(2.0 / math.pi)

    def slope(y, planes):
        for x in range(xl):
            v = local[y, :, x * nz : (x + 1) * nz] + planes[x].astype(f32) + bias[...]
            square = v * v
            t = jnp.tanh(root * (v + 0.044715 * (square * v)))
            g = 0.5 * (1.0 + t)
            g = g + (0.5 * v) * ((1.0 - t * t) * (root * (1.0 + (3.0 * 0.044715) * square)))
            fluid = (1 - wall[x, pl.ds(y, 1), :]).astype(f32)
            wgt[y, x] = ((cot[x, y].astype(f32) * g) * fluid).astype(bf16)
        when(low_straight(y), lambda: low_row(y, me - 1).start())
        when(high_straight(y), lambda: high_row(y, me + 1).start())
        when(low_turned(y), lambda: low_detour(y, down_relay).start())
        when(high_turned(y), lambda: high_detour(y, up_relay).start())

    kacc[...] = jnp.zeros(kacc.shape, f32)

    def row_work(y):
        planes = jnp.concatenate([wgt[y, x] for x in range(xl)], axis=1)
        kacc[...] += lax.dot_general(
            cat[y, 2 * ch :, :], planes, (((1,), (1,)), ((), ())), preferred_element_type=f32
        )
        flat = jnp.concatenate([wgt[y, x] for x in range(xl)], axis=0)
        moved = jnp.dot(flat, shift[...], preferred_element_type=f32).astype(bf16)
        for x in range(xl):
            zs[RAD, x + 1, y + RAD] = wgt[y, x]
            for m, dz in enumerate(moves):
                piece = moved[x * ch : (x + 1) * ch, m * nz : (m + 1) * nz]
                zs[RAD + dz, x + 1, y + RAD] = piece

    slope(me, [stage1[me, j] for j in range(xl)])

    def turn(src):
        back1(src).wait_recv()
        slope(src, [spec1[src, j] for j in range(xl)])
        share2(src).start()

    def turn_work(src):
        turn(src)
        row_work(src)

    others(0, half, by_core, turn)
    row_work(me)
    others(0, half, by_core, row_work)
    others(half, count, by_core, turn_work)

    pairs = tiles // 2
    for t in range(pairs):
        kdense[t * ch : (t + 1) * ch] = jnp.concatenate(
            [
                jnp.transpose(kacc[p * ch : (p + 1) * ch])
                for p in (t, t + pairs)
            ],
            axis=1,
        )

    rows = kpart.shape[1]

    def strip(p):
        return kdense.at[pl.ds(p * rows, rows)]

    def near(body):
        def visit(d):
            body((inner + d) % half)

        each(1, half, visit)

    def ksend_to(p):
        return push(
            strip(p), kpart.at[inner], ksend.at[0, p], krecv.at[0, inner], side * half + p
        )

    def kland(p):
        return push(strip(p), kpart.at[p], ksend.at[0, p], krecv.at[0, p], side * half + p)

    near(lambda p: ksend_to(p).start())
    def pass_up(slot):
        high_detour(slot + half + 1 - via, low_edge).wait_recv()
        high_onward(slot, half).start()

    def pass_down(slot):
        low_detour(slot + half - 1, half).wait_recv()
        low_onward(slot, low_edge).start()

    when(me == up_relay, lambda: each(0, via, pass_up))
    when(me == down_relay, lambda: each(0, via, pass_down))

    acc[...] = jnp.zeros(acc.shape, f32)
    gain([wgt[me, j] for j in range(xl)], me)

    def take2(src):
        land2(src).wait_recv()
        when((src == half) & (me < low_edge), lambda: low_relay().start())
        when((src == low_edge) & (me > half), lambda: high_relay().start())
        gain([pen2[src, j] for j in range(xl)], src)

    when(me < low_edge, lambda: low_pass().wait_send())
    when(me > half, lambda: high_pass().wait_send())
    others(0, count, from_side, take2)
    backward_mix()

    def hand2(peer):
        expand(stage2, peer)
        give2(peer).start()

    others(0, 2, by_core, hand2)
    kpart[inner] = kdense[pl.ds(inner * rows, rows)]
    near(lambda p: kland(p).wait_recv())
    part_sum = kpart[0]
    for p in range(1, half):
        part_sum = part_sum + kpart[p]
    kmine[...] = part_sum
    partner = ((side + 1) % 2) * half + inner
    across = push(kmine, kother, xsend.at[0], xrecv.at[0], partner)
    across.start()
    others(2, count, by_core, hand2)
    expand(stage2, me)

    def halo_rows(y):
        when(me > 0, lambda: high_row(y, me - 1).wait_recv())
        when(me < count - 1, lambda: low_row(y, me + 1).wait_recv())

    each(0, ny, halo_rows)
    spread(lambda y: halo2[0, y], 0)
    spread(lambda y: halo2[1, y], xl + 1)
    gather_rows(-1)

    mix(wb)

    def finish(y, planes):
        for x in range(xl):
            total = local[y, :, x * nz : (x + 1) * nz] + planes[x].astype(f32)
            out[x, y] = total.astype(bf16)

    finish(me, [stage2[me, j] for j in range(xl)])

    def last(src):
        back2(src).wait_recv()
        finish(src, [spec2[src, j] for j in range(xl)])

    across.wait_recv()
    ksum[...] = (kmine[...] + kother[...]) * (float(count * xl * ny * nz) ** -0.5)
    kall[pl.ds(inner * rows, rows)] = ksum[...]

    def piece_of(p):
        return kall.at[pl.ds(p * rows, rows)]

    def kspread(p):
        return push(ksum, piece_of(inner), ksend.at[1, p], krecv.at[1, inner], side * half + p)

    def kcollect(p):
        return push(ksum, piece_of(p), ksend.at[1, p], krecv.at[1, p], side * half + p)

    near(lambda p: kspread(p).start())

    others(half, count, from_side, last)
    others(0, half, from_side, last)
    near(lambda p: kcollect(p).wait_recv())
    for t in range(pairs):
        kout[t] = kall[t * ch : (t + 1) * ch, 0:ch]
        kout[t + pairs] = kall[t * ch : (t + 1) * ch, ch : 2 * ch]

    when(me == half, lambda: low_cross().wait_send())
    when(me == low_edge, lambda: high_cross().wait_send())
    when(me == half, lambda: down_first(down_relay).wait_send())
    when(me == low_edge, lambda: up_first(up_relay).wait_send())
    when(me == up_relay, lambda: up_second(half).wait_send())
    when(me == down_relay, lambda: down_second(low_edge).wait_send())
    when(me == up_relay, lambda: each(0, via, lambda i: high_onward(i, half).wait_send()))
    when(me == down_relay, lambda: each(0, via, lambda i: low_onward(i, low_edge).wait_send()))
    when(inside_low, lambda: low_copy(me - 1).wait_send())
    when(inside_high, lambda: high_copy(me + 1).wait_send())

    def row_sent(y):
        when(low_own(y), lambda: low_row(y, me - 1).wait_send())
        when(high_own(y), lambda: high_row(y, me + 1).wait_send())

    each(0, ny, row_sent)
    when(me < low_edge, lambda: low_relay().wait_send())
    when(me > half, lambda: high_relay().wait_send())
    across.wait_send()

    def near_sent(p):
        ksend_to(p).wait_send()
        kspread(p).wait_send()

    near(near_sent)

    def drain(peer):
        share1(peer).wait_send()
        give1(peer).wait_send()
        share2(peer).wait_send()
        give2(peer).wait_send()

    others(0, count, by_side, drain)


def flush_kernel(field, tile, field_out, tile_out, sems):
    first = pltpu.make_async_copy(field, field_out, sems.at[0])
    second = pltpu.make_async_copy(tile, tile_out, sems.at[1])
    first.start()
    second.start()
    first.wait()
    second.wait()


def fits_kernel(count, features, kernel_weight):
    xl, ny, ch, nz = features.shape
    cells = xl * ny * ch * nz
    tile_rows = kernel_weight.shape[0] * ch
    if ny != count or count % 4 or nz % 128 or ch % 64 or kernel_weight.shape[0] % 2:
        return False
    if tile_rows % (8 * count):
        return False
    return 80 * cells < 24 * 2**20


def fused_device(
    features,
    cotangent,
    wall_flags,
    mode_counts,
    offsets,
    point_weight,
    kernel_weight,
    lap_weight,
    spec_weight,
    bias,
):
    count = lax.axis_size("gx")
    if not fits_kernel(count, features, kernel_weight):
        return per_device(
            features,
            cotangent,
            wall_flags,
            mode_counts,
            offsets,
            point_weight,
            kernel_weight,
            lap_weight,
            spec_weight,
            bias,
        )
    xl, ny, ch, nz = features.shape
    modes, tiles = spec_weight.shape[0], kernel_weight.shape[0]
    half = count // 2
    rows = tiles * ch // (2 * half)
    f32, bf16 = jnp.float32, jnp.bfloat16
    dma = pltpu.SemaphoreType.DMA
    vmem = pl.BlockSpec(memory_space=pltpu.VMEM)
    hbm = pl.BlockSpec(memory_space=pltpu.HBM)
    field_grad, tile_grad = pl.pallas_call(
        functools.partial(fused_kernel, count),
        out_shape=(
            pltpu.VMEM(features.shape, bf16),
            pltpu.VMEM(kernel_weight.shape, f32),
        ),
        in_specs=[hbm, hbm, hbm, hbm, hbm, hbm, hbm, hbm, hbm, hbm, hbm],
        out_specs=(vmem, vmem),
        scratch_shapes=[
            pltpu.VMEM((xl, ny, ch, nz), bf16),
            pltpu.VMEM((xl, ny, ch, nz), bf16),
            pltpu.VMEM((xl, ny, nz), jnp.int32),
            pltpu.VMEM((1, ch), jnp.int32),
            pltpu.VMEM((1, ch), f32),
            pltpu.SMEM((3, tiles), jnp.int32),
            pltpu.SMEM((modes, count * xl), f32),
            pltpu.VMEM((2 + tiles, ch, ch), bf16),
            pltpu.VMEM((modes, ch, ch), bf16),
            pltpu.VMEM((modes, ch, ch), bf16),
            pltpu.VMEM((ch, (2 + tiles) * ch), bf16),
            pltpu.VMEM((ch, (2 + tiles) * ch), bf16),
            pltpu.VMEM((ch, nz), f32),
            pltpu.VMEM((ch, nz), f32),
            pltpu.VMEM((2 * RAD + 1, xl + 2, ny + 2 * RAD, ch, nz), bf16),
            pltpu.VMEM((ny, (2 + tiles) * ch, xl * nz), bf16),
            pltpu.VMEM((ny, ch, xl * nz), f32),
            pltpu.VMEM((modes, ch, nz), f32),
            pltpu.VMEM((modes, ch, nz), f32),
            pltpu.VMEM((count, xl, ch, nz), bf16),
            pltpu.VMEM((count, xl, ch, nz), bf16),
            pltpu.VMEM((count, xl, ch, nz), bf16),
            pltpu.VMEM((count, xl, ch, nz), bf16),
            pltpu.VMEM((count, xl, ch, nz), bf16),
            pltpu.VMEM((count, xl, ch, nz), bf16),
            pltpu.VMEM((ny, xl, ch, nz), bf16),
            pltpu.VMEM((2, ny, ch, nz), bf16),
            pltpu.VMEM((2, ny, ch, nz), bf16),
            pltpu.VMEM((half // 2, ch, nz), bf16),
            pltpu.VMEM((half // 2, ch, nz), bf16),
            pltpu.VMEM((tiles * ch, ch), f32),
            pltpu.VMEM((tiles * ch // 2, 2 * ch), f32),
            pltpu.VMEM((half, rows, 2 * ch), f32),
            pltpu.VMEM((rows, 2 * ch), f32),
            pltpu.VMEM((rows, 2 * ch), f32),
            pltpu.VMEM((rows, 2 * ch), f32),
            pltpu.VMEM((tiles * ch // 2, 2 * ch), f32),
            pltpu.VMEM((nz, 2 * RAD * nz), bf16),
            dma((4, count)),
            dma((4, count)),
            dma((4,)),
            dma((4,)),
            dma((half // 2,)),
            dma((half // 2,)),
            dma((2, ny)),
            dma((2, ny)),
            dma((2, half)),
            dma((2, half)),
            dma((1,)),
            dma((1,)),
            dma((1,)),
            dma((ny,)),
            dma((11,)),
        ],
        compiler_params=pltpu.CompilerParams(
            collective_id=0, has_side_effects=True, vmem_limit_bytes=56 * 2**20
        ),
    )(
        features,
        cotangent,
        wall_flags,
        mode_counts.reshape(1, ch),
        offsets.T,
        basis_constant(modes, count * xl),
        point_weight,
        kernel_weight,
        lap_weight,
        spec_weight,
        bias.reshape(1, ch),
    )
    field_grad, tile_grad = pl.pallas_call(
        flush_kernel,
        out_shape=(
            jax.ShapeDtypeStruct(features.shape, bf16),
            jax.ShapeDtypeStruct(kernel_weight.shape, f32),
        ),
        in_specs=[vmem] * 2,
        out_specs=(hbm,) * 2,
        scratch_shapes=[dma((2,))],
    )(
        pltpu.with_memory_space_constraint(field_grad, pltpu.VMEM),
        pltpu.with_memory_space_constraint(tile_grad, pltpu.VMEM),
    )
    return field_grad, tile_grad


def solution(mesh):
    return jax.shard_map(
        fused_device,
        mesh=mesh,
        in_specs=(
            P(("groups", "gx"), None, None, None),
            P(("groups", "gx"), None, None, None),
            P(("groups", "gx"), None, None),
            P(),
            P(),
            P(),
            P(),
            P(),
            P(),
            P(),
        ),
        out_specs=(P(("groups", "gx"), None, None, None), P("groups", None, None)),
        check_vma=False,
    )
```

```python
import functools
from functools import partial
import math

import jax
import ml_dtypes
import numpy as np
import jax.numpy as jnp
from jax import lax
from jax.experimental import pallas as pl
from jax.experimental.pallas import tpu as pltpu
from jax.sharding import PartitionSpec as P

RAD = 2
MESH = pl.DeviceIdType.MESH


def with_halo(cells, sides, width):
    for axis, dim in sides:
        count = lax.axis_size(axis)
        ends = count - 1
        head = lax.slice_in_dim(cells, 0, width, axis=dim)
        tail = lax.slice_in_dim(cells, cells.shape[dim] - width, cells.shape[dim], axis=dim)
        cells = jnp.concatenate(
            [
                lax.ppermute(tail, axis, [(i, (i + 1) % count) for i in range(ends)]),
                cells,
                lax.ppermute(head, axis, [((i + 1) % count, i) for i in range(ends)]),
            ],
            axis=dim,
        )
    return cells


def basis_table(mode_total, length):
    mode_index = jnp.arange(mode_total, dtype=jnp.float32)[:, None]
    cell_index = jnp.arange(length, dtype=jnp.float32)[None, :]
    phase_angle = math.pi / (2.0 * length) * mode_index * (2.0 * cell_index + 1.0)
    amplitude = jnp.where(mode_index == 0.0, math.sqrt(1.0 / length), math.sqrt(2.0 / length))
    return (amplitude * jnp.cos(phase_angle)).astype(jnp.bfloat16)


def basis_constant(mode_total, length):
    mode_index = np.arange(mode_total, dtype=np.float64)[:, None]
    cell_index = np.arange(length, dtype=np.float64)[None, :]
    phase_angle = math.pi / (2.0 * length) * mode_index * (2.0 * cell_index + 1.0)
    amplitude = np.where(mode_index == 0.0, math.sqrt(1.0 / length), math.sqrt(2.0 / length))
    table = (amplitude * np.cos(phase_angle)).astype(np.float32)
    return table.astype(ml_dtypes.bfloat16).astype(np.float32)


def pencil_work(pencil, spec_weight, kept_modes, adjoint):
    basis = basis_table(spec_weight.shape[0], pencil.shape[0])
    coefficients = jnp.einsum(
        "kx,xycz->kycz", basis, pencil, preferred_element_type=jnp.float32
    ).astype(jnp.bfloat16)
    if adjoint:
        masked = coefficients * kept_modes[:, None, :, None].astype(jnp.bfloat16)
        mixed_modes = jnp.einsum(
            "koc,kyoz->kycz", spec_weight, masked, preferred_element_type=jnp.float32
        ).astype(jnp.bfloat16)
    else:
        mixed_modes = jnp.einsum(
            "koc,kycz->kyoz", spec_weight, coefficients, preferred_element_type=jnp.float32
        )
        mixed_modes = (mixed_modes * kept_modes[:, None, :, None]).astype(jnp.bfloat16)
    return jnp.einsum(
        "kx,kyoz->xyoz", basis, mixed_modes, preferred_element_type=jnp.float32
    ).astype(jnp.bfloat16)


def spectral(slab, spec_weight, kept_modes, adjoint):
    result = pencil_work(
        lax.all_to_all(slab, "gx", split_axis=1, concat_axis=0, tiled=True),
        spec_weight,
        kept_modes,
        adjoint,
    )
    return lax.all_to_all(result, "gx", split_axis=0, concat_axis=1, tiled=True)


def laplace_ext(extended):
    padded = jnp.pad(extended, ((0, 0), (1, 1), (0, 0), (1, 1))).astype(jnp.float32)
    centre_cells = padded[1:-1, 1:-1, :, 1:-1]
    neighbours = padded[2:, 1:-1, :, 1:-1] + padded[:-2, 1:-1, :, 1:-1]
    neighbours = neighbours + padded[1:-1, 2:, :, 1:-1] + padded[1:-1, :-2, :, 1:-1]
    neighbours = neighbours + padded[1:-1, 1:-1, :, 2:] + padded[1:-1, 1:-1, :, :-2]
    return (neighbours - 6.0 * centre_cells).astype(jnp.bfloat16)


def pad_sides(extended):
    return jnp.pad(extended, ((0, 0), (RAD, RAD), (0, 0), (RAD, RAD)))


def window_of(padded, offset, direction, slab_shape):
    starts = (
        1 + direction * offset[0],
        RAD + direction * offset[1],
        0,
        RAD + direction * offset[2],
    )
    return lax.dynamic_slice(padded, starts, slab_shape)


def gelu_slope(preact, upstream):
    _, pullback = jax.vjp(partial(jax.nn.gelu, approximate=True), preact)
    return pullback(upstream)[0]


def sum_over_gx(terms):
    count = lax.axis_size("gx")
    if terms.size % count:
        return lax.psum(terms, "gx")
    pieces = lax.all_to_all(terms.reshape(count, -1), "gx", split_axis=0, concat_axis=0, tiled=True)
    mine = jnp.sum(pieces, axis=0)
    copies = jnp.broadcast_to(mine[None, :], pieces.shape)
    gathered = lax.all_to_all(copies, "gx", split_axis=0, concat_axis=0, tiled=True)
    return gathered.reshape(terms.shape)


def per_device(
    features,
    cotangent,
    wall_flags,
    mode_counts,
    offsets,
    point_weight,
    kernel_weight,
    lap_weight,
    spec_weight,
    bias,
):
    mode_total = spec_weight.shape[0]
    tile_total = kernel_weight.shape[0]
    kept_modes = (jnp.arange(mode_total, dtype=jnp.int32)[:, None] < mode_counts[None, :]).astype(
        jnp.float32
    )
    fluid_mask = (1 - wall_flags).astype(jnp.float32)[:, :, None, :]
    extended = with_halo(features, (("gx", 0),), 1)
    padded_field = pad_sides(extended)
    local_part = jnp.einsum(
        "oc,xycz->xyoz", point_weight, features, preferred_element_type=jnp.float32
    )
    local_part = local_part + jnp.einsum(
        "oc,xycz->xyoz", lap_weight, laplace_ext(extended), preferred_element_type=jnp.float32
    )
    for tile in range(tile_total):
        moved = window_of(padded_field, offsets[tile], 1, features.shape)
        local_part = local_part + jnp.einsum(
            "oc,xycz->xyoz", kernel_weight[tile], moved, preferred_element_type=jnp.float32
        )
    local_part = local_part + bias[:, None]
    spectral_part = spectral(features, spec_weight, kept_modes, False)
    preact = local_part + spectral_part.astype(jnp.float32)
    weighted = (gelu_slope(preact, cotangent.astype(jnp.float32)) * fluid_mask).astype(jnp.bfloat16)
    spec_grad = spectral(weighted, spec_weight, kept_modes, True)
    ext_grad = with_halo(weighted, (("gx", 0),), 1)
    padded_grad = pad_sides(ext_grad)
    input_grad = jnp.einsum(
        "oc,xyoz->xycz", point_weight, weighted, preferred_element_type=jnp.float32
    )
    input_grad = input_grad + jnp.einsum(
        "oc,xyoz->xycz", lap_weight, laplace_ext(ext_grad), preferred_element_type=jnp.float32
    )
    input_grad = input_grad + spec_grad.astype(jnp.float32)
    tile_grads = []
    for tile in range(tile_total):
        back_moved = window_of(padded_grad, offsets[tile], -1, weighted.shape)
        input_grad = input_grad + jnp.einsum(
            "oc,xyoz->xycz", kernel_weight[tile], back_moved, preferred_element_type=jnp.float32
        )
        tile_grads.append(
            jnp.einsum("xyoz,xycz->oc", back_moved, features, preferred_element_type=jnp.float32)
        )
    local_grad = jnp.stack(tile_grads, axis=0)
    scaling = float(
        lax.axis_size("gx") * features.shape[0] * features.shape[1] * features.shape[3]
    ) ** (-0.5)
    summed = sum_over_gx(local_grad)
    return (input_grad.astype(jnp.bfloat16), summed * scaling)


def fused_kernel(
    count,
    feat_in,
    cot_in,
    wall_in,
    mode_in,
    offs_in,
    basis_in,
    point_in,
    tile_in,
    lap_in,
    spec_in,
    bias_in,
    out,
    kout,
    feat,
    cot,
    wall,
    mode_row,
    bias_row,
    offs,
    basis,
    wst,
    wm,
    wmt,
    wf,
    wb,
    mode,
    bias,
    zs,
    cat,
    local,
    acc,
    vh,
    pen1,
    pen2,
    stage1,
    stage2,
    spec1,
    spec2,
    wgt,
    halo1,
    halo2,
    rel1,
    rel2,
    kacc,
    kdense,
    kpart,
    kmine,
    kother,
    ksum,
    kall,
    shift,
    send,
    recv,
    hsend,
    hrecv,
    vsend,
    vrecv,
    rsend,
    rrecv,
    ksend,
    krecv,
    xsend,
    xrecv,
    fsend,
    frecv,
    load,
):
    me = lax.axis_index("gx")
    grp = lax.axis_index("groups")
    xl, ny, ch, nz = feat.shape
    modes = wm.shape[0]
    tiles = offs.shape[1]
    half = count // 2
    quads = half // 2
    f32, bf16 = jnp.float32, jnp.bfloat16
    side = me // half
    inner = me % half
    chip = inner // 2

    def push(src, dst, ssem, rsem, peer):
        return pltpu.make_async_remote_copy(
            src_ref=src,
            dst_ref=dst,
            send_sem=ssem,
            recv_sem=rsem,
            device_id=(grp, peer),
            device_id_type=MESH,
        )

    def each(low, high, body):
        def step(i, carry):
            body(i)
            return carry

        lax.fori_loop(low, high, step, 0)

    def place(cross, turn, core):
        return ((side + cross) % 2) * half + ((chip + turn) % quads) * 2 + core

    def by_core(j):
        core = j // half
        rest = j % half
        return place(1 - rest // quads, rest % quads, core)

    def by_side(j):
        rest = j % half
        return place(1 - j // half, rest // 2, rest % 2)

    def from_side(j):
        rest = j % half
        return place(1 - j // half, quads - rest // 2, rest % 2)

    def from_core(j):
        core = j // half
        rest = j % half
        return place(1 - rest // quads, quads - rest % quads, core)

    def others(low, high, order, body):
        def visit(j):
            peer = order(j)

            @pl.when(peer != me)
            def _():
                body(peer)

        each(low, high, visit)

    def share1(peer):
        return push(
            feat.at[:, peer], pen1.at[me], send.at[0, peer], recv.at[0, me], peer
        )

    def land1(src):
        return push(feat.at[:, src], pen1.at[src], send.at[0, src], recv.at[0, src], src)

    def give1(peer):
        return push(stage1.at[peer], spec1.at[me], send.at[1, peer], recv.at[1, me], peer)

    def back1(src):
        return push(stage1.at[src], spec1.at[src], send.at[1, src], recv.at[1, src], src)

    def share2(peer):
        return push(wgt.at[peer], pen2.at[me], send.at[2, peer], recv.at[2, me], peer)

    def land2(src):
        return push(wgt.at[src], pen2.at[src], send.at[2, src], recv.at[2, src], src)

    def give2(peer):
        return push(stage2.at[peer], spec2.at[me], send.at[3, peer], recv.at[3, me], peer)

    def back2(src):
        return push(stage2.at[src], spec2.at[src], send.at[3, src], recv.at[3, src], src)

    loads = [
        pltpu.make_async_copy(feat_in, feat, load.at[0]),
        pltpu.make_async_copy(point_in, wst.at[0], load.at[1]),
        pltpu.make_async_copy(lap_in, wst.at[1], load.at[2]),
        pltpu.make_async_copy(tile_in, wst.at[pl.ds(2, tiles)], load.at[3]),
        pltpu.make_async_copy(spec_in, wm, load.at[4]),
        pltpu.make_async_copy(mode_in, mode_row, load.at[5]),
        pltpu.make_async_copy(bias_in, bias_row, load.at[6]),
        pltpu.make_async_copy(wall_in, wall, load.at[7]),
        pltpu.make_async_copy(cot_in, cot, load.at[8]),
        pltpu.make_async_copy(offs_in, offs, load.at[9]),
        pltpu.make_async_copy(basis_in, basis, load.at[10]),
    ]
    barrier = pltpu.get_barrier_semaphore()
    each(
        1,
        count,
        lambda d: pl.semaphore_signal(
            barrier, inc=1, device_id=(grp, lax.rem(me + d, count)), device_id_type=MESH
        ),
    )
    for piece in loads:
        piece.start()

    pl.semaphore_wait(barrier, count - 1)
    loads[0].wait()

    low_edge = half - 1
    via = rel1.shape[0]
    up_relay = low_edge - 2
    down_relay = half + 2

    def low_copy(peer):
        return push(feat.at[0], halo1.at[1], hsend.at[0], hrecv.at[0], peer)

    def high_copy(peer):
        return push(feat.at[xl - 1], halo1.at[0], hsend.at[1], hrecv.at[1], peer)

    def low_cross():
        part = pl.ds(half - 1 + via, half + 1 - via)
        return push(feat.at[0, part], halo1.at[1, part], hsend.at[0], hrecv.at[0], low_edge)

    def high_cross():
        part = pl.ds(0, half + 1 - via)
        return push(feat.at[xl - 1, part], halo1.at[0, part], hsend.at[1], hrecv.at[1], half)

    def up_first(peer):
        part = pl.ds(half + 1 - via, via)
        return push(feat.at[xl - 1, part], rel1, hsend.at[2], hrecv.at[2], peer)

    def down_first(peer):
        return push(feat.at[0, pl.ds(half - 1, via)], rel1, hsend.at[2], hrecv.at[2], peer)

    def up_second(peer):
        part = pl.ds(half + 1 - via, via)
        return push(rel1, halo1.at[0, part], hsend.at[3], hrecv.at[3], peer)

    def down_second(peer):
        part = pl.ds(half - 1, via)
        return push(rel1, halo1.at[1, part], hsend.at[3], hrecv.at[3], peer)

    def low_pass():
        return push(pen1.at[half, 0], halo1.at[1, me], fsend.at[0], frecv.at[me], low_edge)

    def high_pass():
        return push(
            pen1.at[low_edge, xl - 1], halo1.at[0, me], fsend.at[0], frecv.at[me], half
        )

    def low_row(y, peer):
        return push(wgt.at[y, 0], halo2.at[1, y], rsend.at[0, y], rrecv.at[0, y], peer)

    def high_row(y, peer):
        return push(wgt.at[y, xl - 1], halo2.at[0, y], rsend.at[1, y], rrecv.at[1, y], peer)

    def low_relay():
        return push(
            pen2.at[half, 0], halo2.at[1, me], fsend.at[0], rrecv.at[0, me], low_edge
        )

    def high_relay():
        return push(
            pen2.at[low_edge, xl - 1], halo2.at[0, me], fsend.at[0], rrecv.at[1, me], half
        )

    def low_detour(y, peer):
        slot = y - (half - 1)
        return push(wgt.at[y, 0], rel2.at[slot], rsend.at[0, y], vrecv.at[slot], peer)

    def high_detour(y, peer):
        slot = y - (half + 1 - via)
        return push(wgt.at[y, xl - 1], rel2.at[slot], rsend.at[1, y], vrecv.at[slot], peer)

    def low_onward(slot, peer):
        y = slot + half - 1
        return push(rel2.at[slot], halo2.at[1, y], vsend.at[slot], rrecv.at[0, y], peer)

    def high_onward(slot, peer):
        y = slot + half + 1 - via
        return push(rel2.at[slot], halo2.at[0, y], vsend.at[slot], rrecv.at[1, y], peer)

    def low_turned(y):
        return (me == half) & (y >= low_edge) & (y < low_edge + via)

    def high_turned(y):
        return (me == low_edge) & (y > half - via) & (y <= half)

    def low_straight(y):
        return (me > 0) & ((me != half) | (y >= low_edge + via))

    def high_straight(y):
        return (me < count - 1) & ((me != low_edge) | (y <= half - via))

    def low_own(y):
        return (me > 0) & ((me != half) | (y >= low_edge))

    def high_own(y):
        return (me < count - 1) & ((me != low_edge) | (y <= half))

    def when(cond, body):
        @pl.when(cond)
        def _():
            body()

    inside_low = (me > 0) & (me != half)
    inside_high = (me < count - 1) & (me != low_edge)
    others(0, half, by_core, lambda peer: share1(peer).start())
    when(me == half, lambda: low_cross().start())
    when(me == low_edge, lambda: high_cross().start())
    when(me == half, lambda: down_first(down_relay).start())
    when(me == low_edge, lambda: up_first(up_relay).start())
    when(inside_low, lambda: low_copy(me - 1).start())
    when(inside_high, lambda: high_copy(me + 1).start())
    others(half, count, by_core, lambda peer: share1(peer).start())

    from_z = lax.broadcasted_iota(jnp.int32, (nz, nz), 0)
    to_z = lax.broadcasted_iota(jnp.int32, (nz, nz), 1)
    for m, dz in enumerate([dz for dz in range(-RAD, RAD + 1) if dz]):
        shift[:, m * nz : (m + 1) * nz] = jnp.where(from_z == to_z + dz, 1.0, 0.0).astype(bf16)

    @pl.when(me == 0)
    def _():
        halo1[0] = jnp.zeros(halo1.shape[1:], bf16)
        halo2[0] = jnp.zeros(halo2.shape[1:], bf16)

    @pl.when(me == count - 1)
    def _():
        halo1[1] = jnp.zeros(halo1.shape[1:], bf16)
        halo2[1] = jnp.zeros(halo2.shape[1:], bf16)

    for edge in (0, RAD + ny):
        for dz in range(2 * RAD + 1):
            for x in range(xl + 2):
                zs[dz, x, edge : edge + RAD] = jnp.zeros((RAD, ch, nz), bf16)

    moves = [dz for dz in range(-RAD, RAD + 1) if dz]
    group = math.gcd(ny, 8)

    def spread(take, place_x):
        def body(i):
            y = i * group
            v = take(pl.ds(y, group))
            zs[RAD, place_x, pl.ds(y + RAD, group)] = v
            flat = v.reshape(group * ch, nz)
            moved = jnp.dot(flat, shift[...], preferred_element_type=f32).astype(bf16)
            for m, dz in enumerate(moves):
                piece = moved[:, m * nz : (m + 1) * nz].reshape(group, ch, nz)
                zs[RAD + dz, place_x, pl.ds(y + RAD, group)] = piece

        each(0, ny // group, body)

    def gather_rows(direction):
        def body(y):
            for x in range(xl):
                lanes = slice(x * nz, (x + 1) * nz)
                centre = zs[RAD, x + 1, y + RAD]
                cat[y, 0:ch, lanes] = centre
                total = zs[RAD, x + 2, y + RAD].astype(f32) + zs[RAD, x, y + RAD].astype(f32)
                total = total + zs[RAD, x + 1, y + RAD + 1].astype(f32)
                total = total + zs[RAD, x + 1, y + RAD - 1].astype(f32)
                total = total + zs[RAD + 1, x + 1, y + RAD].astype(f32)
                total = total + zs[RAD - 1, x + 1, y + RAD].astype(f32)
                cat[y, ch : 2 * ch, lanes] = (total - 6.0 * centre.astype(f32)).astype(bf16)
                for t in range(tiles):
                    moved = zs[
                        RAD + direction * offs[2, t],
                        x + 1 + direction * offs[0, t],
                        y + RAD + direction * offs[1, t],
                    ]
                    cat[y, (2 + t) * ch : (3 + t) * ch, lanes] = moved

        each(0, ny, body)

    unroll = math.gcd(ny, 4)

    def each_row(body):
        def rows_at(i):
            for r in range(unroll):
                body(i * unroll + r)

        each(0, ny // unroll, rows_at)

    def mix(weights):
        def body(y):
            local[y] = jnp.dot(weights[...], cat[y], preferred_element_type=f32)

        each_row(body)

    def gain(planes, src):
        wide = [p.astype(f32) for p in planes]
        for k in range(modes):
            total = acc[k]
            for j in range(xl):
                total = total + basis[k, src * xl + j] * wide[j]
            acc[k] = total

    def forward_mix():
        for k in range(modes):
            v = jnp.dot(wm[k], acc[k].astype(bf16), preferred_element_type=f32)
            v = jnp.where(mode[...] > float(k), v, 0.0)
            vh[k] = v.astype(bf16).astype(f32)

    def backward_mix():
        for k in range(modes):
            u = jnp.where(mode[...] > float(k), acc[k], 0.0).astype(bf16)
            v = jnp.dot(wmt[k], u, preferred_element_type=f32)
            vh[k] = v.astype(bf16).astype(f32)

    def expand(stage, peer):
        for j in range(xl):
            total = basis[0, peer * xl + j] * vh[0]
            for k in range(1, modes):
                total = total + basis[k, peer * xl + j] * vh[k]
            stage[peer, j] = total.astype(bf16)

    for x in range(xl):
        spread(lambda y: feat[x, y], x + 1)
    for piece in loads[1:]:
        piece.wait()

    row_at = lax.broadcasted_iota(jnp.int32, (ch, ch), 0)
    col_at = lax.broadcasted_iota(jnp.int32, (ch, ch), 1)
    diagonal = row_at == col_at
    unit = jnp.where(diagonal, 1.0, 0.0).astype(bf16)

    def upright(row):
        spread_out = jnp.where(diagonal, jnp.broadcast_to(row, (ch, ch)), 0.0)
        column = jnp.sum(spread_out, axis=1, keepdims=True)
        return jnp.broadcast_to(column, (ch, nz))

    mode[...] = upright(mode_row[...].astype(f32))
    bias[...] = upright(bias_row[...])

    def flipped(block):
        return lax.dot_general(
            block, unit, (((0,), (0,)), ((), ())), preferred_element_type=f32
        ).astype(bf16)

    for t in range(2 + tiles):
        wf[:, t * ch : (t + 1) * ch] = wst[t]
        wb[:, t * ch : (t + 1) * ch] = flipped(wst[t])

    def flip_mode(k):
        wmt[k] = flipped(wm[k])

    each(0, modes, flip_mode)

    def passed_low(i):
        push(
            pen1.at[low_edge, xl - 1], halo1.at[0, i], fsend.at[0], frecv.at[i], low_edge
        ).wait_recv()

    def passed_high(i):
        push(pen1.at[half, 0], halo1.at[1, i], fsend.at[0], frecv.at[i], half).wait_recv()

    def forward_stencil():
        when(inside_low, lambda: high_copy(me - 1).wait_recv())
        when(inside_high, lambda: low_copy(me + 1).wait_recv())

        @pl.when(me == half)
        def _():
            high_cross_here = push(
                feat.at[xl - 1, pl.ds(0, half + 1 - via)],
                halo1.at[0, pl.ds(0, half + 1 - via)],
                hsend.at[1],
                hrecv.at[1],
                low_edge,
            )
            high_cross_here.wait_recv()
            up_second(up_relay).wait_recv()
            each(half + 1, count, passed_low)

        @pl.when(me == low_edge)
        def _():
            low_cross_here = push(
                feat.at[0, pl.ds(half - 1 + via, half + 1 - via)],
                halo1.at[1, pl.ds(half - 1 + via, half + 1 - via)],
                hsend.at[0],
                hrecv.at[0],
                half,
            )
            low_cross_here.wait_recv()
            down_second(down_relay).wait_recv()
            each(0, half - 1, passed_high)

        spread(lambda y: halo1[0, y], 0)
        spread(lambda y: halo1[1, y], xl + 1)
        gather_rows(1)
        mix(wf)

    core = me % 2

    @pl.when(me == up_relay)
    def _():
        up_first(low_edge).wait_recv()
        up_second(half).start()

    @pl.when(me == down_relay)
    def _():
        down_first(half).wait_recv()
        down_second(low_edge).start()

    early = (core == 1) & (me != low_edge)
    when(early, forward_stencil)

    acc[...] = jnp.zeros(acc.shape, f32)
    gain([feat[j, me] for j in range(xl)], me)

    def take1(src):
        land1(src).wait_recv()
        when((src == half) & (me < low_edge), lambda: low_pass().start())
        when((src == low_edge) & (me > half), lambda: high_pass().start())
        gain([pen1[src, j] for j in range(xl)], src)

    others(0, count, from_side, take1)
    forward_mix()

    def hand1(peer):
        expand(stage1, peer)
        give1(peer).start()

    others(half, count, by_core, hand1)
    others(0, half, by_core, hand1)
    expand(stage1, me)
    when(jnp.logical_not(early), forward_stencil)
    root = math.sqrt(2.0 / math.pi)

    def slope(y, planes):
        for x in range(xl):
            v = local[y, :, x * nz : (x + 1) * nz] + planes[x].astype(f32) + bias[...]
            square = v * v
            t = jnp.tanh(root * (v + 0.044715 * (square * v)))
            g = 0.5 * (1.0 + t)
            g = g + (0.5 * v) * ((1.0 - t * t) * (root * (1.0 + (3.0 * 0.044715) * square)))
            fluid = (1 - wall[x, pl.ds(y, 1), :]).astype(f32)
            wgt[y, x] = ((cot[x, y].astype(f32) * g) * fluid).astype(bf16)
        when(low_straight(y), lambda: low_row(y, me - 1).start())
        when(high_straight(y), lambda: high_row(y, me + 1).start())
        when(low_turned(y), lambda: low_detour(y, down_relay).start())
        when(high_turned(y), lambda: high_detour(y, up_relay).start())

    kacc[...] = jnp.zeros(kacc.shape, f32)

    def row_work(y):
        planes = jnp.concatenate([wgt[y, x] for x in range(xl)], axis=1)
        kacc[...] += lax.dot_general(
            cat[y, 2 * ch :, :], planes, (((1,), (1,)), ((), ())), preferred_element_type=f32
        )
        flat = jnp.concatenate([wgt[y, x] for x in range(xl)], axis=0)
        moved = jnp.dot(flat, shift[...], preferred_element_type=f32).astype(bf16)
        for x in range(xl):
            zs[RAD, x + 1, y + RAD] = wgt[y, x]
            for m, dz in enumerate(moves):
                piece = moved[x * ch : (x + 1) * ch, m * nz : (m + 1) * nz]
                zs[RAD + dz, x + 1, y + RAD] = piece

    slope(me, [stage1[me, j] for j in range(xl)])

    def turn(src):
        back1(src).wait_recv()
        slope(src, [spec1[src, j] for j in range(xl)])
        share2(src).start()

    def turn_work(src):
        turn(src)
        row_work(src)

    others(0, half, by_core, turn)
    row_work(me)
    others(0, half, by_core, row_work)
    others(half, count, by_core, turn_work)

    pairs = tiles // 2
    for t in range(pairs):
        kdense[t * ch : (t + 1) * ch] = jnp.concatenate(
            [
                jnp.transpose(kacc[p * ch : (p + 1) * ch])
                for p in (t, t + pairs)
            ],
            axis=1,
        )

    rows = kpart.shape[1]

    def strip(p):
        return kdense.at[pl.ds(p * rows, rows)]

    def near(body):
        def visit(d):
            body((inner + d) % half)

        each(1, half, visit)

    def ksend_to(p):
        return push(
            strip(p), kpart.at[inner], ksend.at[0, p], krecv.at[0, inner], side * half + p
        )

    def kland(p):
        return push(strip(p), kpart.at[p], ksend.at[0, p], krecv.at[0, p], side * half + p)

    near(lambda p: ksend_to(p).start())
    def pass_up(slot):
        high_detour(slot + half + 1 - via, low_edge).wait_recv()
        high_onward(slot, half).start()

    def pass_down(slot):
        low_detour(slot + half - 1, half).wait_recv()
        low_onward(slot, low_edge).start()

    when(me == up_relay, lambda: each(0, via, pass_up))
    when(me == down_relay, lambda: each(0, via, pass_down))

    acc[...] = jnp.zeros(acc.shape, f32)
    gain([wgt[me, j] for j in range(xl)], me)

    def take2(src):
        land2(src).wait_recv()
        when((src == half) & (me < low_edge), lambda: low_relay().start())
        when((src == low_edge) & (me > half), lambda: high_relay().start())
        gain([pen2[src, j] for j in range(xl)], src)

    when(me < low_edge, lambda: low_pass().wait_send())
    when(me > half, lambda: high_pass().wait_send())
    others(0, count, from_side, take2)
    backward_mix()

    def hand2(peer):
        expand(stage2, peer)
        give2(peer).start()

    others(0, 3, by_core, hand2)
    kpart[inner] = kdense[pl.ds(inner * rows, rows)]
    near(lambda p: kland(p).wait_recv())
    part_sum = kpart[0]
    for p in range(1, half):
        part_sum = part_sum + kpart[p]
    kmine[...] = part_sum
    partner = ((side + 1) % 2) * half + inner
    across = push(kmine, kother, xsend.at[0], xrecv.at[0], partner)
    across.start()
    others(3, count, by_core, hand2)
    expand(stage2, me)

    def halo_rows(y):
        when(me > 0, lambda: high_row(y, me - 1).wait_recv())
        when(me < count - 1, lambda: low_row(y, me + 1).wait_recv())

    each(0, ny, halo_rows)
    spread(lambda y: halo2[0, y], 0)
    spread(lambda y: halo2[1, y], xl + 1)
    gather_rows(-1)

    mix(wb)

    def finish(y, planes):
        for x in range(xl):
            total = local[y, :, x * nz : (x + 1) * nz] + planes[x].astype(f32)
            out[x, y] = total.astype(bf16)

    finish(me, [stage2[me, j] for j in range(xl)])

    def last(src):
        back2(src).wait_recv()
        finish(src, [spec2[src, j] for j in range(xl)])

    across.wait_recv()
    ksum[...] = (kmine[...] + kother[...]) * (float(count * xl * ny * nz) ** -0.5)
    kall[pl.ds(inner * rows, rows)] = ksum[...]

    def piece_of(p):
        return kall.at[pl.ds(p * rows, rows)]

    def kspread(p):
        return push(ksum, piece_of(inner), ksend.at[1, p], krecv.at[1, inner], side * half + p)

    def kcollect(p):
        return push(ksum, piece_of(p), ksend.at[1, p], krecv.at[1, p], side * half + p)

    near(lambda p: kspread(p).start())

    others(half, count, from_side, last)
    others(0, half, from_side, last)
    near(lambda p: kcollect(p).wait_recv())
    for t in range(pairs):
        kout[t] = kall[t * ch : (t + 1) * ch, 0:ch]
        kout[t + pairs] = kall[t * ch : (t + 1) * ch, ch : 2 * ch]

    when(me == half, lambda: low_cross().wait_send())
    when(me == low_edge, lambda: high_cross().wait_send())
    when(me == half, lambda: down_first(down_relay).wait_send())
    when(me == low_edge, lambda: up_first(up_relay).wait_send())
    when(me == up_relay, lambda: up_second(half).wait_send())
    when(me == down_relay, lambda: down_second(low_edge).wait_send())
    when(me == up_relay, lambda: each(0, via, lambda i: high_onward(i, half).wait_send()))
    when(me == down_relay, lambda: each(0, via, lambda i: low_onward(i, low_edge).wait_send()))
    when(inside_low, lambda: low_copy(me - 1).wait_send())
    when(inside_high, lambda: high_copy(me + 1).wait_send())

    def row_sent(y):
        when(low_own(y), lambda: low_row(y, me - 1).wait_send())
        when(high_own(y), lambda: high_row(y, me + 1).wait_send())

    each(0, ny, row_sent)
    when(me < low_edge, lambda: low_relay().wait_send())
    when(me > half, lambda: high_relay().wait_send())
    across.wait_send()

    def near_sent(p):
        ksend_to(p).wait_send()
        kspread(p).wait_send()

    near(near_sent)

    def drain(peer):
        share1(peer).wait_send()
        give1(peer).wait_send()
        share2(peer).wait_send()
        give2(peer).wait_send()

    others(0, count, by_side, drain)


def flush_kernel(field, tile, field_out, tile_out, sems):
    first = pltpu.make_async_copy(field, field_out, sems.at[0])
    second = pltpu.make_async_copy(tile, tile_out, sems.at[1])
    first.start()
    second.start()
    first.wait()
    second.wait()


def fits_kernel(count, features, kernel_weight):
    xl, ny, ch, nz = features.shape
    cells = xl * ny * ch * nz
    tile_rows = kernel_weight.shape[0] * ch
    if ny != count or count % 4 or nz % 128 or ch % 64 or kernel_weight.shape[0] % 2:
        return False
    if tile_rows % (8 * count):
        return False
    return 80 * cells < 24 * 2**20


def fused_device(
    features,
    cotangent,
    wall_flags,
    mode_counts,
    offsets,
    point_weight,
    kernel_weight,
    lap_weight,
    spec_weight,
    bias,
):
    count = lax.axis_size("gx")
    if not fits_kernel(count, features, kernel_weight):
        return per_device(
            features,
            cotangent,
            wall_flags,
            mode_counts,
            offsets,
            point_weight,
            kernel_weight,
            lap_weight,
            spec_weight,
            bias,
        )
    xl, ny, ch, nz = features.shape
    modes, tiles = spec_weight.shape[0], kernel_weight.shape[0]
    half = count // 2
    rows = tiles * ch // (2 * half)
    f32, bf16 = jnp.float32, jnp.bfloat16
    dma = pltpu.SemaphoreType.DMA
    vmem = pl.BlockSpec(memory_space=pltpu.VMEM)
    hbm = pl.BlockSpec(memory_space=pltpu.HBM)
    field_grad, tile_grad = pl.pallas_call(
        functools.partial(fused_kernel, count),
        out_shape=(
            pltpu.VMEM(features.shape, bf16),
            pltpu.VMEM(kernel_weight.shape, f32),
        ),
        in_specs=[hbm, hbm, hbm, hbm, hbm, hbm, hbm, hbm, hbm, hbm, hbm],
        out_specs=(vmem, vmem),
        scratch_shapes=[
            pltpu.VMEM((xl, ny, ch, nz), bf16),
            pltpu.VMEM((xl, ny, ch, nz), bf16),
            pltpu.VMEM((xl, ny, nz), jnp.int32),
            pltpu.VMEM((1, ch), jnp.int32),
            pltpu.VMEM((1, ch), f32),
            pltpu.SMEM((3, tiles), jnp.int32),
            pltpu.SMEM((modes, count * xl), f32),
            pltpu.VMEM((2 + tiles, ch, ch), bf16),
            pltpu.VMEM((modes, ch, ch), bf16),
            pltpu.VMEM((modes, ch, ch), bf16),
            pltpu.VMEM((ch, (2 + tiles) * ch), bf16),
            pltpu.VMEM((ch, (2 + tiles) * ch), bf16),
            pltpu.VMEM((ch, nz), f32),
            pltpu.VMEM((ch, nz), f32),
            pltpu.VMEM((2 * RAD + 1, xl + 2, ny + 2 * RAD, ch, nz), bf16),
            pltpu.VMEM((ny, (2 + tiles) * ch, xl * nz), bf16),
            pltpu.VMEM((ny, ch, xl * nz), f32),
            pltpu.VMEM((modes, ch, nz), f32),
            pltpu.VMEM((modes, ch, nz), f32),
            pltpu.VMEM((count, xl, ch, nz), bf16),
            pltpu.VMEM((count, xl, ch, nz), bf16),
            pltpu.VMEM((count, xl, ch, nz), bf16),
            pltpu.VMEM((count, xl, ch, nz), bf16),
            pltpu.VMEM((count, xl, ch, nz), bf16),
            pltpu.VMEM((count, xl, ch, nz), bf16),
            pltpu.VMEM((ny, xl, ch, nz), bf16),
            pltpu.VMEM((2, ny, ch, nz), bf16),
            pltpu.VMEM((2, ny, ch, nz), bf16),
            pltpu.VMEM((half // 2, ch, nz), bf16),
            pltpu.VMEM((half // 2, ch, nz), bf16),
            pltpu.VMEM((tiles * ch, ch), f32),
            pltpu.VMEM((tiles * ch // 2, 2 * ch), f32),
            pltpu.VMEM((half, rows, 2 * ch), f32),
            pltpu.VMEM((rows, 2 * ch), f32),
            pltpu.VMEM((rows, 2 * ch), f32),
            pltpu.VMEM((rows, 2 * ch), f32),
            pltpu.VMEM((tiles * ch // 2, 2 * ch), f32),
            pltpu.VMEM((nz, 2 * RAD * nz), bf16),
            dma((4, count)),
            dma((4, count)),
            dma((4,)),
            dma((4,)),
            dma((half // 2,)),
            dma((half // 2,)),
            dma((2, ny)),
            dma((2, ny)),
            dma((2, half)),
            dma((2, half)),
            dma((1,)),
            dma((1,)),
            dma((1,)),
            dma((ny,)),
            dma((11,)),
        ],
        compiler_params=pltpu.CompilerParams(
            collective_id=0, has_side_effects=True, vmem_limit_bytes=56 * 2**20
        ),
    )(
        features,
        cotangent,
        wall_flags,
        mode_counts.reshape(1, ch),
        offsets.T,
        basis_constant(modes, count * xl),
        point_weight,
        kernel_weight,
        lap_weight,
        spec_weight,
        bias.reshape(1, ch),
    )
    field_grad, tile_grad = pl.pallas_call(
        flush_kernel,
        out_shape=(
            jax.ShapeDtypeStruct(features.shape, bf16),
            jax.ShapeDtypeStruct(kernel_weight.shape, f32),
        ),
        in_specs=[vmem] * 2,
        out_specs=(hbm,) * 2,
        scratch_shapes=[dma((2,))],
    )(
        pltpu.with_memory_space_constraint(field_grad, pltpu.VMEM),
        pltpu.with_memory_space_constraint(tile_grad, pltpu.VMEM),
    )
    return field_grad, tile_grad


def solution(mesh):
    return jax.shard_map(
        fused_device,
        mesh=mesh,
        in_specs=(
            P(("groups", "gx"), None, None, None),
            P(("groups", "gx"), None, None, None),
            P(("groups", "gx"), None, None),
            P(),
            P(),
            P(),
            P(),
            P(),
            P(),
            P(),
        ),
        out_specs=(P(("groups", "gx"), None, None, None), P("groups", None, None)),
        check_vma=False,
    )
```

```python
import functools
from functools import partial
import math

import jax
import ml_dtypes
import numpy as np
import jax.numpy as jnp
from jax import lax
from jax.experimental import pallas as pl
from jax.experimental.pallas import tpu as pltpu
from jax.sharding import PartitionSpec as P

RAD = 2
MESH = pl.DeviceIdType.MESH


def with_halo(cells, sides, width):
    for axis, dim in sides:
        count = lax.axis_size(axis)
        ends = count - 1
        head = lax.slice_in_dim(cells, 0, width, axis=dim)
        tail = lax.slice_in_dim(cells, cells.shape[dim] - width, cells.shape[dim], axis=dim)
        cells = jnp.concatenate(
            [
                lax.ppermute(tail, axis, [(i, (i + 1) % count) for i in range(ends)]),
                cells,
                lax.ppermute(head, axis, [((i + 1) % count, i) for i in range(ends)]),
            ],
            axis=dim,
        )
    return cells


def basis_table(mode_total, length):
    mode_index = jnp.arange(mode_total, dtype=jnp.float32)[:, None]
    cell_index = jnp.arange(length, dtype=jnp.float32)[None, :]
    phase_angle = math.pi / (2.0 * length) * mode_index * (2.0 * cell_index + 1.0)
    amplitude = jnp.where(mode_index == 0.0, math.sqrt(1.0 / length), math.sqrt(2.0 / length))
    return (amplitude * jnp.cos(phase_angle)).astype(jnp.bfloat16)


def basis_constant(mode_total, length):
    mode_index = np.arange(mode_total, dtype=np.float64)[:, None]
    cell_index = np.arange(length, dtype=np.float64)[None, :]
    phase_angle = math.pi / (2.0 * length) * mode_index * (2.0 * cell_index + 1.0)
    amplitude = np.where(mode_index == 0.0, math.sqrt(1.0 / length), math.sqrt(2.0 / length))
    table = (amplitude * np.cos(phase_angle)).astype(np.float32)
    return table.astype(ml_dtypes.bfloat16).astype(np.float32)


def pencil_work(pencil, spec_weight, kept_modes, adjoint):
    basis = basis_table(spec_weight.shape[0], pencil.shape[0])
    coefficients = jnp.einsum(
        "kx,xycz->kycz", basis, pencil, preferred_element_type=jnp.float32
    ).astype(jnp.bfloat16)
    if adjoint:
        masked = coefficients * kept_modes[:, None, :, None].astype(jnp.bfloat16)
        mixed_modes = jnp.einsum(
            "koc,kyoz->kycz", spec_weight, masked, preferred_element_type=jnp.float32
        ).astype(jnp.bfloat16)
    else:
        mixed_modes = jnp.einsum(
            "koc,kycz->kyoz", spec_weight, coefficients, preferred_element_type=jnp.float32
        )
        mixed_modes = (mixed_modes * kept_modes[:, None, :, None]).astype(jnp.bfloat16)
    return jnp.einsum(
        "kx,kyoz->xyoz", basis, mixed_modes, preferred_element_type=jnp.float32
    ).astype(jnp.bfloat16)


def spectral(slab, spec_weight, kept_modes, adjoint):
    result = pencil_work(
        lax.all_to_all(slab, "gx", split_axis=1, concat_axis=0, tiled=True),
        spec_weight,
        kept_modes,
        adjoint,
    )
    return lax.all_to_all(result, "gx", split_axis=0, concat_axis=1, tiled=True)


def laplace_ext(extended):
    padded = jnp.pad(extended, ((0, 0), (1, 1), (0, 0), (1, 1))).astype(jnp.float32)
    centre_cells = padded[1:-1, 1:-1, :, 1:-1]
    neighbours = padded[2:, 1:-1, :, 1:-1] + padded[:-2, 1:-1, :, 1:-1]
    neighbours = neighbours + padded[1:-1, 2:, :, 1:-1] + padded[1:-1, :-2, :, 1:-1]
    neighbours = neighbours + padded[1:-1, 1:-1, :, 2:] + padded[1:-1, 1:-1, :, :-2]
    return (neighbours - 6.0 * centre_cells).astype(jnp.bfloat16)


def pad_sides(extended):
    return jnp.pad(extended, ((0, 0), (RAD, RAD), (0, 0), (RAD, RAD)))


def window_of(padded, offset, direction, slab_shape):
    starts = (
        1 + direction * offset[0],
        RAD + direction * offset[1],
        0,
        RAD + direction * offset[2],
    )
    return lax.dynamic_slice(padded, starts, slab_shape)


def gelu_slope(preact, upstream):
    _, pullback = jax.vjp(partial(jax.nn.gelu, approximate=True), preact)
    return pullback(upstream)[0]


def sum_over_gx(terms):
    count = lax.axis_size("gx")
    if terms.size % count:
        return lax.psum(terms, "gx")
    pieces = lax.all_to_all(terms.reshape(count, -1), "gx", split_axis=0, concat_axis=0, tiled=True)
    mine = jnp.sum(pieces, axis=0)
    copies = jnp.broadcast_to(mine[None, :], pieces.shape)
    gathered = lax.all_to_all(copies, "gx", split_axis=0, concat_axis=0, tiled=True)
    return gathered.reshape(terms.shape)


def per_device(
    features,
    cotangent,
    wall_flags,
    mode_counts,
    offsets,
    point_weight,
    kernel_weight,
    lap_weight,
    spec_weight,
    bias,
):
    mode_total = spec_weight.shape[0]
    tile_total = kernel_weight.shape[0]
    kept_modes = (jnp.arange(mode_total, dtype=jnp.int32)[:, None] < mode_counts[None, :]).astype(
        jnp.float32
    )
    fluid_mask = (1 - wall_flags).astype(jnp.float32)[:, :, None, :]
    extended = with_halo(features, (("gx", 0),), 1)
    padded_field = pad_sides(extended)
    local_part = jnp.einsum(
        "oc,xycz->xyoz", point_weight, features, preferred_element_type=jnp.float32
    )
    local_part = local_part + jnp.einsum(
        "oc,xycz->xyoz", lap_weight, laplace_ext(extended), preferred_element_type=jnp.float32
    )
    for tile in range(tile_total):
        moved = window_of(padded_field, offsets[tile], 1, features.shape)
        local_part = local_part + jnp.einsum(
            "oc,xycz->xyoz", kernel_weight[tile], moved, preferred_element_type=jnp.float32
        )
    local_part = local_part + bias[:, None]
    spectral_part = spectral(features, spec_weight, kept_modes, False)
    preact = local_part + spectral_part.astype(jnp.float32)
    weighted = (gelu_slope(preact, cotangent.astype(jnp.float32)) * fluid_mask).astype(jnp.bfloat16)
    spec_grad = spectral(weighted, spec_weight, kept_modes, True)
    ext_grad = with_halo(weighted, (("gx", 0),), 1)
    padded_grad = pad_sides(ext_grad)
    input_grad = jnp.einsum(
        "oc,xyoz->xycz", point_weight, weighted, preferred_element_type=jnp.float32
    )
    input_grad = input_grad + jnp.einsum(
        "oc,xyoz->xycz", lap_weight, laplace_ext(ext_grad), preferred_element_type=jnp.float32
    )
    input_grad = input_grad + spec_grad.astype(jnp.float32)
    tile_grads = []
    for tile in range(tile_total):
        back_moved = window_of(padded_grad, offsets[tile], -1, weighted.shape)
        input_grad = input_grad + jnp.einsum(
            "oc,xyoz->xycz", kernel_weight[tile], back_moved, preferred_element_type=jnp.float32
        )
        tile_grads.append(
            jnp.einsum("xyoz,xycz->oc", back_moved, features, preferred_element_type=jnp.float32)
        )
    local_grad = jnp.stack(tile_grads, axis=0)
    scaling = float(
        lax.axis_size("gx") * features.shape[0] * features.shape[1] * features.shape[3]
    ) ** (-0.5)
    summed = sum_over_gx(local_grad)
    return (input_grad.astype(jnp.bfloat16), summed * scaling)


def fused_kernel(
    count,
    feat_in,
    cot_in,
    wall_in,
    mode_in,
    offs_in,
    basis_in,
    point_in,
    tile_in,
    lap_in,
    spec_in,
    bias_in,
    out,
    kout,
    feat,
    cot,
    wall,
    mode_row,
    bias_row,
    offs,
    basis,
    wst,
    wm,
    wmt,
    wf,
    wb,
    mode,
    bias,
    zs,
    cat,
    local,
    acc,
    vh,
    pen1,
    pen2,
    stage1,
    stage2,
    spec1,
    spec2,
    wgt,
    halo1,
    halo2,
    rel1,
    rel2,
    kacc,
    kdense,
    kpart,
    kmine,
    kother,
    ksum,
    kall,
    shift,
    send,
    recv,
    hsend,
    hrecv,
    vsend,
    vrecv,
    rsend,
    rrecv,
    ksend,
    krecv,
    xsend,
    xrecv,
    fsend,
    frecv,
    load,
):
    me = lax.axis_index("gx")
    grp = lax.axis_index("groups")
    xl, ny, ch, nz = feat.shape
    modes = wm.shape[0]
    tiles = offs.shape[1]
    half = count // 2
    quads = half // 2
    f32, bf16 = jnp.float32, jnp.bfloat16
    side = me // half
    inner = me % half
    chip = inner // 2

    def push(src, dst, ssem, rsem, peer):
        return pltpu.make_async_remote_copy(
            src_ref=src,
            dst_ref=dst,
            send_sem=ssem,
            recv_sem=rsem,
            device_id=(grp, peer),
            device_id_type=MESH,
        )

    def each(low, high, body):
        def step(i, carry):
            body(i)
            return carry

        lax.fori_loop(low, high, step, 0)

    def place(cross, turn, core):
        return ((side + cross) % 2) * half + ((chip + turn) % quads) * 2 + core

    def by_core(j):
        core = j // half
        rest = j % half
        return place(1 - rest // quads, rest % quads, core)

    def by_side(j):
        rest = j % half
        return place(1 - j // half, rest // 2, rest % 2)

    def from_side(j):
        rest = j % half
        return place(1 - j // half, quads - rest // 2, rest % 2)

    def from_core(j):
        core = j // half
        rest = j % half
        return place(1 - rest // quads, quads - rest % quads, core)

    def others(low, high, order, body):
        def visit(j):
            peer = order(j)

            @pl.when(peer != me)
            def _():
                body(peer)

        each(low, high, visit)

    def share1(peer):
        return push(
            feat.at[:, peer], pen1.at[me], send.at[0, peer], recv.at[0, me], peer
        )

    def land1(src):
        return push(feat.at[:, src], pen1.at[src], send.at[0, src], recv.at[0, src], src)

    def give1(peer):
        return push(stage1.at[peer], spec1.at[me], send.at[1, peer], recv.at[1, me], peer)

    def back1(src):
        return push(stage1.at[src], spec1.at[src], send.at[1, src], recv.at[1, src], src)

    def share2(peer):
        return push(wgt.at[peer], pen2.at[me], send.at[2, peer], recv.at[2, me], peer)

    def land2(src):
        return push(wgt.at[src], pen2.at[src], send.at[2, src], recv.at[2, src], src)

    def give2(peer):
        return push(stage2.at[peer], spec2.at[me], send.at[3, peer], recv.at[3, me], peer)

    def back2(src):
        return push(stage2.at[src], spec2.at[src], send.at[3, src], recv.at[3, src], src)

    loads = [
        pltpu.make_async_copy(feat_in, feat, load.at[0]),
        pltpu.make_async_copy(point_in, wst.at[0], load.at[1]),
        pltpu.make_async_copy(lap_in, wst.at[1], load.at[2]),
        pltpu.make_async_copy(tile_in, wst.at[pl.ds(2, tiles)], load.at[3]),
        pltpu.make_async_copy(spec_in, wm, load.at[4]),
        pltpu.make_async_copy(mode_in, mode_row, load.at[5]),
        pltpu.make_async_copy(bias_in, bias_row, load.at[6]),
        pltpu.make_async_copy(wall_in, wall, load.at[7]),
        pltpu.make_async_copy(cot_in, cot, load.at[8]),
        pltpu.make_async_copy(offs_in, offs, load.at[9]),
        pltpu.make_async_copy(basis_in, basis, load.at[10]),
    ]
    barrier = pltpu.get_barrier_semaphore()
    each(
        1,
        count,
        lambda d: pl.semaphore_signal(
            barrier, inc=1, device_id=(grp, lax.rem(me + d, count)), device_id_type=MESH
        ),
    )
    for piece in loads:
        piece.start()

    pl.semaphore_wait(barrier, count - 1)
    loads[0].wait()

    low_edge = half - 1
    via = rel1.shape[0]
    up_relay = low_edge - 2
    down_relay = half + 2

    def low_copy(peer):
        return push(feat.at[0], halo1.at[1], hsend.at[0], hrecv.at[0], peer)

    def high_copy(peer):
        return push(feat.at[xl - 1], halo1.at[0], hsend.at[1], hrecv.at[1], peer)

    def low_cross():
        part = pl.ds(half - 1 + via, half + 1 - via)
        return push(feat.at[0, part], halo1.at[1, part], hsend.at[0], hrecv.at[0], low_edge)

    def high_cross():
        part = pl.ds(0, half + 1 - via)
        return push(feat.at[xl - 1, part], halo1.at[0, part], hsend.at[1], hrecv.at[1], half)

    def up_first(peer):
        part = pl.ds(half + 1 - via, via)
        return push(feat.at[xl - 1, part], rel1, hsend.at[2], hrecv.at[2], peer)

    def down_first(peer):
        return push(feat.at[0, pl.ds(half - 1, via)], rel1, hsend.at[2], hrecv.at[2], peer)

    def up_second(peer):
        part = pl.ds(half + 1 - via, via)
        return push(rel1, halo1.at[0, part], hsend.at[3], hrecv.at[3], peer)

    def down_second(peer):
        part = pl.ds(half - 1, via)
        return push(rel1, halo1.at[1, part], hsend.at[3], hrecv.at[3], peer)

    def low_pass():
        return push(pen1.at[half, 0], halo1.at[1, me], fsend.at[0], frecv.at[me], low_edge)

    def high_pass():
        return push(
            pen1.at[low_edge, xl - 1], halo1.at[0, me], fsend.at[0], frecv.at[me], half
        )

    def low_row(y, peer):
        return push(wgt.at[y, 0], halo2.at[1, y], rsend.at[0, y], rrecv.at[0, y], peer)

    def high_row(y, peer):
        return push(wgt.at[y, xl - 1], halo2.at[0, y], rsend.at[1, y], rrecv.at[1, y], peer)

    def low_relay():
        return push(
            pen2.at[half, 0], halo2.at[1, me], fsend.at[0], rrecv.at[0, me], low_edge
        )

    def high_relay():
        return push(
            pen2.at[low_edge, xl - 1], halo2.at[0, me], fsend.at[0], rrecv.at[1, me], half
        )

    def low_detour(y, peer):
        slot = y - (half - 1)
        return push(wgt.at[y, 0], rel2.at[slot], rsend.at[0, y], vrecv.at[slot], peer)

    def high_detour(y, peer):
        slot = y - (half + 1 - via)
        return push(wgt.at[y, xl - 1], rel2.at[slot], rsend.at[1, y], vrecv.at[slot], peer)

    def low_onward(slot, peer):
        y = slot + half - 1
        return push(rel2.at[slot], halo2.at[1, y], vsend.at[slot], rrecv.at[0, y], peer)

    def high_onward(slot, peer):
        y = slot + half + 1 - via
        return push(rel2.at[slot], halo2.at[0, y], vsend.at[slot], rrecv.at[1, y], peer)

    def low_turned(y):
        return (me == half) & (y >= low_edge) & (y < low_edge + via)

    def high_turned(y):
        return (me == low_edge) & (y > half - via) & (y <= half)

    def low_straight(y):
        return (me > 0) & ((me != half) | (y >= low_edge + via))

    def high_straight(y):
        return (me < count - 1) & ((me != low_edge) | (y <= half - via))

    def low_own(y):
        return (me > 0) & ((me != half) | (y >= low_edge))

    def high_own(y):
        return (me < count - 1) & ((me != low_edge) | (y <= half))

    def when(cond, body):
        @pl.when(cond)
        def _():
            body()

    inside_low = (me > 0) & (me != half)
    inside_high = (me < count - 1) & (me != low_edge)
    others(0, half, by_core, lambda peer: share1(peer).start())
    when(me == half, lambda: low_cross().start())
    when(me == low_edge, lambda: high_cross().start())
    when(me == half, lambda: down_first(down_relay).start())
    when(me == low_edge, lambda: up_first(up_relay).start())
    when(inside_low, lambda: low_copy(me - 1).start())
    when(inside_high, lambda: high_copy(me + 1).start())
    others(half, count, by_core, lambda peer: share1(peer).start())

    from_z = lax.broadcasted_iota(jnp.int32, (nz, nz), 0)
    to_z = lax.broadcasted_iota(jnp.int32, (nz, nz), 1)
    for m, dz in enumerate([dz for dz in range(-RAD, RAD + 1) if dz]):
        shift[:, m * nz : (m + 1) * nz] = jnp.where(from_z == to_z + dz, 1.0, 0.0).astype(bf16)

    @pl.when(me == 0)
    def _():
        halo1[0] = jnp.zeros(halo1.shape[1:], bf16)
        halo2[0] = jnp.zeros(halo2.shape[1:], bf16)

    @pl.when(me == count - 1)
    def _():
        halo1[1] = jnp.zeros(halo1.shape[1:], bf16)
        halo2[1] = jnp.zeros(halo2.shape[1:], bf16)

    for edge in (0, RAD + ny):
        for dz in range(2 * RAD + 1):
            for x in range(xl + 2):
                zs[dz, x, edge : edge + RAD] = jnp.zeros((RAD, ch, nz), bf16)

    moves = [dz for dz in range(-RAD, RAD + 1) if dz]
    group = math.gcd(ny, 8)

    def spread(take, place_x):
        def body(i):
            y = i * group
            v = take(pl.ds(y, group))
            zs[RAD, place_x, pl.ds(y + RAD, group)] = v
            flat = v.reshape(group * ch, nz)
            moved = jnp.dot(flat, shift[...], preferred_element_type=f32).astype(bf16)
            for m, dz in enumerate(moves):
                piece = moved[:, m * nz : (m + 1) * nz].reshape(group, ch, nz)
                zs[RAD + dz, place_x, pl.ds(y + RAD, group)] = piece

        each(0, ny // group, body)

    def gather_rows(direction):
        def body(y):
            for x in range(xl):
                lanes = slice(x * nz, (x + 1) * nz)
                centre = zs[RAD, x + 1, y + RAD]
                cat[y, 0:ch, lanes] = centre
                total = zs[RAD, x + 2, y + RAD].astype(f32) + zs[RAD, x, y + RAD].astype(f32)
                total = total + zs[RAD, x + 1, y + RAD + 1].astype(f32)
                total = total + zs[RAD, x + 1, y + RAD - 1].astype(f32)
                total = total + zs[RAD + 1, x + 1, y + RAD].astype(f32)
                total = total + zs[RAD - 1, x + 1, y + RAD].astype(f32)
                cat[y, ch : 2 * ch, lanes] = (total - 6.0 * centre.astype(f32)).astype(bf16)
                for t in range(tiles):
                    moved = zs[
                        RAD + direction * offs[2, t],
                        x + 1 + direction * offs[0, t],
                        y + RAD + direction * offs[1, t],
                    ]
                    cat[y, (2 + t) * ch : (3 + t) * ch, lanes] = moved

        each(0, ny, body)

    unroll = math.gcd(ny, 4)

    def each_row(body):
        def rows_at(i):
            for r in range(unroll):
                body(i * unroll + r)

        each(0, ny // unroll, rows_at)

    def mix(weights):
        def body(y):
            local[y] = jnp.dot(weights[...], cat[y], preferred_element_type=f32)

        each_row(body)

    def gain(planes, src):
        wide = [p.astype(f32) for p in planes]
        for k in range(modes):
            total = acc[k]
            for j in range(xl):
                total = total + basis[k, src * xl + j] * wide[j]
            acc[k] = total

    def forward_mix():
        for k in range(modes):
            v = jnp.dot(wm[k], acc[k].astype(bf16), preferred_element_type=f32)
            v = jnp.where(mode[...] > float(k), v, 0.0)
            vh[k] = v.astype(bf16).astype(f32)

    def backward_mix():
        for k in range(modes):
            u = jnp.where(mode[...] > float(k), acc[k], 0.0).astype(bf16)
            v = jnp.dot(wmt[k], u, preferred_element_type=f32)
            vh[k] = v.astype(bf16).astype(f32)

    def expand(stage, peer):
        for j in range(xl):
            total = basis[0, peer * xl + j] * vh[0]
            for k in range(1, modes):
                total = total + basis[k, peer * xl + j] * vh[k]
            stage[peer, j] = total.astype(bf16)

    for x in range(xl):
        spread(lambda y: feat[x, y], x + 1)
    for piece in loads[1:]:
        piece.wait()

    row_at = lax.broadcasted_iota(jnp.int32, (ch, ch), 0)
    col_at = lax.broadcasted_iota(jnp.int32, (ch, ch), 1)
    diagonal = row_at == col_at
    unit = jnp.where(diagonal, 1.0, 0.0).astype(bf16)

    def upright(row):
        spread_out = jnp.where(diagonal, jnp.broadcast_to(row, (ch, ch)), 0.0)
        column = jnp.sum(spread_out, axis=1, keepdims=True)
        return jnp.broadcast_to(column, (ch, nz))

    mode[...] = upright(mode_row[...].astype(f32))
    bias[...] = upright(bias_row[...])

    def flipped(block):
        return lax.dot_general(
            block, unit, (((0,), (0,)), ((), ())), preferred_element_type=f32
        ).astype(bf16)

    for t in range(2 + tiles):
        wf[:, t * ch : (t + 1) * ch] = wst[t]
        wb[:, t * ch : (t + 1) * ch] = flipped(wst[t])

    def flip_mode(k):
        wmt[k] = flipped(wm[k])

    each(0, modes, flip_mode)

    def passed_low(i):
        push(
            pen1.at[low_edge, xl - 1], halo1.at[0, i], fsend.at[0], frecv.at[i], low_edge
        ).wait_recv()

    def passed_high(i):
        push(pen1.at[half, 0], halo1.at[1, i], fsend.at[0], frecv.at[i], half).wait_recv()

    def forward_stencil():
        when(inside_low, lambda: high_copy(me - 1).wait_recv())
        when(inside_high, lambda: low_copy(me + 1).wait_recv())

        @pl.when(me == half)
        def _():
            high_cross_here = push(
                feat.at[xl - 1, pl.ds(0, half + 1 - via)],
                halo1.at[0, pl.ds(0, half + 1 - via)],
                hsend.at[1],
                hrecv.at[1],
                low_edge,
            )
            high_cross_here.wait_recv()
            up_second(up_relay).wait_recv()
            each(half + 1, count, passed_low)

        @pl.when(me == low_edge)
        def _():
            low_cross_here = push(
                feat.at[0, pl.ds(half - 1 + via, half + 1 - via)],
                halo1.at[1, pl.ds(half - 1 + via, half + 1 - via)],
                hsend.at[0],
                hrecv.at[0],
                half,
            )
            low_cross_here.wait_recv()
            down_second(down_relay).wait_recv()
            each(0, half - 1, passed_high)

        spread(lambda y: halo1[0, y], 0)
        spread(lambda y: halo1[1, y], xl + 1)
        gather_rows(1)
        mix(wf)

    core = me % 2

    @pl.when(me == up_relay)
    def _():
        up_first(low_edge).wait_recv()
        up_second(half).start()

    @pl.when(me == down_relay)
    def _():
        down_first(half).wait_recv()
        down_second(low_edge).start()

    early = (core == 1) & (me != low_edge)
    when(early, forward_stencil)

    acc[...] = jnp.zeros(acc.shape, f32)
    gain([feat[j, me] for j in range(xl)], me)

    def take1(src):
        land1(src).wait_recv()
        when((src == half) & (me < low_edge), lambda: low_pass().start())
        when((src == low_edge) & (me > half), lambda: high_pass().start())
        gain([pen1[src, j] for j in range(xl)], src)

    others(0, count, from_side, take1)
    forward_mix()

    def hand1(peer):
        expand(stage1, peer)
        give1(peer).start()

    others(half, count, by_core, hand1)
    others(0, half, by_core, hand1)
    expand(stage1, me)
    when(jnp.logical_not(early), forward_stencil)
    root = math.sqrt(2.0 / math.pi)

    def slope(y, planes):
        for x in range(xl):
            v = local[y, :, x * nz : (x + 1) * nz] + planes[x].astype(f32) + bias[...]
            square = v * v
            t = jnp.tanh(root * (v + 0.044715 * (square * v)))
            g = 0.5 * (1.0 + t)
            g = g + (0.5 * v) * ((1.0 - t * t) * (root * (1.0 + (3.0 * 0.044715) * square)))
            fluid = (1 - wall[x, pl.ds(y, 1), :]).astype(f32)
            wgt[y, x] = ((cot[x, y].astype(f32) * g) * fluid).astype(bf16)
        when(low_straight(y), lambda: low_row(y, me - 1).start())
        when(high_straight(y), lambda: high_row(y, me + 1).start())
        when(low_turned(y), lambda: low_detour(y, down_relay).start())
        when(high_turned(y), lambda: high_detour(y, up_relay).start())

    kacc[...] = jnp.zeros(kacc.shape, f32)

    def row_work(y):
        planes = jnp.concatenate([wgt[y, x] for x in range(xl)], axis=1)
        kacc[...] += lax.dot_general(
            cat[y, 2 * ch :, :], planes, (((1,), (1,)), ((), ())), preferred_element_type=f32
        )
        flat = jnp.concatenate([wgt[y, x] for x in range(xl)], axis=0)
        moved = jnp.dot(flat, shift[...], preferred_element_type=f32).astype(bf16)
        for x in range(xl):
            zs[RAD, x + 1, y + RAD] = wgt[y, x]
            for m, dz in enumerate(moves):
                piece = moved[x * ch : (x + 1) * ch, m * nz : (m + 1) * nz]
                zs[RAD + dz, x + 1, y + RAD] = piece

    slope(me, [stage1[me, j] for j in range(xl)])

    def turn(src):
        back1(src).wait_recv()
        slope(src, [spec1[src, j] for j in range(xl)])
        share2(src).start()

    def turn_work(src):
        turn(src)
        row_work(src)

    others(0, half, by_core, turn)
    row_work(me)
    others(0, half, by_core, row_work)
    others(half, count - 3, by_core, turn_work)
    others(count - 3, count, by_core, turn)
    others(count - 3, count, by_core, row_work)

    pairs = tiles // 2
    for t in range(pairs):
        kdense[t * ch : (t + 1) * ch] = jnp.concatenate(
            [
                jnp.transpose(kacc[p * ch : (p + 1) * ch])
                for p in (t, t + pairs)
            ],
            axis=1,
        )

    rows = kpart.shape[1]

    def strip(p):
        return kdense.at[pl.ds(p * rows, rows)]

    def near(body):
        def visit(d):
            body((inner + d) % half)

        each(1, half, visit)

    def ksend_to(p):
        return push(
            strip(p), kpart.at[inner], ksend.at[0, p], krecv.at[0, inner], side * half + p
        )

    def kland(p):
        return push(strip(p), kpart.at[p], ksend.at[0, p], krecv.at[0, p], side * half + p)

    near(lambda p: ksend_to(p).start())
    def pass_up(slot):
        high_detour(slot + half + 1 - via, low_edge).wait_recv()
        high_onward(slot, half).start()

    def pass_down(slot):
        low_detour(slot + half - 1, half).wait_recv()
        low_onward(slot, low_edge).start()

    when(me == up_relay, lambda: each(0, via, pass_up))
    when(me == down_relay, lambda: each(0, via, pass_down))

    acc[...] = jnp.zeros(acc.shape, f32)
    gain([wgt[me, j] for j in range(xl)], me)

    def take2(src):
        land2(src).wait_recv()
        when((src == half) & (me < low_edge), lambda: low_relay().start())
        when((src == low_edge) & (me > half), lambda: high_relay().start())
        gain([pen2[src, j] for j in range(xl)], src)

    when(me < low_edge, lambda: low_pass().wait_send())
    when(me > half, lambda: high_pass().wait_send())
    others(0, count, from_side, take2)
    backward_mix()

    def hand2(peer):
        expand(stage2, peer)
        give2(peer).start()

    others(0, 3, by_core, hand2)
    kpart[inner] = kdense[pl.ds(inner * rows, rows)]
    near(lambda p: kland(p).wait_recv())
    part_sum = kpart[0]
    for p in range(1, half):
        part_sum = part_sum + kpart[p]
    kmine[...] = part_sum
    partner = ((side + 1) % 2) * half + inner
    across = push(kmine, kother, xsend.at[0], xrecv.at[0], partner)
    across.start()
    others(3, count, by_core, hand2)
    expand(stage2, me)

    def halo_rows(y):
        when(me > 0, lambda: high_row(y, me - 1).wait_recv())
        when(me < count - 1, lambda: low_row(y, me + 1).wait_recv())

    each(0, ny, halo_rows)
    spread(lambda y: halo2[0, y], 0)
    spread(lambda y: halo2[1, y], xl + 1)
    gather_rows(-1)

    mix(wb)

    def finish(y, planes):
        for x in range(xl):
            total = local[y, :, x * nz : (x + 1) * nz] + planes[x].astype(f32)
            out[x, y] = total.astype(bf16)

    finish(me, [stage2[me, j] for j in range(xl)])

    def last(src):
        back2(src).wait_recv()
        finish(src, [spec2[src, j] for j in range(xl)])

    across.wait_recv()
    ksum[...] = (kmine[...] + kother[...]) * (float(count * xl * ny * nz) ** -0.5)
    kall[pl.ds(inner * rows, rows)] = ksum[...]

    def piece_of(p):
        return kall.at[pl.ds(p * rows, rows)]

    def kspread(p):
        return push(ksum, piece_of(inner), ksend.at[1, p], krecv.at[1, inner], side * half + p)

    def kcollect(p):
        return push(ksum, piece_of(p), ksend.at[1, p], krecv.at[1, p], side * half + p)

    near(lambda p: kspread(p).start())

    others(half, count, from_side, last)
    others(0, half, from_side, last)
    near(lambda p: kcollect(p).wait_recv())
    for t in range(pairs):
        kout[t] = kall[t * ch : (t + 1) * ch, 0:ch]
        kout[t + pairs] = kall[t * ch : (t + 1) * ch, ch : 2 * ch]

    when(me == half, lambda: low_cross().wait_send())
    when(me == low_edge, lambda: high_cross().wait_send())
    when(me == half, lambda: down_first(down_relay).wait_send())
    when(me == low_edge, lambda: up_first(up_relay).wait_send())
    when(me == up_relay, lambda: up_second(half).wait_send())
    when(me == down_relay, lambda: down_second(low_edge).wait_send())
    when(me == up_relay, lambda: each(0, via, lambda i: high_onward(i, half).wait_send()))
    when(me == down_relay, lambda: each(0, via, lambda i: low_onward(i, low_edge).wait_send()))
    when(inside_low, lambda: low_copy(me - 1).wait_send())
    when(inside_high, lambda: high_copy(me + 1).wait_send())

    def row_sent(y):
        when(low_own(y), lambda: low_row(y, me - 1).wait_send())
        when(high_own(y), lambda: high_row(y, me + 1).wait_send())

    each(0, ny, row_sent)
    when(me < low_edge, lambda: low_relay().wait_send())
    when(me > half, lambda: high_relay().wait_send())
    across.wait_send()

    def near_sent(p):
        ksend_to(p).wait_send()
        kspread(p).wait_send()

    near(near_sent)

    def drain(peer):
        share1(peer).wait_send()
        give1(peer).wait_send()
        share2(peer).wait_send()
        give2(peer).wait_send()

    others(0, count, by_side, drain)


def flush_kernel(field, tile, field_out, tile_out, sems):
    first = pltpu.make_async_copy(field, field_out, sems.at[0])
    second = pltpu.make_async_copy(tile, tile_out, sems.at[1])
    first.start()
    second.start()
    first.wait()
    second.wait()


def fits_kernel(count, features, kernel_weight):
    xl, ny, ch, nz = features.shape
    cells = xl * ny * ch * nz
    tile_rows = kernel_weight.shape[0] * ch
    if ny != count or count % 4 or nz % 128 or ch % 64 or kernel_weight.shape[0] % 2:
        return False
    if tile_rows % (8 * count):
        return False
    return 80 * cells < 24 * 2**20


def fused_device(
    features,
    cotangent,
    wall_flags,
    mode_counts,
    offsets,
    point_weight,
    kernel_weight,
    lap_weight,
    spec_weight,
    bias,
):
    count = lax.axis_size("gx")
    if not fits_kernel(count, features, kernel_weight):
        return per_device(
            features,
            cotangent,
            wall_flags,
            mode_counts,
            offsets,
            point_weight,
            kernel_weight,
            lap_weight,
            spec_weight,
            bias,
        )
    xl, ny, ch, nz = features.shape
    modes, tiles = spec_weight.shape[0], kernel_weight.shape[0]
    half = count // 2
    rows = tiles * ch // (2 * half)
    f32, bf16 = jnp.float32, jnp.bfloat16
    dma = pltpu.SemaphoreType.DMA
    vmem = pl.BlockSpec(memory_space=pltpu.VMEM)
    hbm = pl.BlockSpec(memory_space=pltpu.HBM)
    field_grad, tile_grad = pl.pallas_call(
        functools.partial(fused_kernel, count),
        out_shape=(
            pltpu.VMEM(features.shape, bf16),
            pltpu.VMEM(kernel_weight.shape, f32),
        ),
        in_specs=[hbm, hbm, hbm, hbm, hbm, hbm, hbm, hbm, hbm, hbm, hbm],
        out_specs=(vmem, vmem),
        scratch_shapes=[
            pltpu.VMEM((xl, ny, ch, nz), bf16),
            pltpu.VMEM((xl, ny, ch, nz), bf16),
            pltpu.VMEM((xl, ny, nz), jnp.int32),
            pltpu.VMEM((1, ch), jnp.int32),
            pltpu.VMEM((1, ch), f32),
            pltpu.SMEM((3, tiles), jnp.int32),
            pltpu.SMEM((modes, count * xl), f32),
            pltpu.VMEM((2 + tiles, ch, ch), bf16),
            pltpu.VMEM((modes, ch, ch), bf16),
            pltpu.VMEM((modes, ch, ch), bf16),
            pltpu.VMEM((ch, (2 + tiles) * ch), bf16),
            pltpu.VMEM((ch, (2 + tiles) * ch), bf16),
            pltpu.VMEM((ch, nz), f32),
            pltpu.VMEM((ch, nz), f32),
            pltpu.VMEM((2 * RAD + 1, xl + 2, ny + 2 * RAD, ch, nz), bf16),
            pltpu.VMEM((ny, (2 + tiles) * ch, xl * nz), bf16),
            pltpu.VMEM((ny, ch, xl * nz), f32),
            pltpu.VMEM((modes, ch, nz), f32),
            pltpu.VMEM((modes, ch, nz), f32),
            pltpu.VMEM((count, xl, ch, nz), bf16),
            pltpu.VMEM((count, xl, ch, nz), bf16),
            pltpu.VMEM((count, xl, ch, nz), bf16),
            pltpu.VMEM((count, xl, ch, nz), bf16),
            pltpu.VMEM((count, xl, ch, nz), bf16),
            pltpu.VMEM((count, xl, ch, nz), bf16),
            pltpu.VMEM((ny, xl, ch, nz), bf16),
            pltpu.VMEM((2, ny, ch, nz), bf16),
            pltpu.VMEM((2, ny, ch, nz), bf16),
            pltpu.VMEM((half // 2, ch, nz), bf16),
            pltpu.VMEM((half // 2, ch, nz), bf16),
            pltpu.VMEM((tiles * ch, ch), f32),
            pltpu.VMEM((tiles * ch // 2, 2 * ch), f32),
            pltpu.VMEM((half, rows, 2 * ch), f32),
            pltpu.VMEM((rows, 2 * ch), f32),
            pltpu.VMEM((rows, 2 * ch), f32),
            pltpu.VMEM((rows, 2 * ch), f32),
            pltpu.VMEM((tiles * ch // 2, 2 * ch), f32),
            pltpu.VMEM((nz, 2 * RAD * nz), bf16),
            dma((4, count)),
            dma((4, count)),
            dma((4,)),
            dma((4,)),
            dma((half // 2,)),
            dma((half // 2,)),
            dma((2, ny)),
            dma((2, ny)),
            dma((2, half)),
            dma((2, half)),
            dma((1,)),
            dma((1,)),
            dma((1,)),
            dma((ny,)),
            dma((11,)),
        ],
        compiler_params=pltpu.CompilerParams(
            collective_id=0, has_side_effects=True, vmem_limit_bytes=56 * 2**20
        ),
    )(
        features,
        cotangent,
        wall_flags,
        mode_counts.reshape(1, ch),
        offsets.T,
        basis_constant(modes, count * xl),
        point_weight,
        kernel_weight,
        lap_weight,
        spec_weight,
        bias.reshape(1, ch),
    )
    field_grad, tile_grad = pl.pallas_call(
        flush_kernel,
        out_shape=(
            jax.ShapeDtypeStruct(features.shape, bf16),
            jax.ShapeDtypeStruct(kernel_weight.shape, f32),
        ),
        in_specs=[vmem] * 2,
        out_specs=(hbm,) * 2,
        scratch_shapes=[dma((2,))],
    )(
        pltpu.with_memory_space_constraint(field_grad, pltpu.VMEM),
        pltpu.with_memory_space_constraint(tile_grad, pltpu.VMEM),
    )
    return field_grad, tile_grad


def solution(mesh):
    return jax.shard_map(
        fused_device,
        mesh=mesh,
        in_specs=(
            P(("groups", "gx"), None, None, None),
            P(("groups", "gx"), None, None, None),
            P(("groups", "gx"), None, None),
            P(),
            P(),
            P(),
            P(),
            P(),
            P(),
            P(),
        ),
        out_specs=(P(("groups", "gx"), None, None, None), P("groups", None, None)),
        check_vma=False,
    )
```
